32 devices in a mesh: dp: 4 (over x, core), seq: 8 (over z, y).
Axes of the slice: x: 2, y: 2, z: 4, core: 2. Of those that a mesh axis runs over, the one named last changes fastest.
Arguments:
- layer_input: bfloat16 [16, 2048, 768], P('dp', 'seq'), may hold values from -6 to 6
- cotangent: bfloat16 [16, 2048, 768], P('dp', 'seq'), may hold values from -6 to 6
- first_gain: bfloat16 [768], replicated, may hold values from 0.099609375 to 1.8984375
- light_inputs: bfloat16 [768, 2304], replicated, may hold values from -0.21875 to 0.21875
- light_output: bfloat16 [768, 768], replicated, may hold values from -0.875 to 0.875
- heavy_queries: bfloat16 [768, 768], replicated, may hold values from -0.21875 to 0.21875
- heavy_keyvalue: bfloat16 [768, 1536], replicated, may hold values from -0.21875 to 0.21875
- heavy_output: bfloat16 [768, 768], replicated, may hold values from -1.75 to 1.75
- second_gain: bfloat16 [768], replicated, may hold values from 0.099609375 to 1.8984375
- router: bfloat16 [768], replicated, may hold values from -0.21875 to 0.21875
- light_gates: bfloat16 [768, 2048], replicated, may hold values from -0.21875 to 0.21875
- light_down: bfloat16 [1024, 768], replicated, may hold values from -0.25 to 0.25
- heavy_gates: bfloat16 [768, 8192], replicated, may hold values from -0.21875 to 0.21875
- heavy_down: bfloat16 [4096, 768], replicated, may hold values from -0.25 to 0.25
- query_index: int32 [16, 512], P('dp', 'seq'), may hold values from 0 to 255, as said below
- query_count: int32 [16, 8], P('dp', 'seq'), may hold values from 16 to 64, as said below
- key_index: int32 [16, 512], P('dp', 'seq'), may hold values from 0 to 255, as said below
- key_count: int32 [16, 8], P('dp'), may hold values from 16 to 64, as said below
- feed_slot: int32 [16, 2048], P('dp', 'seq'), may hold values from -1 to 191, as said below
Outputs:
- output: bfloat16 [16, 2048, 768], P('dp', 'seq')
- input_grad: float32 [16, 2048, 768], P('dp', 'seq')
- first_gain_grad: float32 [768], P(('dp', 'seq'))
- light_inputs_grad: float32 [768, 2304], P(('dp', 'seq'))
- light_output_grad: float32 [768, 768], P(('dp', 'seq'))
- heavy_queries_grad: float32 [768, 768], P(('dp', 'seq'))
- heavy_keyvalue_grad: float32 [768, 1536], P(('dp', 'seq'))
- heavy_output_grad: float32 [768, 768], P(('dp', 'seq'))
- second_gain_grad: float32 [768], P(('dp', 'seq'))
- router_grad: float32 [768], P(('dp', 'seq'))
- light_gates_grad: float32 [768, 2048], P(('dp', 'seq'))
- light_down_grad: float32 [1024, 768], P(('dp', 'seq'))
- heavy_gates_grad: float32 [768, 8192], P(('dp', 'seq'))
- heavy_down_grad: float32 [4096, 768], P(('dp', 'seq'))
The draws below stay inside these ranges and needn't reach their ends.
Inputs may be any that keep to these rules, and one draw needn't show every extreme that they name: `query_index`: within each device's 64 slots of a row the positions are distinct. `query_count`: in every row some device has all 64 slots live. `key_index`: within each device's 64 slots of a row the positions are distinct. `key_count`: in every row some device has all 64 slots live. `feed_slot`: A device's send buffer has 8 parts of 24 rows, part j for device j of seq; slot j * 24 + m lies in part j. The slots of one device's tokens are distinct. In every index of dp some device fills every part.
All inputs are finite; a program needn't handle non-finite values.
Results may differ from the reference program's by a relative error of at most 0.018.
Values may be sent and summed in bfloat16 or wider, within the bound.
A program may use at most 320 MiB of HBM per device.

```python
import jax
import jax.numpy as jnp
from jax import lax

D = 768
HL = 8
LHD = 96
HH = 12
HHD = 64
FL = 1024
FH = 4096
RADIUS = 128
TOK_SEQDEV = 256
SEQS = 4
QCAP = 64
KCAP = 64
FFN_CAP = 24
LEN = 2048
BATCH = 16
N_SEQ = 8


def slot_positions(key, capacity):
    devices = LEN // TOK_SEQDEV
    key_list = jax.random.split(key, BATCH * devices)
    chosen = jax.vmap(lambda item: jax.random.permutation(item, TOK_SEQDEV)[:capacity])(key_list)
    return chosen.reshape(BATCH, devices * capacity).astype(jnp.int32)


def slot_counts(key, capacity):
    devices = LEN // TOK_SEQDEV
    key_one, key_two = jax.random.split(key)
    counts = jax.random.randint(key_one, (BATCH, devices), max(1, capacity // 4), capacity + 1)
    chosen = jax.random.randint(key_two, (BATCH, 1), 0, devices)
    forced = jnp.arange(devices)[None, :] == chosen
    return jnp.where(forced, capacity, counts).astype(jnp.int32)


def draw_query_index(key, part):
    return slot_positions(jax.random.fold_in(key, 11), QCAP)


def draw_query_count(key, part):
    return slot_counts(jax.random.fold_in(key, 12), QCAP)


def draw_key_index(key, part):
    return slot_positions(jax.random.fold_in(key, 21), KCAP)


def draw_key_count(key, part):
    return slot_counts(jax.random.fold_in(key, 22), KCAP)


def draw_feed_slot(key, part):
    devices = LEN // TOK_SEQDEV
    groups = BATCH // SEQS
    local = SEQS * TOK_SEQDEV
    capacity = FFN_CAP
    key_one, key_two, key_three = jax.random.split(jax.random.fold_in(key, 31), 3)
    counts = jax.random.randint(key_one, (groups, devices), max(1, local // 16), local // 4 + 1)
    heavy_load = min(local, max(local // 4, devices * capacity))
    chosen = jax.random.randint(key_two, (groups, 1), 0, devices)
    counts = jnp.where(jnp.arange(devices)[None, :] == chosen, heavy_load, counts)
    orders = jax.vmap(lambda item: jax.random.permutation(item, local))(jax.random.split(key_three, groups * devices))
    ranking = jnp.argsort(orders, axis=-1, stable=True).reshape(groups, devices, local)
    routed = ranking < counts[:, :, None]
    position = jnp.cumsum(routed.astype(jnp.int32), axis=-1) - 1
    target = (jnp.arange(devices)[None, :, None] + position) % devices
    column = position // devices
    valid = routed & (column < capacity)
    slots = jnp.where(valid, target * capacity + column, -1)
    slots = slots.reshape(groups, devices, SEQS, TOK_SEQDEV).transpose(0, 2, 1, 3)
    return slots.reshape(BATCH, LEN).astype(jnp.int32)


def level_of(rng, shape, cuts, low, top_value):
    loudness = 1.0
    for axis_at, shards_of in cuts:
        draws = jax.random.uniform(jax.random.fold_in(jax.random.fold_in(rng, 6), axis_at), (shards_of,), jnp.float32, low / len(cuts), top_value / len(cuts))
        loudness = loudness * jnp.repeat(jnp.exp(draws), shape[axis_at] // shards_of).reshape((-1,) + (1,) * (len(shape) - 1 - axis_at))
    return loudness


def noise(rng, shape, spread, limit, cuts=(), kind=jnp.bfloat16):
    values = jax.random.normal(rng, shape, jnp.float32) * spread
    if len(cuts) > 0:
        values = level_of(rng, shape, cuts, -0.22, 0.18) * values
    return jnp.clip(values, min=-limit, max=limit).astype(kind)


def setup_inputs(seed: int = 0) -> dict:
    splits = jax.random.split(jax.random.key(seed), 20)
    layer_input = noise(splits[0], (BATCH, LEN, D), 1.0, 6.0, ((0, 4), (1, 8)))
    cotangent = noise(splits[1], (BATCH, LEN, D), 1.0, 6.0, ((0, 4), (1, 8)))
    first_gain = jnp.clip(1.0 + 0.18 * jax.random.normal(splits[2], (D,), jnp.float32), 0.099609375, 1.8984375).astype(jnp.bfloat16)
    light_inputs = noise(splits[3], (D, 3 * D), D ** -0.5, 0.21875)
    light_output = noise(splits[4], (D, D), (D // 16) ** -0.5, 0.875)
    heavy_queries = noise(splits[5], (D, D), D ** -0.5, 0.21875)
    heavy_keyvalue = noise(splits[6], (D, 2 * D), D ** -0.5, 0.21875)
    heavy_output = noise(splits[7], (D, D), (D // 64) ** -0.5, 1.75)
    second_gain = jnp.clip(1.0 + 0.18 * jax.random.normal(splits[8], (D,), jnp.float32), 0.099609375, 1.8984375).astype(jnp.bfloat16)
    router = noise(splits[9], (D,), D ** -0.5, 0.21875)
    light_gates = noise(splits[10], (D, 2 * FL), D ** -0.5, 0.21875)
    light_down = noise(splits[11], (FL, D), (FL // 2) ** -0.5, 0.25)
    heavy_gates = noise(splits[12], (D, 2 * FH), D ** -0.5, 0.21875)
    heavy_down = noise(splits[13], (FH, D), (FH // 8) ** -0.5, 0.25)
    query_index = draw_query_index(jax.random.fold_in(splits[19], 71), 0)
    query_count = draw_query_count(jax.random.fold_in(splits[19], 71), 0)
    key_index = draw_key_index(jax.random.fold_in(splits[19], 71), 0)
    key_count = draw_key_count(jax.random.fold_in(splits[19], 71), 0)
    feed_slot = draw_feed_slot(jax.random.fold_in(splits[19], 71), 0)
    return {"layer_input": layer_input, "cotangent": cotangent, "first_gain": first_gain, "light_inputs": light_inputs, "light_output": light_output, "heavy_queries": heavy_queries, "heavy_keyvalue": heavy_keyvalue, "heavy_output": heavy_output, "second_gain": second_gain, "router": router, "light_gates": light_gates, "light_down": light_down, "heavy_gates": heavy_gates, "heavy_down": heavy_down, "query_index": query_index, "query_count": query_count, "key_index": key_index, "key_count": key_count, "feed_slot": feed_slot}


epsilon = 1e-06
precise = lax.Precision.HIGHEST

@jax.custom_vjp
def low(v):
    return lax.optimization_barrier(v.astype(jnp.bfloat16)).astype(jnp.float32)

@jax.custom_vjp
def low_back(v):
    return v

def low_keep(v):
    return (low(v), None)

def low_pass(kept, grad):
    return (grad,)

def back_keep(v):
    return (v, None)

def back_low(kept, grad):
    return (low(grad),)
low.defvjp(low_keep, low_pass)
low_back.defvjp(back_keep, back_low)

def matmul(matrix, factor):
    return jnp.dot(matrix, factor, precision=precise, preferred_element_type=jnp.float32)

def norm_rows(values, scales):
    return values * lax.rsqrt(lax.optimization_barrier(jnp.mean(values * values, axis=-1, keepdims=True)) + epsilon) * scales

def glu_rows(joined):
    split_at = joined.shape[-1] // 2
    return jax.nn.gelu(joined[..., :split_at]) * joined[..., split_at:]

def banded_attention(queries, keys_all, values_all):
    length = queries.shape[0]
    block_rows = min(512, length)
    padding = ((RADIUS, RADIUS), (0, 0), (0, 0))
    keys_pad = jnp.pad(keys_all, padding)
    values_pad = jnp.pad(values_all, padding)

    def one_block(offset):
        query_part = lax.dynamic_slice_in_dim(queries, offset, block_rows, 0)
        key_part = lax.dynamic_slice_in_dim(keys_pad, offset, block_rows + 2 * RADIUS, 0)
        value_part = lax.dynamic_slice_in_dim(values_pad, offset, block_rows + 2 * RADIUS, 0)
        scores = low_back(jnp.einsum('qhe,khe->hqk', query_part, key_part, precision=precise) * LHD ** (-0.5))
        row_pos = offset + jnp.arange(block_rows, dtype=jnp.int32)
        col_pos = offset - RADIUS + jnp.arange(block_rows + 2 * RADIUS, dtype=jnp.int32)
        keep_mask = (jnp.abs(row_pos[:, None] - col_pos[None, :]) <= RADIUS) & (col_pos[None, :] >= 0) & (col_pos[None, :] < length)
        weights = low(jax.nn.softmax(jnp.where(keep_mask[None], scores, -1e+30), axis=-1))
        return jnp.einsum('hqk,khe->qhe', weights, value_part, precision=precise)
    offsets = jnp.arange(length // block_rows, dtype=jnp.int32) * block_rows
    mixture = lax.map(jax.checkpoint(one_block), offsets)
    return mixture.reshape(length, HL * LHD)

def routed_attention(queries, keys_all, values_all, key_live):
    query_total = queries.shape[0]

    def one_block(offset):
        query_part = lax.dynamic_slice_in_dim(queries, offset, QCAP, 0)
        keys_here = low_back(keys_all)
        values_here = low_back(values_all)
        scores = low_back(jnp.einsum('qhe,khe->hqk', query_part, keys_here, precision=precise) * HHD ** (-0.5))
        weights = low(jax.nn.softmax(jnp.where(key_live[None, None, :], scores, -1e+30), axis=-1))
        return jnp.einsum('hqk,khe->qhe', weights, values_here, precision=precise)
    offsets = jnp.arange(query_total // QCAP, dtype=jnp.int32) * QCAP
    mixture = lax.map(jax.checkpoint(one_block), offsets)
    return mixture.reshape(query_total, HH * HHD)

def block_forward(params, inputs, seq_query_index, seq_query_count, seq_key_index, seq_key_count, seq_slots):
    first_gain, light_inputs, light_output, heavy_queries, heavy_keyvalue, heavy_output, second_gain, router, light_gates, light_down, heavy_gates, heavy_down = params
    length = inputs.shape[0]
    starts = jnp.arange(N_SEQ, dtype=jnp.int32)[:, None] * TOK_SEQDEV
    query_pos = (seq_query_index.reshape(N_SEQ, QCAP) + starts).reshape(-1)
    query_live = (jnp.arange(QCAP, dtype=jnp.int32)[None, :] < seq_query_count[:, None]).reshape(-1)
    key_pos = (seq_key_index.reshape(N_SEQ, KCAP) + starts).reshape(-1)
    key_live = (jnp.arange(KCAP, dtype=jnp.int32)[None, :] < seq_key_count[:, None]).reshape(-1)
    normed_first = low(norm_rows(inputs, first_gain))
    projected = low_back(low(matmul(normed_first, light_inputs)))
    light_query = projected[:, :D].reshape(length, HL, LHD)
    light_keys = projected[:, D:2 * D].reshape(length, HL, LHD)
    light_values = projected[:, 2 * D:].reshape(length, HL, LHD)
    light_att = low_back(low(banded_attention(light_query, light_keys, light_values)))
    light_branch = low_back(matmul(light_att, light_output))
    heavy_query = low_back(low(matmul(normed_first[query_pos], heavy_queries))).reshape(-1, HH, HHD)
    heavy_pairs = low_back(low(matmul(normed_first[key_pos], heavy_keyvalue)))
    heavy_keys = heavy_pairs[:, :D].reshape(-1, HH, HHD)
    heavy_values = heavy_pairs[:, D:].reshape(-1, HH, HHD)
    heavy_att = low_back(low(routed_attention(heavy_query, heavy_keys, heavy_values, key_live)))
    heavy_rows = low_back(matmul(heavy_att, heavy_output))
    heavy_branch = jnp.zeros_like(inputs).at[query_pos].add(jnp.where(query_live[:, None], heavy_rows, 0.0))
    middle = inputs + light_branch + heavy_branch
    normed_second = low(norm_rows(middle, second_gain))
    light_hidden = low(glu_rows(low_back(matmul(normed_second, light_gates))))
    light_feed = low_back(matmul(light_hidden, light_down))
    heavy_hidden = low(glu_rows(low_back(matmul(normed_second, heavy_gates))))
    heavy_result = low_back(low(matmul(heavy_hidden, heavy_down)))
    gating = jax.nn.sigmoid(matmul(normed_second, router))
    routed = seq_slots >= 0
    heavy_feed = jnp.where(routed[:, None], gating[:, None] * heavy_result, 0.0)
    return middle + light_feed + heavy_feed

def reference(layer_input, cotangent, first_gain, light_inputs, light_output, heavy_queries, heavy_keyvalue, heavy_output, second_gain, router, light_gates, light_down, heavy_gates, heavy_down, query_index, query_count, key_index, key_count, feed_slot):
    params = tuple((weight.astype(jnp.float32) for weight in (first_gain, light_inputs, light_output, heavy_queries, heavy_keyvalue, heavy_output, second_gain, router, light_gates, light_down, heavy_gates, heavy_down)))
    starting = tuple((jnp.zeros(weight.shape, jnp.float32) for weight in params))

    def one_sequence(running, sequence):
        inputs, seq_cotangent, seq_query_index, seq_query_count, seq_key_index, seq_key_count, seq_slots = sequence

        def forward(weights, values):
            return block_forward(weights, values, seq_query_index, seq_query_count, seq_key_index, seq_key_count, seq_slots)
        result, pullback = jax.vjp(forward, params, inputs.astype(jnp.float32))
        grad_params, grad_inputs = pullback(seq_cotangent.astype(jnp.float32))
        running = tuple((earlier + addend for earlier, addend in zip(running, grad_params)))
        return (running, (result.astype(jnp.bfloat16), grad_inputs))
    totals, (output, input_grad) = lax.scan(one_sequence, starting, (layer_input, cotangent, query_index, query_count, key_index, key_count, feed_slot))
    return (output, input_grad, totals[0], totals[1], totals[2], totals[3], totals[4], totals[5], totals[6], totals[7], totals[8], totals[9], totals[10], totals[11])
```

```python
import functools
import jax
import jax.numpy as jnp
from jax import lax
from jax.experimental import pallas as pl
from jax.experimental.pallas import tpu as pltpu
from jax.sharding import PartitionSpec as P
D = 768
HL = 8
LHD = 96
HH = 12
HHD = 64
RADIUS = 128
QCAP = 64
KCAP = 64
CORES = 2
DEPTH = 4
MESH = pl.DeviceIdType.MESH
epsilon = 1e-06
bf16 = jnp.bfloat16
f32 = jnp.float32


def dot(left, right, over):
    return lax.dot_general(left, right, (over, ((), ())), preferred_element_type=f32)


def mm(left, right):
    return dot(left, right, ((1,), (0,)))


def mm_nt(left, right):
    return dot(left, right, ((1,), (1,)))


def mm_tn(left, right):
    return dot(left, right, ((0,), (0,)))


class Ring:
    def __init__(self, axis, stride, count):
        self.axis, self.stride, self.count = axis, stride, count
        self.place = (lax.axis_index(axis) // stride) % count

    def shift(self, value, by):
        total = lax.axis_size(self.axis)
        pairs = []
        for i in range(total):
            c = (i // self.stride) % self.count
            pairs.append((i, i + ((c + by) % self.count - c) * self.stride))
        return lax.ppermute(value, self.axis, pairs)

    def scatter_sum(self, value, dim):
        own = lax.dynamic_index_in_dim(value, self.place, dim, keepdims=False)
        total = own.astype(f32)
        for by in range(1, self.count):
            send = lax.dynamic_index_in_dim(
                value, (self.place + by) % self.count, dim, keepdims=False
            )
            total = total + self.shift(send, by).astype(f32)
        return total

    def gather(self, value):
        return jnp.stack([value] + [self.shift(value, by) for by in range(1, self.count)])

    def return_sum(self, stacked):
        total = stacked[0].astype(f32)
        for by in range(1, self.count):
            total = total + self.shift(stacked[by], self.count - by).astype(f32)
        return total


def norm_parts(values):
    scale = lax.rsqrt(jnp.mean(values * values, axis=-1, keepdims=True) + epsilon)
    return values * scale, scale


def norm_pull(grad, values, scale, gain):
    weighted = grad * gain
    inner = jnp.mean(weighted * values, axis=-1, keepdims=True)
    return scale * weighted - values * (scale * scale * scale) * inner


def glu_rows(gate, up):
    return jax.nn.gelu(gate) * up


def head_windows():
    windows = []
    for h in range(4):
        first, end = h * LHD, (h + 1) * LHD
        windows.append((first // 128 * 128, -(-end // 128) * 128, first, end))
    return windows


def lane_mask(shape, first, end):
    lane = lax.broadcasted_iota(jnp.int32, shape, 1)
    return (lane >= first) & (lane < end)


def join_heads(parts):
    lane = lax.broadcasted_iota(jnp.int32, (parts[0].shape[0], 128), 1)
    return jnp.concatenate(
        [
            jnp.where(lane < 96, parts[0], parts[1][:, :128]),
            jnp.where(lane < 64, parts[1][:, 128:], parts[2][:, :128]),
            jnp.where(lane < 32, parts[2][:, 128:], parts[3]),
        ],
        axis=1,
    )


def light_kernel(ends_ref, own_ref, edge_ref, out_ref):
    half = RADIUS
    factor = LHD ** (-0.5)
    for block in range(2):
        rows = slice(block * half, (block + 1) * half)
        row = lax.broadcasted_iota(jnp.int32, (half, 2 * half), 0)
        col = lax.broadcasted_iota(jnp.int32, (half, 2 * half), 1)
        keep_own = col <= row + half if block == 0 else col >= row
        row, col = row[:, :half], col[:, :half]
        keep_edge = (col >= row if block == 0 else col <= row) & (ends_ref[block] > 0)
        for group in range(2):
            mixed = []
            for a, b, first, end in head_windows():
                lanes = slice(group * 384 + a, group * 384 + b)
                keys = slice(D + lanes.start, D + lanes.stop)
                values = slice(2 * D + lanes.start, 2 * D + lanes.stop)
                query = own_ref[0, rows, lanes]
                query = jnp.where(
                    lane_mask(query.shape, first - a, end - a), query, jnp.zeros_like(query)
                )
                s_own = jnp.where(keep_own, mm_nt(query, own_ref[0, :, keys]), -1e30)
                s_edge = jnp.where(keep_edge, mm_nt(query, edge_ref[0, rows, lanes]), -1e30)
                top = jnp.maximum(
                    jnp.max(s_own, axis=1, keepdims=True), jnp.max(s_edge, axis=1, keepdims=True)
                )
                e_own = jnp.exp((s_own - top) * factor)
                e_edge = jnp.exp((s_edge - top) * factor)
                total = jnp.sum(e_own, axis=1, keepdims=True) + jnp.sum(
                    e_edge, axis=1, keepdims=True
                )
                mix = mm(e_own.astype(bf16), own_ref[0, :, values])
                mix += mm(
                    e_edge.astype(bf16), edge_ref[0, rows, slice(D + lanes.start, D + lanes.stop)]
                )
                mixed.append(mix * (1.0 / total))
            out_ref[0, rows, group * 384 : (group + 1) * 384] = join_heads(mixed).astype(bf16)


def light_attention(ends, own, edge):
    pieces, tokens = own.shape[:2]
    return pl.pallas_call(
        light_kernel,
        out_shape=jax.ShapeDtypeStruct((pieces, tokens, D), bf16),
        grid_spec=pltpu.PrefetchScalarGridSpec(
            num_scalar_prefetch=1,
            grid=(pieces,),
            in_specs=[
                pl.BlockSpec((1, tokens, 3 * D), lambda p, e: (p, 0, 0)),
                pl.BlockSpec((1, 2 * RADIUS, 2 * D), lambda p, e: (p, 0, 0)),
            ],
            out_specs=pl.BlockSpec((1, tokens, D), lambda p, e: (p, 0, 0)),
        ),
        compiler_params=pltpu.CompilerParams(vmem_limit_bytes=32 << 20),
        cost_estimate=pl.CostEstimate(
            flops=pieces * HL * tokens * 384 * 256 * 4,
            bytes_accessed=pieces * (tokens * 4 * D + 2 * RADIUS * 2 * D) * 2,
            transcendentals=pieces * HL * tokens * 384,
        ),
        name="light_attention",
    )(ends, own, edge)


def light_back_kernel(ends_ref, own_ref, edge_ref, grad_ref, own_out, edge_out):
    half = RADIUS
    factor = LHD ** (-0.5)
    for group in range(2):
        dk_own, dv_own = [None] * 4, [None] * 4
        for block in range(2):
            rows = slice(block * half, (block + 1) * half)
            key = lax.broadcasted_iota(jnp.int32, (2 * half, half), 0)
            que = lax.broadcasted_iota(jnp.int32, (2 * half, half), 1)
            keep_own = key <= que + half if block == 0 else key >= que
            key, que = key[:half], que[:half]
            keep_edge = (key >= que if block == 0 else key <= que) & (ends_ref[block] > 0)
            dq, dk_edge, dv_edge = [], [], []
            for h, (a, b, first, end) in enumerate(head_windows()):
                lanes = slice(group * 384 + a, group * 384 + b)
                after = slice(D + lanes.start, D + lanes.stop)
                last = slice(2 * D + lanes.start, 2 * D + lanes.stop)
                mask = lane_mask((half, b - a), first - a, end - a)
                query = own_ref[0, rows, lanes]
                query = jnp.where(mask, query, jnp.zeros_like(query))
                grad = grad_ref[0, rows, lanes]
                grad = jnp.where(mask, grad, jnp.zeros_like(grad))
                k_own, k_edge = own_ref[0, :, after], edge_ref[0, rows, lanes]
                v_own, v_edge = own_ref[0, :, last], edge_ref[0, rows, after]
                s_own = jnp.where(keep_own, mm_nt(k_own, query), -1e30)
                s_edge = jnp.where(keep_edge, mm_nt(k_edge, query), -1e30)
                top = jnp.maximum(
                    jnp.max(s_own, axis=0, keepdims=True), jnp.max(s_edge, axis=0, keepdims=True)
                )
                e_own = jnp.exp((s_own - top) * factor)
                e_edge = jnp.exp((s_edge - top) * factor)
                total = jnp.sum(e_own, axis=0, keepdims=True) + jnp.sum(
                    e_edge, axis=0, keepdims=True
                )
                scale = 1.0 / total
                p_own, p_edge = e_own * scale, e_edge * scale
                g_own, g_edge = mm_nt(v_own, grad), mm_nt(v_edge, grad)
                inner = jnp.sum(p_own * g_own, axis=0, keepdims=True) + jnp.sum(
                    p_edge * g_edge, axis=0, keepdims=True
                )
                d_own = (p_own * (g_own - inner)).astype(bf16)
                d_edge = (p_edge * (g_edge - inner)).astype(bf16)
                dv = mm(p_own.astype(bf16), grad)
                dk = mm(d_own, query)
                dv_own[h] = dv if block == 0 else dv_own[h] + dv
                dk_own[h] = dk if block == 0 else dk_own[h] + dk
                dv_edge.append(mm(p_edge.astype(bf16), grad))
                dk_edge.append(mm(d_edge, query) * factor)
                dq.append((mm_tn(d_own, k_own) + mm_tn(d_edge, k_edge)) * factor)
            at = slice(group * 384, (group + 1) * 384)
            at_v = slice(D + at.start, D + at.stop)
            own_out[0, rows, at] = join_heads(dq).astype(bf16)
            edge_out[0, rows, at] = join_heads(dk_edge).astype(bf16)
            edge_out[0, rows, at_v] = join_heads(dv_edge).astype(bf16)
        at_w = slice(2 * D + at.start, 2 * D + at.stop)
        own_out[0, :, at_v] = (join_heads(dk_own) * factor).astype(bf16)
        own_out[0, :, at_w] = join_heads(dv_own).astype(bf16)


def light_attention_back(ends, own, edge, grad):
    pieces, tokens = own.shape[:2]
    return pl.pallas_call(
        light_back_kernel,
        out_shape=[
            jax.ShapeDtypeStruct((pieces, tokens, 3 * D), bf16),
            jax.ShapeDtypeStruct((pieces, 2 * RADIUS, 2 * D), bf16),
        ],
        grid_spec=pltpu.PrefetchScalarGridSpec(
            num_scalar_prefetch=1,
            grid=(pieces,),
            in_specs=[
                pl.BlockSpec((1, tokens, 3 * D), lambda p, e: (p, 0, 0)),
                pl.BlockSpec((1, 2 * RADIUS, 2 * D), lambda p, e: (p, 0, 0)),
                pl.BlockSpec((1, tokens, D), lambda p, e: (p, 0, 0)),
            ],
            out_specs=[
                pl.BlockSpec((1, tokens, 3 * D), lambda p, e: (p, 0, 0)),
                pl.BlockSpec((1, 2 * RADIUS, 2 * D), lambda p, e: (p, 0, 0)),
            ],
        ),
        compiler_params=pltpu.CompilerParams(vmem_limit_bytes=32 << 20),
        cost_estimate=pl.CostEstimate(
            flops=pieces * HL * tokens * 384 * 256 * 10,
            bytes_accessed=pieces * (tokens * 7 * D + 2 * RADIUS * 4 * D) * 2,
            transcendentals=pieces * HL * tokens * 384,
        ),
        name="light_attention_back",
    )(ends, own, edge, grad)


def spread_heads(value):
    tall = jnp.concatenate([value] * 4, axis=0)
    row = lax.broadcasted_iota(jnp.int32, tall.shape, 0) // QCAP
    lane = lax.broadcasted_iota(jnp.int32, tall.shape, 1) // HHD
    return jnp.where(row == lane, tall, jnp.zeros_like(tall))


def fold_heads(tall):
    lane = lax.broadcasted_iota(jnp.int32, (QCAP, 4 * HHD), 1) // HHD
    total = tall[:QCAP]
    for r in range(1, 4):
        total = jnp.where(lane == r, tall[r * QCAP : (r + 1) * QCAP], total)
    return total


def heavy_kernel(query_ref, pair_ref, live_ref, out_ref):
    factor = HHD ** (-0.5)
    keep = live_ref[0] > 0
    for group in range(HH // 4):
        lanes = slice(group * 256, (group + 1) * 256)
        query = spread_heads(query_ref[0, :, lanes])
        scores = jnp.where(keep, mm_nt(query, pair_ref[0, :, lanes]), -1e30)
        top = jnp.max(scores, axis=1, keepdims=True)
        raised = jnp.exp((scores - top) * factor)
        total = jnp.sum(raised, axis=1, keepdims=True)
        mix = mm(raised.astype(bf16), pair_ref[0, :, D + lanes.start : D + lanes.stop])
        out_ref[0, :, lanes] = fold_heads(mix * (1.0 / total)).astype(bf16)


def heavy_attention(query, pairs, live):
    pieces, slots = pairs.shape[:2]
    return pl.pallas_call(
        heavy_kernel,
        out_shape=jax.ShapeDtypeStruct((pieces, QCAP, D), bf16),
        grid=(pieces,),
        in_specs=[
            pl.BlockSpec((1, QCAP, D), lambda p: (p, 0, 0)),
            pl.BlockSpec((1, slots, 2 * D), lambda p: (p, 0, 0)),
            pl.BlockSpec((1, 1, slots), lambda p: (p, 0, 0)),
        ],
        out_specs=pl.BlockSpec((1, QCAP, D), lambda p: (p, 0, 0)),
        compiler_params=pltpu.CompilerParams(vmem_limit_bytes=32 << 20),
        cost_estimate=pl.CostEstimate(
            flops=pieces * 3 * 4 * 256 * 256 * slots,
            bytes_accessed=pieces * (slots + QCAP) * 2 * D * 2,
            transcendentals=pieces * HH * QCAP * slots,
        ),
        name="heavy_attention",
    )(query, pairs, live)


def heavy_back_kernel(query_ref, pair_ref, live_ref, grad_ref, query_out, pair_out):
    factor = HHD ** (-0.5)
    keep = live_ref[0] > 0
    for group in range(HH // 4):
        lanes = slice(group * 256, (group + 1) * 256)
        after = slice(D + lanes.start, D + lanes.stop)
        query = spread_heads(query_ref[0, :, lanes])
        grad = spread_heads(grad_ref[0, :, lanes])
        keys = pair_ref[0, :, lanes]
        scores = jnp.where(keep, mm_nt(keys, query), -1e30)
        top = jnp.max(scores, axis=0, keepdims=True)
        raised = jnp.exp((scores - top) * factor)
        probs = raised * (1.0 / jnp.sum(raised, axis=0, keepdims=True))
        grad_probs = mm_nt(pair_ref[0, :, after], grad)
        inner = jnp.sum(probs * grad_probs, axis=0, keepdims=True)
        grad_scores = (probs * (grad_probs - inner)).astype(bf16)
        pair_out[0, :, after] = mm(probs.astype(bf16), grad).astype(bf16)
        pair_out[0, :, lanes] = (mm(grad_scores, query) * factor).astype(bf16)
        query_out[0, :, lanes] = (fold_heads(mm_tn(grad_scores, keys)) * factor).astype(bf16)


def heavy_attention_back(query, pairs, live, grad):
    pieces, slots = pairs.shape[:2]
    return pl.pallas_call(
        heavy_back_kernel,
        out_shape=[
            jax.ShapeDtypeStruct((pieces, QCAP, D), bf16),
            jax.ShapeDtypeStruct((pieces, slots, 2 * D), bf16),
        ],
        grid=(pieces,),
        in_specs=[
            pl.BlockSpec((1, QCAP, D), lambda p: (p, 0, 0)),
            pl.BlockSpec((1, slots, 2 * D), lambda p: (p, 0, 0)),
            pl.BlockSpec((1, slots, 1), lambda p: (p, 0, 0)),
            pl.BlockSpec((1, QCAP, D), lambda p: (p, 0, 0)),
        ],
        out_specs=[
            pl.BlockSpec((1, QCAP, D), lambda p: (p, 0, 0)),
            pl.BlockSpec((1, slots, 2 * D), lambda p: (p, 0, 0)),
        ],
        compiler_params=pltpu.CompilerParams(vmem_limit_bytes=32 << 20),
        cost_estimate=pl.CostEstimate(
            flops=pieces * 3 * 10 * 256 * 256 * slots,
            bytes_accessed=pieces * (2 * slots + 2 * QCAP) * 2 * D * 2,
            transcendentals=pieces * HH * QCAP * slots,
        ),
        name="heavy_attention_back",
    )(query, pairs, live, grad)


def reduce_kernel(jobs, sizes, *refs):
    n_x, n_y = sizes
    count = len(jobs)
    sources, outs, scratch = refs[:count], refs[count : 2 * count], refs[2 * count :]
    names = ("own", "core", "ax", "ay", "by", "bx", "zz", "lsem", "rsem", "ssem")
    held = [
        dict(zip(names, scratch[len(names) * a : len(names) * (a + 1)])) for a in range(count)
    ]
    dp, seq = lax.axis_index("dp"), lax.axis_index("seq")
    x, c = dp // CORES, dp % CORES
    z, y = seq // n_y, seq % n_y

    def to_core():
        return (x * CORES + (1 - c), seq)

    def to_x(by):
        return (((x + by) % n_x) * CORES + c, seq)

    def to_y(by):
        return (dp, z * n_y + (y + by) % n_y)

    def to_z(by):
        return (dp, ((z + by) % DEPTH) * n_y + y)

    peers = [to_core()]
    peers += [to_x(by) for by in range(1, n_x)]
    peers += [to_y(by) for by in range(1, n_y)]
    peers += [to_z(by) for by in range(1, DEPTH)]
    barrier = pltpu.get_barrier_semaphore()
    for peer in peers:
        pl.semaphore_signal(barrier, inc=1, device_id=peer, device_id_type=MESH)
    pl.semaphore_wait(barrier, len(peers))

    def send(src, dst, a, stage, k, peer):
        h = held[a]
        pltpu.make_async_remote_copy(
            src_ref=src,
            dst_ref=dst,
            send_sem=h["ssem"].at[stage],
            recv_sem=h["rsem"].at[stage, k],
            device_id=peer,
            device_id_type=MESH,
        ).start()

    def arrived(buffer, a, stage, k):
        h = held[a]
        pltpu.make_async_remote_copy(
            src_ref=buffer,
            dst_ref=buffer,
            send_sem=h["ssem"].at[stage],
            recv_sem=h["rsem"].at[stage, k],
            device_id=to_core(),
            device_id_type=MESH,
        ).wait_recv()

    def columns(a, k):
        width = jobs[a][0]
        return pl.ds(k * width, width)

    def local(a, k):
        h = held[a]
        return pltpu.make_async_copy(
            sources[a].at[:, c, :, :, :, columns(a, k)], h["own"].at[k], h["lsem"].at[k]
        )

    def stage_core_start(a, k):
        local(a, k).start()
        send(
            sources[a].at[:, 1 - c, :, :, :, columns(a, k)],
            held[a]["core"].at[k],
            a,
            0,
            k,
            to_core(),
        )

    def add_blocks(total, index_of, pieces):
        @pl.loop(0, total)
        def _(i):
            for target, addend in pieces:
                at = index_of(i)
                target[at] = target[at] + addend[at]

    def stage_core(a, k):
        h = held[a]
        local(a, k).wait()
        arrived(h["core"].at[k], a, 0, k)
        own, other = h["own"], h["core"]

        @pl.loop(0, n_x * DEPTH)
        def _(i):
            for j in range(n_y):
                at = (k, i // DEPTH, i % DEPTH, j)
                own[at] = own[at] + other[at]

        half = k // 2
        if k % 2 == 0:
            for by in range(1, n_x):
                send(own.at[k, (x + by) % n_x], h["ax"].at[half, by - 1], a, 1, k, to_x(by))
        else:
            for by in range(1, n_y):
                send(own.at[k, :, :, (y + by) % n_y], h["by"].at[half, by - 1], a, 2, k, to_y(by))

    def stage_second(a, k):
        h = held[a]
        own, half = h["own"], k // 2
        if k % 2 == 0:
            arrived(h["ax"].at[half], a, 1, k)

            @pl.loop(0, DEPTH)
            def _(i):
                for j in range(n_y):
                    for s in range(n_x - 1):
                        at = (k, x, i, j)
                        own[at] = own[at] + h["ax"][half, s, i, j]

            for by in range(1, n_y):
                send(
                    own.at[k, x, :, (y + by) % n_y], h["ay"].at[half, by - 1], a, 2, k, to_y(by)
                )
        else:
            arrived(h["by"].at[half], a, 2, k)

            @pl.loop(0, DEPTH)
            def _(i):
                for j in range(n_x):
                    for s in range(n_y - 1):
                        at = (k, j, i, y)
                        own[at] = own[at] + h["by"][half, s, j, i]

            for by in range(1, n_x):
                send(
                    own.at[k, (x + by) % n_x, :, y], h["bx"].at[half, by - 1], a, 1, k, to_x(by)
                )

    def stage_third(a, k):
        h = held[a]
        own, half = h["own"], k // 2
        name, stage, others = ("ay", 2, n_y - 1) if k % 2 == 0 else ("bx", 1, n_x - 1)
        arrived(h[name].at[half], a, stage, k)

        @pl.loop(0, DEPTH)
        def _(i):
            for s in range(others):
                at = (k, x, i, y)
                own[at] = own[at] + h[name][half, s, i]

        for by in range(1, DEPTH):
            send(own.at[k, x, (z + by) % DEPTH, y], h["zz"].at[k, by - 1], a, 3, k, to_z(by))

    def stage_last(a, k):
        h = held[a]
        width = jobs[a][0]
        arrived(h["zz"].at[k], a, 3, k)
        total = h["own"][k, x, z, y].astype(f32)
        for s in range(DEPTH - 1):
            total = total + h["zz"][k, s].astype(f32)
        outs[a][:, k * width : (k + 1) * width] = total

    order = [(a, k) for a in range(count) for k in range(jobs[a][1])]
    for a, k in order:
        stage_core_start(a, k)
    lags = [(stage_core, 0), (stage_second, 4), (stage_third, 8), (stage_last, 12)]
    for step in range(len(order) + lags[-1][1]):
        for stage, lag in lags:
            if 0 <= step - lag < len(order):
                stage(*order[step - lag])

    for a in range(count):
        h = held[a]

        def sent(buffer, stage):
            pltpu.make_async_remote_copy(
                src_ref=buffer,
                dst_ref=buffer,
                send_sem=h["ssem"].at[stage],
                recv_sem=h["rsem"].at[stage, 0],
                device_id=to_core(),
                device_id_type=MESH,
            ).wait_send()

        sent(h["core"], 0)
        sent(h["ax"], 1)
        sent(h["bx"], 1)
        sent(h["by"], 2)
        sent(h["ay"], 2)
        sent(h["zz"], 3)


def reduce_all(values, widths, n_x, n_y, collective_id):
    jobs, operands, out_shape, scratch = [], [], [], []
    devices = n_x * CORES * DEPTH * n_y
    for value, width in zip(values, widths):
        height, columns = value.shape
        chunk = height // devices
        k = columns // width
        jobs.append((width, k))
        operands.append(value.reshape(n_x, CORES, DEPTH, n_y, chunk, columns))
        out_shape.append(jax.ShapeDtypeStruct((chunk, columns), f32))
        tile = (chunk, width)
        scratch += [
            pltpu.VMEM((k, n_x, DEPTH, n_y) + tile, bf16),
            pltpu.VMEM((k, n_x, DEPTH, n_y) + tile, bf16),
            pltpu.VMEM((k // 2, n_x - 1, DEPTH, n_y) + tile, bf16),
            pltpu.VMEM((k // 2, n_y - 1, DEPTH) + tile, bf16),
            pltpu.VMEM((k // 2, n_y - 1, n_x, DEPTH) + tile, bf16),
            pltpu.VMEM((k // 2, n_x - 1, DEPTH) + tile, bf16),
            pltpu.VMEM((k, DEPTH - 1) + tile, bf16),
            pltpu.SemaphoreType.DMA((k,)),
            pltpu.SemaphoreType.DMA((4, k)),
            pltpu.SemaphoreType.DMA((4,)),
        ]
    total = sum(v.size for v in values)
    return pl.pallas_call(
        functools.partial(reduce_kernel, tuple(jobs), (n_x, n_y)),
        out_shape=out_shape,
        in_specs=[pl.BlockSpec(memory_space=pl.ANY)] * len(values),
        out_specs=[pl.BlockSpec(memory_space=pltpu.VMEM)] * len(values),
        scratch_shapes=scratch,
        compiler_params=pltpu.CompilerParams(
            collective_id=collective_id, has_side_effects=True, vmem_limit_bytes=60 << 20
        ),
        cost_estimate=pl.CostEstimate(flops=2 * total, bytes_accessed=4 * total, transcendentals=0),
        name="reduce_gradients",
    )(*operands)


def per_device(
    layer_input,
    cotangent,
    first_gain,
    light_inputs,
    light_output,
    heavy_queries,
    heavy_keyvalue,
    heavy_output,
    second_gain,
    router,
    light_gates,
    light_down,
    heavy_gates,
    heavy_down,
    query_index,
    query_count,
    key_index,
    key_count,
    feed_slot,
):
    pieces, tokens = layer_input.shape[:2]
    rows = pieces * tokens
    n_dp, n_seq = lax.axis_size("dp"), lax.axis_size("seq")
    n_x, n_y = n_dp // CORES, n_seq // DEPTH
    seq_rank = lax.axis_index("seq")
    core = Ring("dp", 1, CORES)
    ring_x = Ring("dp", CORES, n_x)
    ring_y = Ring("seq", 1, n_y)
    ring_z = Ring("seq", n_y, DEPTH)
    capacity = max(2, 3 * rows // (16 * n_seq))
    slots = n_seq * capacity
    light_factor = LHD ** (-0.5)
    heavy_factor = HHD ** (-0.5)

    def reduce_grad(value, first, second):
        height, width = value.shape
        chunk = height // (n_dp * n_seq)
        parts = value.reshape(n_x, CORES, DEPTH, n_y, chunk, width)
        parts = core.scatter_sum(parts, 1).astype(bf16)
        dims = ["x", "z", "y"]
        rings = {"x": ring_x, "y": ring_y, "z": ring_z}
        order = [first, second, [d for d in dims if d not in (first, second)][0]]
        for i, d in enumerate(order):
            at = dims.index(d)
            parts = rings[d].scatter_sum(parts, at)
            if i < 2:
                parts = parts.astype(bf16)
            dims.remove(d)
        return parts

    def reduce_split(value):
        half = value.shape[1] // 2
        return jnp.concatenate(
            [
                reduce_grad(value[:, :half], "x", "y"),
                reduce_grad(value[:, half:], "y", "x"),
            ],
            axis=1,
        )

    def reduce_vectors(value):
        count, width = value.shape
        chunk = width // (n_dp * n_seq)
        parts = value.reshape(count, n_x, CORES, DEPTH, n_y, chunk)
        parts = core.scatter_sum(parts, 2)
        parts = ring_x.scatter_sum(parts, 1)
        parts = ring_z.scatter_sum(parts, 1)
        return ring_y.scatter_sum(parts, 1)

    ends = n_seq - 1
    left_rows = lax.ppermute(
        layer_input[:, tokens - RADIUS :], "seq", [(i, i + 1) for i in range(ends)]
    )
    right_rows = lax.ppermute(layer_input[:, :RADIUS], "seq", [(i + 1, i) for i in range(ends)])
    position = jnp.arange(tokens, dtype=jnp.int32)
    key_pick = (key_index[:, :, None] == position[None, None, :]).astype(bf16)
    query_live = jnp.arange(QCAP, dtype=jnp.int32)[None, :] < query_count
    query_pick = (query_index[:, :, None] == position[None, None, :]).astype(bf16)
    live_pick = query_pick * query_live[:, :, None].astype(bf16)
    key_raw = jnp.einsum("pkt,ptd->pkd", key_pick, layer_input, preferred_element_type=f32).astype(
        bf16
    )
    key_all = ring_y.gather(ring_z.gather(key_raw))

    gain_first = first_gain.astype(f32)
    inputs = layer_input.astype(f32)
    unit_first, scale_first = norm_parts(inputs)
    normed_first = (unit_first * gain_first).astype(bf16)
    normed_flat = normed_first.reshape(rows, D)
    own_proj = mm(normed_flat, light_inputs).astype(bf16).reshape(pieces, tokens, 3 * D)
    edge_rows = jnp.concatenate([left_rows, right_rows], axis=1)
    normed_edge = (norm_parts(edge_rows.astype(f32))[0] * gain_first).astype(bf16)
    edge_flat = normed_edge.reshape(pieces * 2 * RADIUS, D)
    edge_proj = mm(edge_flat, light_inputs[:, D:]).astype(bf16)
    edge_proj = edge_proj.reshape(pieces, 2 * RADIUS, 2 * D)

    reach = jnp.stack([seq_rank > 0, seq_rank < n_seq - 1]).astype(jnp.int32)
    light_att = light_attention(reach, own_proj, edge_proj).reshape(rows, D)

    key_slots = n_seq * KCAP
    key_rows_all = key_all.transpose(2, 0, 1, 3, 4).reshape(pieces * key_slots, D)
    normed_keys = (norm_parts(key_rows_all.astype(f32))[0] * gain_first).astype(bf16)
    heavy_pairs = mm(normed_keys, heavy_keyvalue).astype(bf16).reshape(pieces, key_slots, 2 * D)
    from_z = (ring_z.place - jnp.arange(DEPTH, dtype=jnp.int32)) % DEPTH
    from_y = (ring_y.place - jnp.arange(n_y, dtype=jnp.int32)) % n_y
    sources = (from_z[None, :] * n_y + from_y[:, None]).reshape(-1)
    counts_here = jnp.sum(
        jnp.where(
            sources[None, :, None] == jnp.arange(n_seq, dtype=jnp.int32)[None, None, :],
            key_count[:, None, :],
            0,
        ),
        axis=-1,
    )
    key_live = jnp.arange(KCAP, dtype=jnp.int32)[None, None, :] < counts_here[:, :, None]
    key_live = key_live.reshape(pieces, 1, key_slots).astype(f32)
    query_rows = (
        jnp.einsum("pqt,ptd->pqd", query_pick, normed_first, preferred_element_type=f32)
        .astype(bf16)
        .reshape(pieces * QCAP, D)
    )
    heavy_query = mm(query_rows, heavy_queries).astype(bf16).reshape(pieces, QCAP, D)
    heavy_att = heavy_attention(heavy_query, heavy_pairs, key_live)
    heavy_spread = (
        jnp.einsum("pqt,pqd->ptd", live_pick, heavy_att, preferred_element_type=f32)
        .astype(bf16)
        .reshape(rows, D)
    )

    middle = (
        inputs.reshape(rows, D) + mm(light_att, light_output) + mm(heavy_spread, heavy_output)
    )
    gain_second = second_gain.astype(f32)
    unit_second, scale_second = norm_parts(middle)
    normed_second = (unit_second * gain_second).astype(bf16)

    slot_of = feed_slot.reshape(1, rows)
    pick = (jnp.arange(slots, dtype=jnp.int32)[:, None] == slot_of).astype(bf16)
    routed = feed_slot.reshape(rows, 1) >= 0
    cot = cotangent.reshape(rows, D)
    gating = jax.nn.sigmoid(
        jnp.sum(normed_second.astype(f32) * router.astype(f32), axis=-1, keepdims=True)
    )
    grad_token = (gating * cot.astype(f32)).astype(bf16)
    feed_in = mm(pick, normed_second).astype(bf16)
    grad_in = mm(pick, grad_token).astype(bf16)

    hidden = light_gates.shape[1] // 2
    light_gate = mm(normed_second, light_gates[:, :hidden])
    light_up = mm(normed_second, light_gates[:, hidden:])
    light_act, light_pull = jax.vjp(glu_rows, light_gate, light_up)
    light_act = light_act.astype(bf16)
    light_feed = mm(light_act, light_down)
    grad_light_gate, grad_light_up = light_pull(mm_nt(cot, light_down))
    grad_light_pre = jnp.concatenate([grad_light_gate.astype(bf16), grad_light_up.astype(bf16)], 1)

    wide_hidden = heavy_gates.shape[1] // 2
    heavy_gate = mm(feed_in, heavy_gates[:, :wide_hidden])
    heavy_up = mm(feed_in, heavy_gates[:, wide_hidden:])
    heavy_act, heavy_pull = jax.vjp(glu_rows, heavy_gate, heavy_up)
    heavy_act = heavy_act.astype(bf16)
    heavy_result = mm(heavy_act, heavy_down).astype(bf16)
    grad_heavy_gate, grad_heavy_up = heavy_pull(mm_nt(grad_in, heavy_down))
    grad_heavy_pre = jnp.concatenate([grad_heavy_gate.astype(bf16), grad_heavy_up.astype(bf16)], 1)
    grad_feed_in = mm_nt(grad_heavy_pre, heavy_gates).astype(bf16)
    heavy_down_grad = mm_tn(heavy_act, grad_in).astype(bf16)
    heavy_gates_grad = mm_tn(feed_in, grad_heavy_pre).astype(bf16)
    light_down_grad = mm_tn(light_act, cot).astype(bf16)
    light_gates_grad = mm_tn(normed_second, grad_light_pre).astype(bf16)

    token_result = mm_tn(pick, heavy_result)
    output = (middle + light_feed + gating * token_result).astype(bf16).reshape(layer_input.shape)
    grad_gating = jnp.sum(cot.astype(f32) * token_result, axis=-1, keepdims=True)
    grad_logit = grad_gating * gating * (1.0 - gating)
    grad_second = (
        mm_nt(grad_light_pre, light_gates)
        + mm_tn(pick, grad_feed_in)
        + grad_logit * router.astype(f32)
    )
    router_grad = jnp.sum(grad_logit * normed_second.astype(f32), axis=0)
    second_gain_grad = jnp.sum(grad_second * unit_second, axis=0)
    grad_middle = cot.astype(f32) + norm_pull(grad_second, middle, scale_second, gain_second)
    grad_mid_low = grad_middle.astype(bf16)

    light_output_grad = mm_tn(light_att, grad_mid_low).astype(bf16)
    grad_light_att = mm_nt(grad_mid_low, light_output).astype(bf16)
    grad_query_rows = (
        jnp.einsum(
            "pqt,ptd->pqd",
            live_pick,
            grad_mid_low.reshape(pieces, tokens, D),
            preferred_element_type=f32,
        )
        .astype(bf16)
        .reshape(pieces * QCAP, D)
    )
    heavy_output_grad = mm_tn(heavy_att.reshape(pieces * QCAP, D), grad_query_rows).astype(bf16)
    grad_heavy_att = mm_nt(grad_query_rows, heavy_output).astype(bf16)

    grad_hq_low, grad_hkv_low = heavy_attention_back(
        heavy_query,
        heavy_pairs,
        key_live.reshape(pieces, key_slots, 1),
        grad_heavy_att.reshape(pieces, QCAP, D),
    )
    grad_hq_low = grad_hq_low.reshape(pieces * QCAP, D)
    grad_hkv_low = grad_hkv_low.reshape(pieces * key_slots, 2 * D)
    grad_key_rows = mm_nt(grad_hkv_low, heavy_keyvalue).astype(bf16)
    grad_key_rows = grad_key_rows.reshape(pieces, n_y, DEPTH, KCAP, D).transpose(1, 2, 0, 3, 4)
    grad_key_own = ring_z.return_sum(ring_y.return_sum(grad_key_rows).astype(bf16))
    heavy_keyvalue_grad = mm_tn(normed_keys, grad_hkv_low).astype(bf16)
    heavy_queries_grad = mm_tn(query_rows, grad_hq_low).astype(bf16)

    grad_own, grad_edge = light_attention_back(
        reach, own_proj, edge_proj, grad_light_att.reshape(pieces, tokens, D)
    )
    grad_own = grad_own.reshape(rows, 3 * D)
    grad_edge = grad_edge.reshape(pieces * 2 * RADIUS, 2 * D)
    grad_edge_rows = mm_nt(grad_edge, light_inputs[:, D:]).astype(bf16)
    grad_edge_rows = grad_edge_rows.reshape(pieces, 2 * RADIUS, D)
    from_right = lax.ppermute(
        grad_edge_rows[:, :RADIUS], "seq", [(i + 1, i) for i in range(ends)]
    )
    from_left = lax.ppermute(
        grad_edge_rows[:, RADIUS:], "seq", [(i, i + 1) for i in range(ends)]
    )
    light_inputs_grad = jnp.concatenate(
        [
            mm_tn(normed_flat, grad_own[:, :D]),
            mm_tn(normed_flat, grad_own[:, D:]) + mm_tn(edge_flat, grad_edge),
        ],
        axis=1,
    ).astype(bf16)

    grad_hq_rows = mm_nt(grad_hq_low, heavy_queries).astype(bf16).reshape(pieces, QCAP, D)
    grad_first = mm_nt(grad_own, light_inputs).reshape(pieces, tokens, D)
    grad_first = (
        grad_first
        + jnp.einsum("pqt,pqd->ptd", query_pick, grad_hq_rows, preferred_element_type=f32)
        + jnp.einsum("pkt,pkd->ptd", key_pick, grad_key_own.astype(bf16), preferred_element_type=f32)
        + jnp.concatenate([from_left, from_right], axis=1).astype(f32)
    )
    first_gain_grad = jnp.sum(grad_first * unit_first, axis=(0, 1))
    input_grad = grad_middle.reshape(pieces, tokens, D) + norm_pull(
        grad_first, inputs, scale_first, gain_first
    )
    vectors = jnp.stack([first_gain_grad, second_gain_grad, router_grad])
    devices = n_dp * n_seq
    feed_grads = [heavy_gates_grad, heavy_down_grad, light_gates_grad, light_down_grad]
    late_grads = [
        light_inputs_grad,
        light_output_grad,
        heavy_queries_grad,
        heavy_keyvalue_grad,
        heavy_output_grad,
    ]
    if D // devices % 8 == 0:
        each = D // devices
        lines = vectors.reshape(3, devices, each).transpose(1, 0, 2)
        lines = jnp.pad(lines, ((0, 0), (0, 5), (0, 256 - each))).reshape(devices * 8, 256)
        feed_grads = reduce_all(feed_grads, (512, 128, 512, 384), n_x, n_y, 0)
        *late_grads, lines = reduce_all(
            late_grads + [lines.astype(bf16)], (384,) * 5 + (128,), n_x, n_y, 1
        )
        vectors = lines[:3, :each]
    else:
        feed_grads = [reduce_split(v) for v in feed_grads]
        late_grads = [reduce_split(v) for v in late_grads]
        vectors = reduce_vectors(vectors)
    return (
        output,
        input_grad,
        vectors[0],
        *late_grads,
        vectors[1],
        vectors[2],
        feed_grads[2],
        feed_grads[3],
        feed_grads[0],
        feed_grads[1],
    )


def solution(mesh):
    rows = P(("dp", "seq"), None)
    line = P(("dp", "seq"))
    tokens = P("dp", "seq", None)
    slots = P("dp", "seq")
    return jax.shard_map(
        per_device,
        mesh=mesh,
        in_specs=(tokens, tokens) + (P(),) * 12 + (slots, slots, slots, P("dp", None), slots),
        out_specs=(tokens, tokens, line) + (rows,) * 5 + (line, line) + (rows,) * 4,
        check_vma=False,
    )
```

```python
import functools
import math
import jax
import jax.numpy as jnp
from jax import lax
from jax.experimental import pallas as pl
from jax.experimental.pallas import tpu as pltpu
from jax.sharding import PartitionSpec as P
D = 768
HL = 8
LHD = 96
HH = 12
HHD = 64
RADIUS = 128
QCAP = 64
KCAP = 64
CORES = 2
DEPTH = 4
MESH = pl.DeviceIdType.MESH
epsilon = 1e-06
bf16 = jnp.bfloat16
f32 = jnp.float32


def dot(left, right, over):
    return lax.dot_general(left, right, (over, ((), ())), preferred_element_type=f32)


def mm(left, right):
    return dot(left, right, ((1,), (0,)))


def mm_nt(left, right):
    return dot(left, right, ((1,), (1,)))


def mm_tn(left, right):
    return dot(left, right, ((0,), (0,)))


class Ring:
    def __init__(self, axis, stride, count):
        self.axis, self.stride, self.count = axis, stride, count
        self.place = (lax.axis_index(axis) // stride) % count

    def shift(self, value, by):
        total = lax.axis_size(self.axis)
        pairs = []
        for i in range(total):
            c = (i // self.stride) % self.count
            pairs.append((i, i + ((c + by) % self.count - c) * self.stride))
        return lax.ppermute(value, self.axis, pairs)

    def scatter_sum(self, value, dim):
        own = lax.dynamic_index_in_dim(value, self.place, dim, keepdims=False)
        total = own.astype(f32)
        for by in range(1, self.count):
            send = lax.dynamic_index_in_dim(
                value, (self.place + by) % self.count, dim, keepdims=False
            )
            total = total + self.shift(send, by).astype(f32)
        return total

    def gather(self, value, dim):
        parts = [value] + [self.shift(value, by) for by in range(1, self.count)]
        return jnp.concatenate(parts, axis=dim)

    def return_sum(self, joined, dim):
        parts = jnp.split(joined, self.count, axis=dim)
        total = parts[0].astype(f32)
        for by in range(1, self.count):
            total = total + self.shift(parts[by], self.count - by).astype(f32)
        return total


def norm_parts(values):
    scale = lax.rsqrt(jnp.mean(values * values, axis=-1, keepdims=True) + epsilon)
    return values * scale, scale


def norm_pull(grad, values, scale, gain):
    weighted = grad * gain
    inner = jnp.mean(weighted * values, axis=-1, keepdims=True)
    return scale * weighted - values * (scale * scale * scale) * inner


def glu_rows(gate, up):
    return jax.nn.gelu(gate) * up


def head_windows():
    windows = []
    for h in range(4):
        first, end = h * LHD, (h + 1) * LHD
        windows.append((first // 128 * 128, -(-end // 128) * 128, first, end))
    return windows


def lane_mask(shape, first, end):
    lane = lax.broadcasted_iota(jnp.int32, shape, 1)
    return (lane >= first) & (lane < end)


def join_heads(parts):
    lane = lax.broadcasted_iota(jnp.int32, (parts[0].shape[0], 128), 1)
    return jnp.concatenate(
        [
            jnp.where(lane < 96, parts[0], parts[1][:, :128]),
            jnp.where(lane < 64, parts[1][:, 128:], parts[2][:, :128]),
            jnp.where(lane < 32, parts[2][:, 128:], parts[3]),
        ],
        axis=1,
    )


def light_kernel(ends_ref, own_ref, edge_ref, out_ref):
    half = RADIUS
    factor = LHD ** (-0.5)
    for block in range(2):
        rows = slice(block * half, (block + 1) * half)
        row = lax.broadcasted_iota(jnp.int32, (half, 2 * half), 0)
        col = lax.broadcasted_iota(jnp.int32, (half, 2 * half), 1)
        keep_own = col <= row + half if block == 0 else col >= row
        row, col = row[:, :half], col[:, :half]
        keep_edge = (col >= row if block == 0 else col <= row) & (ends_ref[block] > 0)
        for group in range(2):
            mixed = []
            for a, b, first, end in head_windows():
                lanes = slice(group * 384 + a, group * 384 + b)
                keys = slice(D + lanes.start, D + lanes.stop)
                values = slice(2 * D + lanes.start, 2 * D + lanes.stop)
                query = own_ref[0, rows, lanes]
                query = jnp.where(
                    lane_mask(query.shape, first - a, end - a), query, jnp.zeros_like(query)
                )
                s_own = jnp.where(keep_own, mm_nt(query, own_ref[0, :, keys]), -1e30)
                s_edge = jnp.where(keep_edge, mm_nt(query, edge_ref[0, rows, lanes]), -1e30)
                top = jnp.maximum(
                    jnp.max(s_own, axis=1, keepdims=True), jnp.max(s_edge, axis=1, keepdims=True)
                )
                e_own = jnp.exp((s_own - top) * factor)
                e_edge = jnp.exp((s_edge - top) * factor)
                total = jnp.sum(e_own, axis=1, keepdims=True) + jnp.sum(
                    e_edge, axis=1, keepdims=True
                )
                mix = mm(e_own.astype(bf16), own_ref[0, :, values])
                mix += mm(
                    e_edge.astype(bf16), edge_ref[0, rows, slice(D + lanes.start, D + lanes.stop)]
                )
                mixed.append(mix * (1.0 / total))
            out_ref[0, rows, group * 384 : (group + 1) * 384] = join_heads(mixed).astype(bf16)


def light_attention(ends, own, edge):
    pieces, tokens = own.shape[:2]
    return pl.pallas_call(
        light_kernel,
        out_shape=jax.ShapeDtypeStruct((pieces, tokens, D), bf16),
        grid_spec=pltpu.PrefetchScalarGridSpec(
            num_scalar_prefetch=1,
            grid=(pieces,),
            in_specs=[
                pl.BlockSpec((1, tokens, 3 * D), lambda p, e: (p, 0, 0)),
                pl.BlockSpec((1, 2 * RADIUS, 2 * D), lambda p, e: (p, 0, 0)),
            ],
            out_specs=pl.BlockSpec((1, tokens, D), lambda p, e: (p, 0, 0)),
        ),
        compiler_params=pltpu.CompilerParams(vmem_limit_bytes=32 << 20),
        cost_estimate=pl.CostEstimate(
            flops=pieces * HL * tokens * 384 * 256 * 4,
            bytes_accessed=pieces * (tokens * 4 * D + 2 * RADIUS * 2 * D) * 2,
            transcendentals=pieces * HL * tokens * 384,
        ),
        name="light_attention",
    )(ends, own, edge)


def light_back_unit(reach, groups, own_ref, edge_ref, grad_ref, own_out, edge_out):
    half = RADIUS
    factor = LHD ** (-0.5)
    for group in groups:
        dk_own, dv_own = [None] * 4, [None] * 4
        for block in range(2):
            rows = slice(block * half, (block + 1) * half)
            key = lax.broadcasted_iota(jnp.int32, (2 * half, half), 0)
            que = lax.broadcasted_iota(jnp.int32, (2 * half, half), 1)
            keep_own = key <= que + half if block == 0 else key >= que
            key, que = key[:half], que[:half]
            keep_edge = (key >= que if block == 0 else key <= que) & reach[block]
            dq, dk_edge, dv_edge = [], [], []
            for h, (a, b, first, end) in enumerate(head_windows()):
                lanes = slice(group * 384 + a, group * 384 + b)
                after = slice(D + lanes.start, D + lanes.stop)
                last = slice(2 * D + lanes.start, 2 * D + lanes.stop)
                mask = lane_mask((half, b - a), first - a, end - a)
                query = own_ref[0, rows, lanes]
                query = jnp.where(mask, query, jnp.zeros_like(query))
                grad = grad_ref[0, rows, lanes]
                grad = jnp.where(mask, grad, jnp.zeros_like(grad))
                k_own, k_edge = own_ref[0, :, after], edge_ref[0, rows, lanes]
                v_own, v_edge = own_ref[0, :, last], edge_ref[0, rows, after]
                s_own = jnp.where(keep_own, mm_nt(k_own, query), -1e30)
                s_edge = jnp.where(keep_edge, mm_nt(k_edge, query), -1e30)
                top = jnp.maximum(
                    jnp.max(s_own, axis=0, keepdims=True), jnp.max(s_edge, axis=0, keepdims=True)
                )
                e_own = jnp.exp((s_own - top) * factor)
                e_edge = jnp.exp((s_edge - top) * factor)
                total = jnp.sum(e_own, axis=0, keepdims=True) + jnp.sum(
                    e_edge, axis=0, keepdims=True
                )
                scale = 1.0 / total
                p_own, p_edge = e_own * scale, e_edge * scale
                g_own, g_edge = mm_nt(v_own, grad), mm_nt(v_edge, grad)
                inner = jnp.sum(p_own * g_own, axis=0, keepdims=True) + jnp.sum(
                    p_edge * g_edge, axis=0, keepdims=True
                )
                d_own = (p_own * (g_own - inner)).astype(bf16)
                d_edge = (p_edge * (g_edge - inner)).astype(bf16)
                dv = mm(p_own.astype(bf16), grad)
                dk = mm(d_own, query)
                dv_own[h] = dv if block == 0 else dv_own[h] + dv
                dk_own[h] = dk if block == 0 else dk_own[h] + dk
                dv_edge.append(mm(p_edge.astype(bf16), grad))
                dk_edge.append(mm(d_edge, query) * factor)
                dq.append((mm_tn(d_own, k_own) + mm_tn(d_edge, k_edge)) * factor)
            at = slice(group * 384, (group + 1) * 384)
            at_v = slice(D + at.start, D + at.stop)
            own_out[0, rows, at] = join_heads(dq).astype(bf16)
            edge_out[0, rows, at] = join_heads(dk_edge).astype(bf16)
            edge_out[0, rows, at_v] = join_heads(dv_edge).astype(bf16)
        at_w = slice(2 * D + at.start, 2 * D + at.stop)
        own_out[0, :, at_v] = (join_heads(dk_own) * factor).astype(bf16)
        own_out[0, :, at_w] = join_heads(dv_own).astype(bf16)


def light_back_kernel(ends_ref, *refs):
    light_back_unit((ends_ref[0] > 0, ends_ref[1] > 0), range(2), *refs)


def light_attention_back(ends, own, edge, grad):
    pieces, tokens = own.shape[:2]
    return pl.pallas_call(
        light_back_kernel,
        out_shape=[
            jax.ShapeDtypeStruct((pieces, tokens, 3 * D), bf16),
            jax.ShapeDtypeStruct((pieces, 2 * RADIUS, 2 * D), bf16),
        ],
        grid_spec=pltpu.PrefetchScalarGridSpec(
            num_scalar_prefetch=1,
            grid=(pieces,),
            in_specs=[
                pl.BlockSpec((1, tokens, 3 * D), lambda p, e: (p, 0, 0)),
                pl.BlockSpec((1, 2 * RADIUS, 2 * D), lambda p, e: (p, 0, 0)),
                pl.BlockSpec((1, tokens, D), lambda p, e: (p, 0, 0)),
            ],
            out_specs=[
                pl.BlockSpec((1, tokens, 3 * D), lambda p, e: (p, 0, 0)),
                pl.BlockSpec((1, 2 * RADIUS, 2 * D), lambda p, e: (p, 0, 0)),
            ],
        ),
        compiler_params=pltpu.CompilerParams(vmem_limit_bytes=32 << 20),
        cost_estimate=pl.CostEstimate(
            flops=pieces * HL * tokens * 384 * 256 * 10,
            bytes_accessed=pieces * (tokens * 7 * D + 2 * RADIUS * 4 * D) * 2,
            transcendentals=pieces * HL * tokens * 384,
        ),
        name="light_attention_back",
    )(ends, own, edge, grad)


def spread_heads(value):
    tall = jnp.concatenate([value] * 4, axis=0)
    row = lax.broadcasted_iota(jnp.int32, tall.shape, 0) // QCAP
    lane = lax.broadcasted_iota(jnp.int32, tall.shape, 1) // HHD
    return jnp.where(row == lane, tall, jnp.zeros_like(tall))


def fold_heads(tall):
    lane = lax.broadcasted_iota(jnp.int32, (QCAP, 4 * HHD), 1) // HHD
    total = tall[:QCAP]
    for r in range(1, 4):
        total = jnp.where(lane == r, tall[r * QCAP : (r + 1) * QCAP], total)
    return total


def heavy_kernel(query_ref, pair_ref, live_ref, out_ref):
    factor = HHD ** (-0.5)
    keep = live_ref[0] > 0
    for group in range(HH // 4):
        lanes = slice(group * 256, (group + 1) * 256)
        query = spread_heads(query_ref[0, :, lanes])
        scores = jnp.where(keep, mm_nt(query, pair_ref[0, :, lanes]), -1e30)
        top = jnp.max(scores, axis=1, keepdims=True)
        raised = jnp.exp((scores - top) * factor)
        total = jnp.sum(raised, axis=1, keepdims=True)
        mix = mm(raised.astype(bf16), pair_ref[0, :, D + lanes.start : D + lanes.stop])
        out_ref[0, :, lanes] = fold_heads(mix * (1.0 / total)).astype(bf16)


def heavy_attention(query, pairs, live):
    pieces, slots = pairs.shape[:2]
    return pl.pallas_call(
        heavy_kernel,
        out_shape=jax.ShapeDtypeStruct((pieces, QCAP, D), bf16),
        grid=(pieces,),
        in_specs=[
            pl.BlockSpec((1, QCAP, D), lambda p: (p, 0, 0)),
            pl.BlockSpec((1, slots, 2 * D), lambda p: (p, 0, 0)),
            pl.BlockSpec((1, 1, slots), lambda p: (p, 0, 0)),
        ],
        out_specs=pl.BlockSpec((1, QCAP, D), lambda p: (p, 0, 0)),
        compiler_params=pltpu.CompilerParams(vmem_limit_bytes=32 << 20),
        cost_estimate=pl.CostEstimate(
            flops=pieces * 3 * 4 * 256 * 256 * slots,
            bytes_accessed=pieces * (slots + QCAP) * 2 * D * 2,
            transcendentals=pieces * HH * QCAP * slots,
        ),
        name="heavy_attention",
    )(query, pairs, live)


def heavy_back_kernel(query_ref, pair_ref, live_ref, grad_ref, query_out, pair_out):
    factor = HHD ** (-0.5)
    slots = pair_ref.shape[1]
    keep = jnp.broadcast_to(live_ref[0], (128, slots)).T[:, :1] > 0
    for group in range(HH // 4):
        lanes = slice(group * 256, (group + 1) * 256)
        after = slice(D + lanes.start, D + lanes.stop)
        query = spread_heads(query_ref[0, :, lanes])
        grad = spread_heads(grad_ref[0, :, lanes])
        keys = pair_ref[0, :, lanes]
        scores = jnp.where(keep, mm_nt(keys, query), -1e30)
        top = jnp.max(scores, axis=0, keepdims=True)
        raised = jnp.exp((scores - top) * factor)
        probs = raised * (1.0 / jnp.sum(raised, axis=0, keepdims=True))
        grad_probs = mm_nt(pair_ref[0, :, after], grad)
        inner = jnp.sum(probs * grad_probs, axis=0, keepdims=True)
        grad_scores = (probs * (grad_probs - inner)).astype(bf16)
        pair_out[0, :, after] = mm(probs.astype(bf16), grad).astype(bf16)
        pair_out[0, :, lanes] = (mm(grad_scores, query) * factor).astype(bf16)
        query_out[0, :, lanes] = (fold_heads(mm_tn(grad_scores, keys)) * factor).astype(bf16)


def heavy_attention_back(query, pairs, live, grad):
    pieces, slots = pairs.shape[:2]
    return pl.pallas_call(
        heavy_back_kernel,
        out_shape=[
            jax.ShapeDtypeStruct((pieces, QCAP, D), bf16),
            jax.ShapeDtypeStruct((pieces, slots, 2 * D), bf16),
        ],
        grid=(pieces,),
        in_specs=[
            pl.BlockSpec((1, QCAP, D), lambda p: (p, 0, 0)),
            pl.BlockSpec((1, slots, 2 * D), lambda p: (p, 0, 0)),
            pl.BlockSpec((1, 1, slots), lambda p: (p, 0, 0)),
            pl.BlockSpec((1, QCAP, D), lambda p: (p, 0, 0)),
        ],
        out_specs=[
            pl.BlockSpec((1, QCAP, D), lambda p: (p, 0, 0)),
            pl.BlockSpec((1, slots, 2 * D), lambda p: (p, 0, 0)),
        ],
        compiler_params=pltpu.CompilerParams(vmem_limit_bytes=32 << 20),
        cost_estimate=pl.CostEstimate(
            flops=pieces * 3 * 10 * 256 * 256 * slots,
            bytes_accessed=pieces * (2 * slots + 2 * QCAP) * 2 * D * 2,
            transcendentals=pieces * HH * QCAP * slots,
        ),
        name="heavy_attention_back",
    )(query, pairs, live, grad)


def reduce_kernel(jobs, arrays, sizes, work, *refs):
    n_x, n_y = sizes
    n_dp = n_x * CORES
    given, made = (3, 2) if work else (0, 0)
    sources, outs = refs[:arrays], refs[arrays + given : 2 * arrays + given]
    operands = refs[arrays : arrays + given] + refs[2 * arrays + given :][:made]
    scratch = list(refs[2 * arrays + given + made :])
    held = []
    for job in jobs:
        names = SCRATCH[job[1]]
        held.append(dict(zip(names, scratch[: len(names)])))
        del scratch[: len(names)]
    dp, seq = lax.axis_index("dp"), lax.axis_index("seq")
    x, c = dp // CORES, dp % CORES
    z, y = seq // n_y, seq % n_y

    def to_dp(by):
        return (lax.rem(dp + by, n_dp), seq)

    def to_core():
        return (x * CORES + (1 - c), seq)

    def to_x(by):
        return (((x + by) % n_x) * CORES + c, seq)

    def to_y(by):
        return (dp, z * n_y + (y + by) % n_y)

    def to_z(by):
        return (dp, ((z + by) % DEPTH) * n_y + y)

    peers = [to_dp(by) for by in range(1, n_dp)]
    peers += [to_y(by) for by in range(1, n_y)]
    peers += [to_z(by) for by in range(1, DEPTH)]
    barrier = pltpu.get_barrier_semaphore()
    for peer in peers:
        pl.semaphore_signal(barrier, inc=1, device_id=peer, device_id_type=MESH)
    pl.semaphore_wait(barrier, len(peers))

    def copy(src, dst, a, stage, k, peer):
        h = held[a]
        return pltpu.make_async_remote_copy(
            src_ref=src,
            dst_ref=dst,
            send_sem=h["ssem"].at[stage],
            recv_sem=h["rsem"].at[stage, k],
            device_id=peer,
            device_id_type=MESH,
        )

    def arrived(name, a, stage, k):
        buffer = held[a][name].at[k]
        copy(buffer, buffer, a, stage, k, to_core()).wait_recv()

    def columns(a, k):
        _, _, start, width, _ = jobs[a]
        return pl.ds(start + k * width, width)

    def source(a):
        return sources[jobs[a][0]]

    def local(a, k):
        h, cols = held[a], columns(a, k)
        whole = source(a)
        part = whole.at[:, c, :, :, :, cols] if "core" in h else whole.at[..., cols]
        return pltpu.make_async_copy(part, h["own"].at[k], h["lsem"].at[k])

    def add_all(target, pairs):
        for at, addend, place in pairs:
            target[at] = target[at] + addend[place]

    def begin(a, k):
        h = held[a]
        local(a, k).start()
        if "core" in h:
            src = source(a).at[:, 1 - c, :, :, :, columns(a, k)]
            copy(src, h["core"].at[k], a, 0, k, to_core()).start()
        else:
            for by in range(1, n_y):
                src = source(a).at[:, :, (y + by) % n_y, :, columns(a, k)]
                copy(src, h["yy"].at[k, by - 1], a, 2, k, to_y(by)).start()

    def first(a, k):
        h, kind = held[a], jobs[a][1]
        local(a, k).wait()
        if "core" not in h:
            return
        own = h["own"]
        arrived("core", a, 0, k)

        @pl.loop(0, n_x * DEPTH)
        def _(i):
            for j in range(n_y):
                at = (k, i // DEPTH, i % DEPTH, j)
                own[at] = own[at] + h["core"][at]

        if kind == "xy":
            for by in range(1, n_x):
                src = own.at[k, (x + by) % n_x]
                copy(src, h["xx"].at[k, by - 1], a, 1, k, to_x(by)).start()
        else:
            for by in range(1, n_y):
                src = own.at[k, :, :, (y + by) % n_y]
                copy(src, h["yy"].at[k, by - 1], a, 2, k, to_y(by)).start()

    def second(a, k):
        h, kind = held[a], jobs[a][1]
        own = h.get("own")
        if kind == "xy":
            arrived("xx", a, 1, k)

            @pl.loop(0, DEPTH)
            def _(i):
                for j in range(n_y):
                    for s in range(n_x - 1):
                        at = (k, x, i, j)
                        own[at] = own[at] + h["xx"][k, s, i, j]

            for by in range(1, n_y):
                src = own.at[k, x, :, (y + by) % n_y]
                copy(src, h["yy"].at[k, by - 1], a, 2, k, to_y(by)).start()
        elif kind == "yx":
            arrived("yy", a, 2, k)

            @pl.loop(0, DEPTH)
            def _(i):
                for j in range(n_x):
                    for s in range(n_y - 1):
                        at = (k, j, i, y)
                        own[at] = own[at] + h["yy"][k, s, j, i]

            for by in range(1, n_x):
                src = own.at[k, (x + by) % n_x, :, y]
                copy(src, h["xx"].at[k, by - 1], a, 1, k, to_x(by)).start()

    def third(a, k):
        h, kind = held[a], jobs[a][1]
        own = h.get("own")
        if kind in ("xy", "yx"):
            name, stage, others = ("yy", 2, n_y - 1) if kind == "xy" else ("xx", 1, n_x - 1)
            arrived(name, a, stage, k)

            @pl.loop(0, DEPTH)
            def _(i):
                for s in range(others):
                    at = (k, x, i, y)
                    own[at] = own[at] + h[name][k, s, i]

            for by in range(1, DEPTH):
                src = own.at[k, x, (z + by) % DEPTH, y]
                copy(src, h["zz"].at[k, by - 1], a, 3, k, to_z(by)).start()
        else:
            arrived("yy", a, 2, k)

            @pl.loop(0, DEPTH)
            def _(i):
                for g in range(own.shape[1]):
                    for s in range(n_y - 1):
                        at = (k, g, i, y)
                        own[at] = own[at] + h["yy"][k, s, g, i]

            for by in range(1, DEPTH):
                src = own.at[k, :, (z + by) % DEPTH, y]
                copy(src, h["zz"].at[k, by - 1], a, 3, k, to_z(by)).start()

    def fourth(a, k):
        h = held[a]
        array, kind, start, width, chunks = jobs[a]
        arrived("zz", a, 3, k)
        if kind != "gates":
            here = h["own"].at[k, 0, z, y] if kind == "seq" else h["own"].at[k, x, z, y]
            total = here[...].astype(f32)
            for s in range(DEPTH - 1):
                block = h["zz"][k, s, 0] if kind == "seq" else h["zz"][k, s]
                total = total + block.astype(f32)
            outs[array][:, start + k * width : start + (k + 1) * width] = total
        else:

            @pl.loop(0, n_dp)
            def _(g):
                total = h["own"][k, g, z, y].astype(f32)
                for s in range(DEPTH - 1):
                    total = total + h["zz"][k, s, g].astype(f32)
                h["sum"][k, g] = total.astype(bf16)

            h["dd"][k, dp] = h["sum"][k, dp]
            for by in range(1, n_dp):
                peer = lax.rem(dp + by, n_dp)
                copy(h["sum"].at[k, peer], h["dd"].at[k, dp], a, 0, k, to_dp(by)).start()

    def last(a, k):
        h = held[a]
        array, kind, start, width, chunks = jobs[a]
        if kind == "gates":
            part = h["dd"].at[k, pl.ds(0, n_dp - 1)]
            copy(part, part, a, 0, k, to_core()).wait_recv()
            half = chunks // 2
            for g in range(n_dp):
                to = (((k // half) * n_dp + g) * half + k % half) * width
                outs[array][:, to : to + width] = h["dd"][k, g].astype(f32)

    lists = {"all": [], "rest": []}
    for a, job in enumerate(jobs):
        group = "all" if "core" in held[a] else "rest"
        lists[group].append([(a, k) for k in range(job[4])])
    events = []
    for group, parts in lists.items():
        order = interleave(parts)
        pace = max(len(interleave(p)) for p in lists.values()) / max(1, len(order))
        for i, (a, k) in enumerate(order):
            for stage, lag in zip((begin, first, second, third, fourth, last), LAGS[group]):
                events.append((i * pace + lag, len(events), stage, (a, k)))
    if work:
        reach = (seq > 0, seq < DEPTH * n_y - 1)

        def unit(p, g):
            light_back_unit(reach, (g,), *[ref.at[pl.ds(p, 1)] for ref in operands])

        for p in range(operands[0].shape[0]):
            for g in range(2):
                events.append(((2 * p + g) * 1.5, len(events), unit, (p, g)))
    for _, _, stage, what in sorted(events, key=lambda e: e[:2]):
        stage(*what)

    for a, job in enumerate(jobs):
        h = held[a]
        for name, stage in (("core", 0), ("xx", 1), ("yy", 2), ("zz", 3)):
            if name in h:
                copy(h[name], h[name], a, stage, 0, to_core()).wait_send()
        if job[1] == "gates":
            part = h["dd"].at[:, pl.ds(0, n_dp - 1)]
            copy(part, part, a, 0, 0, to_core()).wait_send()


def interleave(parts):
    keyed = [((i + 0.5) / len(p), n, v) for n, p in enumerate(parts) for i, v in enumerate(p)]
    return [v for _, _, v in sorted(keyed)]


LAGS = {"all": (-4, 0, 2, 4, 6.5, 9), "rest": (-2, -1, -1, 1, 3.5, 6)}
SCRATCH = {
    "xy": ("own", "core", "xx", "yy", "zz", "lsem", "rsem", "ssem"),
    "yx": ("own", "core", "xx", "yy", "zz", "lsem", "rsem", "ssem"),
    "seq": ("own", "yy", "zz", "lsem", "rsem", "ssem"),
    "gates": ("own", "yy", "zz", "sum", "dd", "lsem", "rsem", "ssem"),
}


def copy_kernel(*refs):
    count = len(refs) // 2
    for i in range(count):
        refs[count + i][...] = refs[i][...]


def copy_all(values):
    count = len(values)
    return pl.pallas_call(
        copy_kernel,
        out_shape=[jax.ShapeDtypeStruct(v.shape, v.dtype) for v in values],
        in_specs=[pl.BlockSpec(memory_space=pltpu.VMEM)] * count,
        out_specs=[pl.BlockSpec(memory_space=pltpu.VMEM)] * count,
        name="copy_outputs",
    )(*values)


def reduce_all(values, jobs, n_x, n_y, collective_id, work=()):
    n_dp = n_x * CORES
    kinds = {array: kind for array, kind, _, _, _ in jobs}
    operands, out_shape, scratch = [], [], []
    for array, value in enumerate(values):
        height, columns = value.shape
        groups = {"seq": (1,), "gates": (n_dp,)}.get(kinds[array], (n_x, CORES))
        chunk = height // (n_y * DEPTH * math.prod(groups))
        operands.append(value.reshape(groups + (DEPTH, n_y, chunk, columns)))
        columns *= n_dp if kinds[array] == "gates" else 1
        out_shape.append(jax.ShapeDtypeStruct((chunk, columns), f32))
    for array, kind, _, width, k in jobs:
        tile = (out_shape[array].shape[0], width)
        lead = {"seq": (1,), "gates": (n_dp,)}.get(kind, (n_x,))
        shapes = [(k,) + lead + (DEPTH, n_y)]
        if kind == "xy":
            shapes += shapes + [(k, n_x - 1, DEPTH, n_y), (k, n_y - 1, DEPTH), (k, DEPTH - 1)]
        elif kind == "yx":
            shapes += shapes + [(k, n_x - 1, DEPTH), (k, n_y - 1, n_x, DEPTH), (k, DEPTH - 1)]
        else:
            shapes += [(k, n_y - 1) + lead + (DEPTH,), (k, DEPTH - 1) + lead]
        if kind == "gates":
            shapes += [(k, n_dp)] * 2
        scratch += [pltpu.VMEM(shape + tile, bf16) for shape in shapes]
        scratch += [
            pltpu.SemaphoreType.DMA((k,)),
            pltpu.SemaphoreType.DMA((4, k)),
            pltpu.SemaphoreType.DMA((4,)),
        ]
    total = sum(v.size for v in values)
    out_shape += [jax.ShapeDtypeStruct(v.shape, bf16) for v in work[:2]]
    here = pl.BlockSpec(memory_space=pltpu.VMEM)
    return pl.pallas_call(
        functools.partial(reduce_kernel, tuple(jobs), len(values), (n_x, n_y), bool(work)),
        out_shape=out_shape,
        in_specs=[pl.BlockSpec(memory_space=pl.ANY)] * len(values) + [here] * len(work),
        out_specs=[here] * len(out_shape),
        scratch_shapes=scratch,
        compiler_params=pltpu.CompilerParams(
            collective_id=collective_id, has_side_effects=True, vmem_limit_bytes=60 << 20
        ),
        cost_estimate=pl.CostEstimate(
            flops=2 * total, bytes_accessed=32 * total, transcendentals=0
        ),
        name="reduce_gradients",
    )(*operands, *work)


def per_device(
    layer_input,
    cotangent,
    first_gain,
    light_inputs,
    light_output,
    heavy_queries,
    heavy_keyvalue,
    heavy_output,
    second_gain,
    router,
    light_gates,
    light_down,
    heavy_gates,
    heavy_down,
    query_index,
    query_count,
    key_index,
    key_count,
    feed_slot,
):
    pieces, tokens = layer_input.shape[:2]
    rows = pieces * tokens
    n_dp, n_seq = lax.axis_size("dp"), lax.axis_size("seq")
    n_x, n_y = n_dp // CORES, n_seq // DEPTH
    seq_rank = lax.axis_index("seq")
    core = Ring("dp", 1, CORES)
    ring_x = Ring("dp", CORES, n_x)
    ring_y = Ring("seq", 1, n_y)
    ring_z = Ring("seq", n_y, DEPTH)
    capacity = max(2, 3 * rows // (16 * n_seq))
    slots = n_seq * capacity
    light_factor = LHD ** (-0.5)
    heavy_factor = HHD ** (-0.5)

    def reduce_grad(value, first, second):
        height, width = value.shape
        chunk = height // (n_dp * n_seq)
        parts = value.reshape(n_x, CORES, DEPTH, n_y, chunk, width)
        parts = core.scatter_sum(parts, 1).astype(bf16)
        dims = ["x", "z", "y"]
        rings = {"x": ring_x, "y": ring_y, "z": ring_z}
        order = [first, second, [d for d in dims if d not in (first, second)][0]]
        for i, d in enumerate(order):
            at = dims.index(d)
            parts = rings[d].scatter_sum(parts, at)
            if i < 2:
                parts = parts.astype(bf16)
            dims.remove(d)
        return parts

    def reduce_split(value):
        half = value.shape[1] // 2
        return jnp.concatenate(
            [
                reduce_grad(value[:, :half], "x", "y"),
                reduce_grad(value[:, half:], "y", "x"),
            ],
            axis=1,
        )

    def reduce_seq(value):
        parts = value.reshape(1, DEPTH, n_y, value.shape[0] // n_seq, value.shape[1])
        parts = ring_z.scatter_sum(parts, 1).astype(bf16)
        return ring_y.scatter_sum(parts, 1)[0]

    def reduce_vectors(value):
        count, width = value.shape
        chunk = width // (n_dp * n_seq)
        parts = value.reshape(count, n_x, CORES, DEPTH, n_y, chunk)
        parts = core.scatter_sum(parts, 2)
        parts = ring_x.scatter_sum(parts, 1)
        parts = ring_z.scatter_sum(parts, 1)
        return ring_y.scatter_sum(parts, 1)

    ends = n_seq - 1
    left_rows = lax.ppermute(
        layer_input[:, tokens - RADIUS :], "seq", [(i, i + 1) for i in range(ends)]
    )
    right_rows = lax.ppermute(layer_input[:, :RADIUS], "seq", [(i + 1, i) for i in range(ends)])
    position = jnp.arange(tokens, dtype=jnp.int32)
    key_pick = (key_index[:, :, None] == position[None, None, :]).astype(bf16)
    query_live = jnp.arange(QCAP, dtype=jnp.int32)[None, :] < query_count
    query_pick = (query_index[:, :, None] == position[None, None, :]).astype(bf16)
    live_pick = query_pick * query_live[:, :, None].astype(bf16)
    key_raw = jnp.einsum("pkt,ptd->pkd", key_pick, layer_input, preferred_element_type=f32).astype(
        bf16
    )
    key_all = lax.all_gather(key_raw, "seq", axis=1, tiled=True)

    gain_first = first_gain.astype(f32)
    inputs = layer_input.astype(f32)
    unit_first, scale_first = norm_parts(inputs)
    normed_first = (unit_first * gain_first).astype(bf16)
    normed_flat = normed_first.reshape(rows, D)
    own_proj = mm(normed_flat, light_inputs).astype(bf16).reshape(pieces, tokens, 3 * D)
    edge_rows = jnp.concatenate([left_rows, right_rows], axis=1)
    normed_edge = (norm_parts(edge_rows.astype(f32))[0] * gain_first).astype(bf16)
    edge_flat = normed_edge.reshape(pieces * 2 * RADIUS, D)
    edge_proj = mm(edge_flat, light_inputs[:, D:]).astype(bf16)
    edge_proj = edge_proj.reshape(pieces, 2 * RADIUS, 2 * D)

    reach = jnp.stack([seq_rank > 0, seq_rank < n_seq - 1]).astype(jnp.int32)
    light_att = light_attention(reach, own_proj, edge_proj).reshape(rows, D)

    key_slots = n_seq * KCAP
    key_rows_all = key_all.reshape(pieces * key_slots, D)
    normed_keys = (norm_parts(key_rows_all.astype(f32))[0] * gain_first).astype(bf16)
    heavy_pairs = mm(normed_keys, heavy_keyvalue).astype(bf16).reshape(pieces, key_slots, 2 * D)
    key_live = jnp.arange(KCAP, dtype=jnp.int32)[None, None, :] < key_count[:, :, None]
    key_live = key_live.reshape(pieces, 1, key_slots).astype(f32)
    query_rows = (
        jnp.einsum("pqt,ptd->pqd", query_pick, normed_first, preferred_element_type=f32)
        .astype(bf16)
        .reshape(pieces * QCAP, D)
    )
    heavy_query = mm(query_rows, heavy_queries).astype(bf16).reshape(pieces, QCAP, D)
    heavy_att = heavy_attention(heavy_query, heavy_pairs, key_live)
    heavy_spread = (
        jnp.einsum("pqt,pqd->ptd", live_pick, heavy_att, preferred_element_type=f32)
        .astype(bf16)
        .reshape(rows, D)
    )

    middle = (
        inputs.reshape(rows, D) + mm(light_att, light_output) + mm(heavy_spread, heavy_output)
    )
    gain_second = second_gain.astype(f32)
    unit_second, scale_second = norm_parts(middle)
    normed_second = (unit_second * gain_second).astype(bf16)

    slot_of = feed_slot.reshape(1, rows)
    pick = (jnp.arange(slots, dtype=jnp.int32)[:, None] == slot_of).astype(bf16)
    routed = feed_slot.reshape(rows, 1) >= 0
    cot = cotangent.reshape(rows, D)
    gating = jax.nn.sigmoid(
        jnp.sum(normed_second.astype(f32) * router.astype(f32), axis=-1, keepdims=True)
    )
    grad_token = (gating * cot.astype(f32)).astype(bf16)
    feed_in = mm(pick, normed_second).astype(bf16)
    grad_in = mm(pick, grad_token).astype(bf16)

    hidden = light_gates.shape[1] // 2
    light_gate = mm(normed_second, light_gates[:, :hidden])
    light_up = mm(normed_second, light_gates[:, hidden:])
    light_act, light_pull = jax.vjp(glu_rows, light_gate, light_up)
    light_act = light_act.astype(bf16)
    light_feed = mm(light_act, light_down)
    grad_light_gate, grad_light_up = light_pull(mm_nt(cot, light_down))
    grad_light_pre = jnp.concatenate([grad_light_gate.astype(bf16), grad_light_up.astype(bf16)], 1)

    dp_rank = lax.axis_index("dp")
    share = heavy_gates.shape[1] // (2 * n_dp)
    gates_here = [
        lax.dynamic_slice_in_dim(heavy_gates, (part * n_dp + dp_rank) * share, share, 1)
        for part in range(2)
    ]
    down_here = lax.dynamic_slice_in_dim(heavy_down, dp_rank * share, share, 0)
    feed_all = core.gather(ring_x.gather(jnp.stack([feed_in, grad_in]), 1), 1)
    feed_all, light_act, grad_light_pre = lax.optimization_barrier(
        (feed_all, light_act, grad_light_pre)
    )
    feed_rows, grad_rows = feed_all[0], feed_all[1]
    heavy_gate = mm(feed_rows, gates_here[0])
    heavy_up = mm(feed_rows, gates_here[1])
    heavy_act, heavy_pull = jax.vjp(glu_rows, heavy_gate, heavy_up)
    heavy_act = heavy_act.astype(bf16)
    heavy_part = mm(heavy_act, down_here).astype(bf16)
    grad_heavy_gate, grad_heavy_up = heavy_pull(mm_nt(grad_rows, down_here))
    grad_heavy_pre = [grad_heavy_gate.astype(bf16), grad_heavy_up.astype(bf16)]
    grad_part = (
        mm_nt(grad_heavy_pre[0], gates_here[0]) + mm_nt(grad_heavy_pre[1], gates_here[1])
    ).astype(bf16)
    back = core.return_sum(jnp.stack([heavy_part, grad_part]), 1).astype(bf16)
    back, light_act_late, grad_light_late = lax.optimization_barrier(
        (back, light_act, grad_light_pre)
    )
    back = ring_x.return_sum(back, 1).astype(bf16)
    heavy_result, grad_feed_in = back[0], back[1]
    heavy_down_grad = mm_tn(heavy_act, grad_rows).astype(bf16)
    heavy_gates_grad = jnp.concatenate(
        [mm_tn(feed_rows, grad_heavy_pre[0]), mm_tn(feed_rows, grad_heavy_pre[1])], axis=1
    ).astype(bf16)
    light_down_grad = mm_tn(light_act_late, cot).astype(bf16)
    light_gates_grad = mm_tn(normed_second, grad_light_late).astype(bf16)

    token_result = mm_tn(pick, heavy_result)
    output = (middle + light_feed + gating * token_result).astype(bf16).reshape(layer_input.shape)
    grad_gating = jnp.sum(cot.astype(f32) * token_result, axis=-1, keepdims=True)
    grad_logit = grad_gating * gating * (1.0 - gating)
    grad_second = (
        mm_nt(grad_light_pre, light_gates)
        + mm_tn(pick, grad_feed_in)
        + grad_logit * router.astype(f32)
    )
    router_grad = jnp.sum(grad_logit * normed_second.astype(f32), axis=0)
    second_gain_grad = jnp.sum(grad_second * unit_second, axis=0)
    grad_middle = cot.astype(f32) + norm_pull(grad_second, middle, scale_second, gain_second)
    grad_mid_low = grad_middle.astype(bf16)

    light_output_grad = mm_tn(light_att, grad_mid_low).astype(bf16)
    grad_light_att = mm_nt(grad_mid_low, light_output).astype(bf16)
    grad_query_rows = (
        jnp.einsum(
            "pqt,ptd->pqd",
            live_pick,
            grad_mid_low.reshape(pieces, tokens, D),
            preferred_element_type=f32,
        )
        .astype(bf16)
        .reshape(pieces * QCAP, D)
    )
    heavy_output_grad = mm_tn(heavy_att.reshape(pieces * QCAP, D), grad_query_rows).astype(bf16)
    grad_heavy_att = mm_nt(grad_query_rows, heavy_output).astype(bf16)

    grad_hq_low, grad_hkv_low = heavy_attention_back(
        heavy_query,
        heavy_pairs,
        key_live,
        grad_heavy_att.reshape(pieces, QCAP, D),
    )
    grad_hq_low = grad_hq_low.reshape(pieces * QCAP, D)
    grad_hkv_low = grad_hkv_low.reshape(pieces * key_slots, 2 * D)
    grad_key_rows = mm_nt(grad_hkv_low, heavy_keyvalue).astype(bf16)
    heavy_keyvalue_grad = mm_tn(normed_keys, grad_hkv_low).astype(bf16)
    heavy_queries_grad = mm_tn(query_rows, grad_hq_low).astype(bf16)

    grad_light_att, grad_key_rows = lax.optimization_barrier((grad_light_att, grad_key_rows))
    grad_key_own = lax.psum_scatter(
        grad_key_rows.reshape(pieces, key_slots, D), "seq", scatter_dimension=1, tiled=True
    )
    grad_light_att = grad_light_att.reshape(pieces, tokens, D)
    each = D // (n_dp * n_seq)
    early = [
        light_gates_grad,
        light_down_grad,
        light_output_grad,
        heavy_output_grad,
        heavy_gates_grad,
        heavy_down_grad,
    ]
    if each % 8 == 0:
        jobs = [
            (0, "xy", 0, 512, light_gates_grad.shape[1] // 512),
            (1, "xy", 0, 384, D // 384),
            (2, "xy", 0, 384, D // 384),
            (3, "xy", 0, 384, D // 384),
            (4, "gates", 0, 256, heavy_gates_grad.shape[1] // 256),
            (5, "seq", 0, 128, D // 128),
        ]
        *early, grad_own, grad_edge = reduce_all(
            early, jobs, n_x, n_y, 0, (own_proj, edge_proj, grad_light_att)
        )
    else:
        grad_own, grad_edge = light_attention_back(reach, own_proj, edge_proj, grad_light_att)
        parts = heavy_gates_grad.reshape(n_dp, DEPTH, n_y, each, -1)
        parts = ring_z.scatter_sum(parts, 1).astype(bf16)
        parts = ring_y.scatter_sum(parts, 1).astype(bf16)
        parts = lax.all_to_all(parts, "dp", split_axis=0, concat_axis=0, tiled=True)
        parts = parts.reshape(n_dp, each, 2, -1).transpose(1, 2, 0, 3)
        early = [reduce_split(v) for v in early[:4]]
        early += [parts.reshape(each, -1).astype(f32), reduce_seq(heavy_down_grad)]
    grad_own = grad_own.reshape(rows, 3 * D)
    grad_edge = grad_edge.reshape(pieces * 2 * RADIUS, 2 * D)
    grad_edge_rows = mm_nt(grad_edge, light_inputs[:, D:]).astype(bf16)
    grad_edge_rows = grad_edge_rows.reshape(pieces, 2 * RADIUS, D)
    from_right = lax.ppermute(
        grad_edge_rows[:, :RADIUS], "seq", [(i + 1, i) for i in range(ends)]
    )
    from_left = lax.ppermute(
        grad_edge_rows[:, RADIUS:], "seq", [(i, i + 1) for i in range(ends)]
    )
    light_inputs_grad = jnp.concatenate(
        [
            mm_tn(normed_flat, grad_own[:, :D]),
            mm_tn(normed_flat, grad_own[:, D:]) + mm_tn(edge_flat, grad_edge),
        ],
        axis=1,
    ).astype(bf16)

    grad_hq_rows = mm_nt(grad_hq_low, heavy_queries).astype(bf16).reshape(pieces, QCAP, D)
    grad_first = mm_nt(grad_own, light_inputs).reshape(pieces, tokens, D)
    grad_first = (
        grad_first
        + jnp.einsum("pqt,pqd->ptd", query_pick, grad_hq_rows, preferred_element_type=f32)
        + jnp.einsum("pkt,pkd->ptd", key_pick, grad_key_own.astype(bf16), preferred_element_type=f32)
        + jnp.concatenate([from_left, from_right], axis=1).astype(f32)
    )
    first_gain_grad = jnp.sum(grad_first * unit_first, axis=(0, 1))
    input_grad = grad_middle.reshape(pieces, tokens, D) + norm_pull(
        grad_first, inputs, scale_first, gain_first
    )
    vectors = jnp.stack([first_gain_grad, second_gain_grad, router_grad])
    devices = n_dp * n_seq
    late = [light_inputs_grad, heavy_queries_grad, heavy_keyvalue_grad]
    if each % 8 == 0:
        lines = vectors.reshape(3, devices, each).transpose(1, 0, 2)
        lines = jnp.pad(lines, ((0, 0), (0, 5), (0, 256 - each))).reshape(devices * 8, 256)
        jobs = []
        for array, value in enumerate(late):
            half = value.shape[1] // 2
            jobs += [(array, "xy", 0, 384, half // 384), (array, "yx", half, 384, half // 384)]
        jobs.append((len(late), "xy", 0, 256, 1))
        sums = reduce_all(late + [lines.astype(bf16)], jobs, n_x, n_y, 1)
        *sums, lines = copy_all([*early, *sums])
        early, late = sums[: len(early)], sums[len(early) :]
        vectors = lines[:3, :each]
    else:
        late = [reduce_split(v) for v in late]
        vectors = reduce_vectors(vectors)
    light_gates_grad, light_down_grad, light_output_grad, heavy_output_grad = early[:4]
    return (
        output,
        input_grad,
        vectors[0],
        late[0],
        light_output_grad,
        late[1],
        late[2],
        heavy_output_grad,
        vectors[1],
        vectors[2],
        light_gates_grad,
        light_down_grad,
        early[4],
        early[5],
    )


def solution(mesh):
    rows = P(("dp", "seq"), None)
    line = P(("dp", "seq"))
    tokens = P("dp", "seq", None)
    slots = P("dp", "seq")
    return jax.shard_map(
        per_device,
        mesh=mesh,
        in_specs=(tokens, tokens) + (P(),) * 12 + (slots, slots, slots, P("dp", None), slots),
        out_specs=(tokens, tokens, line) + (rows,) * 5 + (line, line) + (rows,) * 4,
        check_vma=False,
    )
```

```python
import functools
import math
import jax
import jax.numpy as jnp
from jax import lax
from jax.experimental import pallas as pl
from jax.experimental.pallas import tpu as pltpu
from jax.sharding import PartitionSpec as P
D = 768
HL = 8
LHD = 96
HH = 12
HHD = 64
RADIUS = 128
QCAP = 64
KCAP = 64
CORES = 2
DEPTH = 4
MESH = pl.DeviceIdType.MESH
epsilon = 1e-06
bf16 = jnp.bfloat16
f32 = jnp.float32


def dot(left, right, over):
    return lax.dot_general(left, right, (over, ((), ())), preferred_element_type=f32)


def mm(left, right):
    return dot(left, right, ((1,), (0,)))


def mm_nt(left, right):
    return dot(left, right, ((1,), (1,)))


def mm_tn(left, right):
    return dot(left, right, ((0,), (0,)))


class Ring:
    def __init__(self, axis, stride, count):
        self.axis, self.stride, self.count = axis, stride, count
        self.place = (lax.axis_index(axis) // stride) % count

    def shift(self, value, by):
        total = lax.axis_size(self.axis)
        pairs = []
        for i in range(total):
            c = (i // self.stride) % self.count
            pairs.append((i, i + ((c + by) % self.count - c) * self.stride))
        return lax.ppermute(value, self.axis, pairs)

    def scatter_sum(self, value, dim):
        own = lax.dynamic_index_in_dim(value, self.place, dim, keepdims=False)
        total = own.astype(f32)
        for by in range(1, self.count):
            send = lax.dynamic_index_in_dim(
                value, (self.place + by) % self.count, dim, keepdims=False
            )
            total = total + self.shift(send, by).astype(f32)
        return total

    def gather(self, value, dim):
        parts = [value] + [self.shift(value, by) for by in range(1, self.count)]
        return jnp.concatenate(parts, axis=dim)

    def return_sum(self, joined, dim):
        parts = jnp.split(joined, self.count, axis=dim)
        total = parts[0].astype(f32)
        for by in range(1, self.count):
            total = total + self.shift(parts[by], self.count - by).astype(f32)
        return total


def norm_parts(values):
    scale = lax.rsqrt(jnp.mean(values * values, axis=-1, keepdims=True) + epsilon)
    return values * scale, scale


def norm_pull(grad, values, scale, gain):
    weighted = grad * gain
    inner = jnp.mean(weighted * values, axis=-1, keepdims=True)
    return scale * weighted - values * (scale * scale * scale) * inner


def head_windows():
    windows = []
    for h in range(4):
        first, end = h * LHD, (h + 1) * LHD
        windows.append((first // 128 * 128, -(-end // 128) * 128, first, end))
    return windows


def lane_mask(shape, first, end):
    lane = lax.broadcasted_iota(jnp.int32, shape, 1)
    return (lane >= first) & (lane < end)


def join_heads(parts):
    lane = lax.broadcasted_iota(jnp.int32, (parts[0].shape[0], 128), 1)
    return jnp.concatenate(
        [
            jnp.where(lane < 96, parts[0], parts[1][:, :128]),
            jnp.where(lane < 64, parts[1][:, 128:], parts[2][:, :128]),
            jnp.where(lane < 32, parts[2][:, 128:], parts[3]),
        ],
        axis=1,
    )


def light_kernel(ends_ref, own_ref, edge_ref, out_ref):
    half = RADIUS
    factor = LHD ** (-0.5)
    for block in range(2):
        rows = slice(block * half, (block + 1) * half)
        row = lax.broadcasted_iota(jnp.int32, (half, 2 * half), 0)
        col = lax.broadcasted_iota(jnp.int32, (half, 2 * half), 1)
        keep_own = col <= row + half if block == 0 else col >= row
        row, col = row[:, :half], col[:, :half]
        keep_edge = (col >= row if block == 0 else col <= row) & (ends_ref[block] > 0)
        for group in range(2):
            mixed = []
            for a, b, first, end in head_windows():
                lanes = slice(group * 384 + a, group * 384 + b)
                keys = slice(D + lanes.start, D + lanes.stop)
                values = slice(2 * D + lanes.start, 2 * D + lanes.stop)
                query = own_ref[0, rows, lanes]
                query = jnp.where(
                    lane_mask(query.shape, first - a, end - a), query, jnp.zeros_like(query)
                )
                s_own = jnp.where(keep_own, mm_nt(query, own_ref[0, :, keys]), -1e30)
                s_edge = jnp.where(keep_edge, mm_nt(query, edge_ref[0, rows, lanes]), -1e30)
                top = jnp.maximum(
                    jnp.max(s_own, axis=1, keepdims=True), jnp.max(s_edge, axis=1, keepdims=True)
                )
                e_own = jnp.exp((s_own - top) * factor)
                e_edge = jnp.exp((s_edge - top) * factor)
                total = jnp.sum(e_own, axis=1, keepdims=True) + jnp.sum(
                    e_edge, axis=1, keepdims=True
                )
                mix = mm(e_own.astype(bf16), own_ref[0, :, values])
                mix += mm(
                    e_edge.astype(bf16), edge_ref[0, rows, slice(D + lanes.start, D + lanes.stop)]
                )
                mixed.append(mix * (1.0 / total))
            out_ref[0, rows, group * 384 : (group + 1) * 384] = join_heads(mixed).astype(bf16)


def light_attention(ends, own, edge):
    pieces, tokens = own.shape[:2]
    return pl.pallas_call(
        light_kernel,
        out_shape=jax.ShapeDtypeStruct((pieces, tokens, D), bf16),
        grid_spec=pltpu.PrefetchScalarGridSpec(
            num_scalar_prefetch=1,
            grid=(pieces,),
            in_specs=[
                pl.BlockSpec((1, tokens, 3 * D), lambda p, e: (p, 0, 0)),
                pl.BlockSpec((1, 2 * RADIUS, 2 * D), lambda p, e: (p, 0, 0)),
            ],
            out_specs=pl.BlockSpec((1, tokens, D), lambda p, e: (p, 0, 0)),
        ),
        compiler_params=pltpu.CompilerParams(vmem_limit_bytes=32 << 20),
        cost_estimate=pl.CostEstimate(
            flops=pieces * HL * tokens * 384 * 256 * 4,
            bytes_accessed=pieces * (tokens * 4 * D + 2 * RADIUS * 2 * D) * 2,
            transcendentals=pieces * HL * tokens * 384,
        ),
        name="light_attention",
    )(ends, own, edge)


def light_back_unit(reach, groups, own_ref, edge_ref, grad_ref, own_out, edge_out):
    half = RADIUS
    factor = LHD ** (-0.5)
    for group in groups:
        dk_own, dv_own = [None] * 4, [None] * 4
        for block in range(2):
            rows = slice(block * half, (block + 1) * half)
            key = lax.broadcasted_iota(jnp.int32, (2 * half, half), 0)
            que = lax.broadcasted_iota(jnp.int32, (2 * half, half), 1)
            keep_own = key <= que + half if block == 0 else key >= que
            key, que = key[:half], que[:half]
            keep_edge = (key >= que if block == 0 else key <= que) & reach[block]
            dq, dk_edge, dv_edge = [], [], []
            for h, (a, b, first, end) in enumerate(head_windows()):
                lanes = slice(group * 384 + a, group * 384 + b)
                after = slice(D + lanes.start, D + lanes.stop)
                last = slice(2 * D + lanes.start, 2 * D + lanes.stop)
                mask = lane_mask((half, b - a), first - a, end - a)
                query = own_ref[0, rows, lanes]
                query = jnp.where(mask, query, jnp.zeros_like(query))
                grad = grad_ref[0, rows, lanes]
                grad = jnp.where(mask, grad, jnp.zeros_like(grad))
                k_own, k_edge = own_ref[0, :, after], edge_ref[0, rows, lanes]
                v_own, v_edge = own_ref[0, :, last], edge_ref[0, rows, after]
                s_own = jnp.where(keep_own, mm_nt(k_own, query), -1e30)
                s_edge = jnp.where(keep_edge, mm_nt(k_edge, query), -1e30)
                top = jnp.maximum(
                    jnp.max(s_own, axis=0, keepdims=True), jnp.max(s_edge, axis=0, keepdims=True)
                )
                e_own = jnp.exp((s_own - top) * factor)
                e_edge = jnp.exp((s_edge - top) * factor)
                total = jnp.sum(e_own, axis=0, keepdims=True) + jnp.sum(
                    e_edge, axis=0, keepdims=True
                )
                scale = 1.0 / total
                p_own, p_edge = e_own * scale, e_edge * scale
                g_own, g_edge = mm_nt(v_own, grad), mm_nt(v_edge, grad)
                inner = jnp.sum(p_own * g_own, axis=0, keepdims=True) + jnp.sum(
                    p_edge * g_edge, axis=0, keepdims=True
                )
                d_own = (p_own * (g_own - inner)).astype(bf16)
                d_edge = (p_edge * (g_edge - inner)).astype(bf16)
                dv = mm(p_own.astype(bf16), grad)
                dk = mm(d_own, query)
                dv_own[h] = dv if block == 0 else dv_own[h] + dv
                dk_own[h] = dk if block == 0 else dk_own[h] + dk
                dv_edge.append(mm(p_edge.astype(bf16), grad))
                dk_edge.append(mm(d_edge, query) * factor)
                dq.append((mm_tn(d_own, k_own) + mm_tn(d_edge, k_edge)) * factor)
            at = slice(group * 384, (group + 1) * 384)
            at_v = slice(D + at.start, D + at.stop)
            own_out[0, rows, at] = join_heads(dq).astype(bf16)
            edge_out[0, rows, at] = join_heads(dk_edge).astype(bf16)
            edge_out[0, rows, at_v] = join_heads(dv_edge).astype(bf16)
        at_w = slice(2 * D + at.start, 2 * D + at.stop)
        own_out[0, :, at_v] = (join_heads(dk_own) * factor).astype(bf16)
        own_out[0, :, at_w] = join_heads(dv_own).astype(bf16)


def light_back_kernel(ends_ref, *refs):
    light_back_unit((ends_ref[0] > 0, ends_ref[1] > 0), range(2), *refs)


def light_attention_back(ends, own, edge, grad):
    pieces, tokens = own.shape[:2]
    return pl.pallas_call(
        light_back_kernel,
        out_shape=[
            jax.ShapeDtypeStruct((pieces, tokens, 3 * D), bf16),
            jax.ShapeDtypeStruct((pieces, 2 * RADIUS, 2 * D), bf16),
        ],
        grid_spec=pltpu.PrefetchScalarGridSpec(
            num_scalar_prefetch=1,
            grid=(pieces,),
            in_specs=[
                pl.BlockSpec((1, tokens, 3 * D), lambda p, e: (p, 0, 0)),
                pl.BlockSpec((1, 2 * RADIUS, 2 * D), lambda p, e: (p, 0, 0)),
                pl.BlockSpec((1, tokens, D), lambda p, e: (p, 0, 0)),
            ],
            out_specs=[
                pl.BlockSpec((1, tokens, 3 * D), lambda p, e: (p, 0, 0)),
                pl.BlockSpec((1, 2 * RADIUS, 2 * D), lambda p, e: (p, 0, 0)),
            ],
        ),
        compiler_params=pltpu.CompilerParams(vmem_limit_bytes=32 << 20),
        cost_estimate=pl.CostEstimate(
            flops=pieces * HL * tokens * 384 * 256 * 10,
            bytes_accessed=pieces * (tokens * 7 * D + 2 * RADIUS * 4 * D) * 2,
            transcendentals=pieces * HL * tokens * 384,
        ),
        name="light_attention_back",
    )(ends, own, edge, grad)


def spread_heads(value):
    tall = jnp.concatenate([value] * 4, axis=0)
    row = lax.broadcasted_iota(jnp.int32, tall.shape, 0) // QCAP
    lane = lax.broadcasted_iota(jnp.int32, tall.shape, 1) // HHD
    return jnp.where(row == lane, tall, jnp.zeros_like(tall))


def fold_heads(tall):
    lane = lax.broadcasted_iota(jnp.int32, (QCAP, 4 * HHD), 1) // HHD
    total = tall[:QCAP]
    for r in range(1, 4):
        total = jnp.where(lane == r, tall[r * QCAP : (r + 1) * QCAP], total)
    return total


def heavy_kernel(query_ref, pair_ref, live_ref, out_ref):
    factor = HHD ** (-0.5)
    keep = live_ref[0] > 0
    for group in range(HH // 4):
        lanes = slice(group * 256, (group + 1) * 256)
        query = spread_heads(query_ref[0, :, lanes])
        scores = jnp.where(keep, mm_nt(query, pair_ref[0, :, lanes]), -1e30)
        top = jnp.max(scores, axis=1, keepdims=True)
        raised = jnp.exp((scores - top) * factor)
        total = jnp.sum(raised, axis=1, keepdims=True)
        mix = mm(raised.astype(bf16), pair_ref[0, :, D + lanes.start : D + lanes.stop])
        out_ref[0, :, lanes] = fold_heads(mix * (1.0 / total)).astype(bf16)


def heavy_attention(query, pairs, live):
    pieces, slots = pairs.shape[:2]
    return pl.pallas_call(
        heavy_kernel,
        out_shape=jax.ShapeDtypeStruct((pieces, QCAP, D), bf16),
        grid=(pieces,),
        in_specs=[
            pl.BlockSpec((1, QCAP, D), lambda p: (p, 0, 0)),
            pl.BlockSpec((1, slots, 2 * D), lambda p: (p, 0, 0)),
            pl.BlockSpec((1, 1, slots), lambda p: (p, 0, 0)),
        ],
        out_specs=pl.BlockSpec((1, QCAP, D), lambda p: (p, 0, 0)),
        compiler_params=pltpu.CompilerParams(vmem_limit_bytes=32 << 20),
        cost_estimate=pl.CostEstimate(
            flops=pieces * 3 * 4 * 256 * 256 * slots,
            bytes_accessed=pieces * (slots + QCAP) * 2 * D * 2,
            transcendentals=pieces * HH * QCAP * slots,
        ),
        name="heavy_attention",
    )(query, pairs, live)


def heavy_back_kernel(query_ref, pair_ref, live_ref, grad_ref, query_out, pair_out):
    factor = HHD ** (-0.5)
    slots = pair_ref.shape[1]
    keep = jnp.broadcast_to(live_ref[0], (128, slots)).T[:, :1] > 0
    for group in range(HH // 4):
        lanes = slice(group * 256, (group + 1) * 256)
        after = slice(D + lanes.start, D + lanes.stop)
        query = spread_heads(query_ref[0, :, lanes])
        grad = spread_heads(grad_ref[0, :, lanes])
        keys = pair_ref[0, :, lanes]
        scores = jnp.where(keep, mm_nt(keys, query), -1e30)
        top = jnp.max(scores, axis=0, keepdims=True)
        raised = jnp.exp((scores - top) * factor)
        probs = raised * (1.0 / jnp.sum(raised, axis=0, keepdims=True))
        grad_probs = mm_nt(pair_ref[0, :, after], grad)
        inner = jnp.sum(probs * grad_probs, axis=0, keepdims=True)
        grad_scores = (probs * (grad_probs - inner)).astype(bf16)
        pair_out[0, :, after] = mm(probs.astype(bf16), grad).astype(bf16)
        pair_out[0, :, lanes] = (mm(grad_scores, query) * factor).astype(bf16)
        query_out[0, :, lanes] = (fold_heads(mm_tn(grad_scores, keys)) * factor).astype(bf16)


def heavy_attention_back(query, pairs, live, grad):
    pieces, slots = pairs.shape[:2]
    return pl.pallas_call(
        heavy_back_kernel,
        out_shape=[
            jax.ShapeDtypeStruct((pieces, QCAP, D), bf16),
            jax.ShapeDtypeStruct((pieces, slots, 2 * D), bf16),
        ],
        grid=(pieces,),
        in_specs=[
            pl.BlockSpec((1, QCAP, D), lambda p: (p, 0, 0)),
            pl.BlockSpec((1, slots, 2 * D), lambda p: (p, 0, 0)),
            pl.BlockSpec((1, 1, slots), lambda p: (p, 0, 0)),
            pl.BlockSpec((1, QCAP, D), lambda p: (p, 0, 0)),
        ],
        out_specs=[
            pl.BlockSpec((1, QCAP, D), lambda p: (p, 0, 0)),
            pl.BlockSpec((1, slots, 2 * D), lambda p: (p, 0, 0)),
        ],
        compiler_params=pltpu.CompilerParams(vmem_limit_bytes=32 << 20),
        cost_estimate=pl.CostEstimate(
            flops=pieces * 3 * 10 * 256 * 256 * slots,
            bytes_accessed=pieces * (2 * slots + 2 * QCAP) * 2 * D * 2,
            transcendentals=pieces * HH * QCAP * slots,
        ),
        name="heavy_attention_back",
    )(query, pairs, live, grad)


def glu_and_pull(gate, up, grad):
    slope = 0.7978845608028654
    square = gate * gate
    curve = jnp.tanh(gate * (slope + (slope * 0.044715) * square))
    half = 0.5 + 0.5 * curve
    gelu = gate * half
    bend = (0.5 * gate) * (1.0 - curve * curve) * (slope + (3 * slope * 0.044715) * square)
    return gelu * up, grad * up * (half + bend), grad * gelu


def feed_kernel(
    n_y,
    normed,
    cot,
    own_rows,
    gates,
    down,
    gates_heavy,
    down_heavy,
    act_out,
    pre_out,
    feed_out,
    grad_out,
    back_out,
    rows_out,
    heavy_act_out,
    heavy_pre_out,
    wide,
    tall,
    rows,
    part,
    from_core,
    to_y,
    from_y,
    weight_sem,
    rows_rsem,
    rows_ssem,
    core_rsem,
    core_ssem,
    y_rsem,
    y_ssem,
):
    dp, seq = lax.axis_index("dp"), lax.axis_index("seq")
    c, y = dp % CORES, seq % n_y
    me = c * n_y + y
    to_core, to_beside = (dp + 1 - 2 * c, seq), (dp, seq + 1 - 2 * y)
    share = tall.shape[0]
    total = gates_heavy.shape[1] // 2
    slots = rows.shape[2]
    loads = [
        pltpu.make_async_copy(
            gates_heavy.at[:, pl.ds(pl.multiple_of(i * total + me * share, share), share)],
            wide.at[i],
            weight_sem.at[i],
        )
        for i in range(2)
    ]
    loads.append(
        pltpu.make_async_copy(
            down_heavy.at[pl.ds(pl.multiple_of(me * share, share), share)], tall, weight_sem.at[2]
        )
    )
    for load in loads:
        load.start()
    barrier = pltpu.get_barrier_semaphore()
    for peer in (to_core, to_beside):
        pl.semaphore_signal(barrier, inc=1, device_id=peer, device_id_type=MESH)
    pl.semaphore_wait(barrier, 2)

    def copy(src, dst, ssem, rsem, peer):
        return pltpu.make_async_remote_copy(
            src_ref=src,
            dst_ref=dst,
            send_sem=ssem,
            recv_sem=rsem,
            device_id=peer,
            device_id_type=MESH,
        )

    def rows_copy(slot, i, peer):
        return copy(rows.at[slot], rows.at[slot], rows_ssem.at[i], rows_rsem.at[slot], peer)

    rows[me] = own_rows[...]
    rows_copy(me, 0, to_beside).start()
    rows_copy(me, 1, to_core).start()
    beside, diagonal, other = c * n_y + 1 - y, (1 - c) * n_y + 1 - y, (1 - c) * n_y + y
    hidden = down.shape[0]
    step = 256

    @pl.loop(0, normed.shape[0] // step)
    def _(t):
        at = pl.ds(pl.multiple_of(t * step, step), step)
        gate = mm(normed[at], gates[:, :hidden])
        up = mm(normed[at], gates[:, hidden:])
        act, grad_gate, grad_up = glu_and_pull(gate, up, mm_nt(cot[at], down[...]))
        act = act.astype(bf16)
        grad_gate = grad_gate.astype(bf16)
        grad_up = grad_up.astype(bf16)
        act_out[at] = act
        pre_out[at, :hidden] = grad_gate
        pre_out[at, hidden:] = grad_up
        feed_out[at] = mm(act, down[...])
        grad_out[at] = mm_nt(grad_gate, gates[:, :hidden]) + mm_nt(grad_up, gates[:, hidden:])

    for load in loads:
        load.wait()
    rows_copy(beside, 2, to_core).wait_recv()
    rows_copy(beside, 2, to_core).start()

    @pl.loop(0, 4)
    def _(i):
        first, second, third = i == 0, i == 1, i == 2
        slot = jnp.where(
            first, me, jnp.where(second, diagonal, jnp.where(third, beside, other))
        )

        @pl.when(second)
        def _():
            rows_copy(diagonal, 0, to_core).wait_recv()

        @pl.when(i == 3)
        def _():
            rows_copy(other, 0, to_core).wait_recv()

        value, grad = rows[slot, 0], rows[slot, 1]
        gate, up = mm(value, wide[0]), mm(value, wide[1])
        act, grad_gate, grad_up = glu_and_pull(gate, up, mm_nt(grad, tall[...]))
        act = act.astype(bf16)
        grad_gate = grad_gate.astype(bf16)
        grad_up = grad_up.astype(bf16)
        heavy_act_out[slot] = act
        heavy_pre_out[slot, :, :share] = grad_gate
        heavy_pre_out[slot, :, share:] = grad_up
        part[i, 0] = mm(act, tall[...]).astype(bf16)
        part[i, 1] = (mm_nt(grad_gate, wide[0]) + mm_nt(grad_up, wide[1])).astype(bf16)

        @pl.when(second)
        def _():
            copy(part.at[1], from_core.at[0], core_ssem.at[0], core_rsem.at[0], to_core).start()

        @pl.when(third)
        def _():
            copy(part.at[1], from_core.at[0], core_ssem.at[0], core_rsem.at[0], to_core).wait_recv()
            to_y[...] = part[2] + from_core[0]
            copy(to_y, from_y, y_ssem, y_rsem, to_beside).start()

        @pl.when(i == 3)
        def _():
            copy(part.at[3], from_core.at[1], core_ssem.at[1], core_rsem.at[1], to_core).start()

    rows_out[...] = rows[...]
    copy(part.at[3], from_core.at[1], core_ssem.at[1], core_rsem.at[1], to_core).wait()
    copy(to_y, from_y, y_ssem, y_rsem, to_beside).wait()
    sums = part[0].astype(f32) + from_core[1].astype(f32) + from_y[...].astype(f32)
    back_out[...] = sums.astype(bf16)
    copy(part.at[1], from_core.at[0], core_ssem.at[0], core_rsem.at[0], to_core).wait_send()
    for i, slot in enumerate((me, me, beside)):
        rows_copy(slot, i, to_core).wait_send()


def feed_forward(normed, cot, own_rows, gates, down, gates_heavy, down_heavy, n_y):
    count, hidden = normed.shape[0], down.shape[0]
    slots = own_rows.shape[1]
    share = down_heavy.shape[0] // 4
    here, anywhere = pl.BlockSpec(memory_space=pltpu.VMEM), pl.BlockSpec(memory_space=pl.ANY)
    pair = (2, slots, D)
    return pl.pallas_call(
        functools.partial(feed_kernel, n_y),
        out_shape=[
            jax.ShapeDtypeStruct((count, hidden), bf16),
            jax.ShapeDtypeStruct((count, 2 * hidden), bf16),
            jax.ShapeDtypeStruct((count, D), f32),
            jax.ShapeDtypeStruct((count, D), f32),
            jax.ShapeDtypeStruct(pair, bf16),
            jax.ShapeDtypeStruct((4,) + pair, bf16),
            jax.ShapeDtypeStruct((4, slots, share), bf16),
            jax.ShapeDtypeStruct((4, slots, 2 * share), bf16),
        ],
        in_specs=[here] * 5 + [anywhere] * 2,
        out_specs=[here] * 8,
        scratch_shapes=[
            pltpu.VMEM((2, D, share), bf16),
            pltpu.VMEM((share, D), bf16),
            pltpu.VMEM((4,) + pair, bf16),
            pltpu.VMEM((4,) + pair, bf16),
            pltpu.VMEM((2,) + pair, bf16),
            pltpu.VMEM(pair, bf16),
            pltpu.VMEM(pair, bf16),
            pltpu.SemaphoreType.DMA((3,)),
            pltpu.SemaphoreType.DMA((4,)),
            pltpu.SemaphoreType.DMA((3,)),
            pltpu.SemaphoreType.DMA((2,)),
            pltpu.SemaphoreType.DMA((2,)),
            pltpu.SemaphoreType.DMA,
            pltpu.SemaphoreType.DMA,
        ],
        compiler_params=pltpu.CompilerParams(
            collective_id=2, has_side_effects=True, vmem_limit_bytes=60 << 20
        ),
        cost_estimate=pl.CostEstimate(
            flops=12 * count * D * hidden + 48 * slots * D * share,
            bytes_accessed=30 << 20,
            transcendentals=count * hidden + 4 * slots * share,
        ),
        name="feed_forward",
    )(normed, cot, own_rows, gates, down, gates_heavy, down_heavy)


def reduce_kernel(jobs, counts, n_y, *refs):
    n_sources, n_outs, light = counts
    refs = list(refs)

    def take(count):
        taken = refs[:count]
        del refs[:count]
        return taken

    sources = take(n_sources)
    given = take(4 if light else 0)
    outs = take(n_outs)
    made = take(3 if light else 0)
    held = [dict(zip(SCRATCH[job[0]], take(len(SCRATCH[job[0]])))) for job in jobs]
    kinds = [job[0] for job in jobs]
    dp, seq = lax.axis_index("dp"), lax.axis_index("seq")
    x, c = dp // CORES, dp % CORES
    z, y = seq // n_y, seq % n_y
    z_high, z_low = z // 2, z % 2
    group = c * n_y + y

    def device(x=x, c=c, z=z, y=y):
        return (x * CORES + c, z * n_y + y)

    to = {
        "core": device(c=1 - c),
        "x": device(x=1 - x),
        "y": device(y=1 - y),
        "low": device(z=z_high * 2 + 1 - z_low),
        "high": device(z=(1 - z_high) * 2 + z_low),
    }
    owner = (group, x * DEPTH + z)
    origin = device(x=seq // DEPTH, c=dp // n_y, z=seq % DEPTH, y=dp % n_y)
    moved = jnp.logical_or(owner[0] != dp, owner[1] != seq)

    barrier = pltpu.get_barrier_semaphore()

    def greet(peer):
        pl.semaphore_signal(barrier, inc=1, device_id=peer, device_id_type=MESH)

    for peer in to.values():
        greet(peer)
    expected = len(to)
    if "gates" in kinds:
        greet(device(c=1 - c, y=1 - y))
        expected += 1
    pairs = []
    if "down" in kinds:
        pairs += [(moved, owner), (moved, origin)]
    if light:
        pairs += [(seq > 0, (dp, seq - 1)), (seq < DEPTH * n_y - 1, (dp, seq + 1))]
    for present, peer in pairs:

        @pl.when(present)
        def _():
            greet(peer)

    for present, _ in pairs:
        expected = expected + jnp.where(present, 1, 0)
    pl.semaphore_wait(barrier, expected)

    def copy(src, dst, a, stage, k, peer):
        return pltpu.make_async_remote_copy(
            src_ref=src,
            dst_ref=dst,
            send_sem=held[a]["ssem"].at[stage],
            recv_sem=held[a]["rsem"].at[stage, k],
            device_id=peer,
            device_id_type=MESH,
        )

    def send(src, name, k, a, place=None, slot=None):
        dst = held[a][name].at[k] if slot is None else held[a][name].at[k, slot]
        copy(src, dst, a, STAGES[name], k, place).start()

    def arrived(name, a, k):
        buffer = held[a][name].at[k]
        copy(buffer, buffer, a, STAGES[name], k, to["core"]).wait_recv()

    def columns(a, k):
        start, width = jobs[a][2:4]
        return pl.ds(start + k * width, width)

    def local(a, k):
        whole, cols = sources[jobs[a][1]], columns(a, k)
        if kinds[a] in ("xy", "yx"):
            part = whole.at[:, c, :, :, :, cols]
        else:
            part = whole.at[x, :, :, :, :, cols]
        return pltpu.make_async_copy(part, held[a]["own"].at[k], held[a]["lsem"].at[k])

    def begin(a, k):
        whole, cols = sources[jobs[a][1]], columns(a, k)
        local(a, k).start()
        if kinds[a] in ("xy", "yx"):
            send(whole.at[:, 1 - c, :, :, :, cols], "core", k, a, to["core"])
        else:
            send(whole.at[1 - x, :, :, :, :, cols], "xx", k, a, to["x"])

    def first(a, k):
        h, kind = held[a], kinds[a]
        own = h["own"]
        local(a, k).wait()
        if kind not in ("xy", "yx"):
            return
        arrived("core", a, k)

        @pl.loop(0, 2 * DEPTH)
        def _(i):
            for j in range(n_y):
                at = (k, i // DEPTH, i % DEPTH, j)
                own[at] = own[at] + h["core"][at]

        if kind == "xy":
            send(own.at[k, 1 - x], "xx", k, a, to["x"])
        else:
            send(own.at[k, :, :, 1 - y], "yy", k, a, to["y"])

    def second(a, k):
        h, kind = held[a], kinds[a]
        own = h["own"]
        if kind == "xy":
            arrived("xx", a, k)

            @pl.loop(0, DEPTH)
            def _(i):
                for j in range(n_y):
                    at = (k, x, i, j)
                    own[at] = own[at] + h["xx"][k, i, j]

            send(own.at[k, x, :, 1 - y], "yy", k, a, to["y"])
        elif kind == "yx":
            arrived("yy", a, k)

            @pl.loop(0, DEPTH)
            def _(i):
                for j in range(2):
                    at = (k, j, i, y)
                    own[at] = own[at] + h["yy"][k, j, i]

            send(own.at[k, 1 - x, :, y], "xx", k, a, to["x"])

    def third(a, k):
        h, kind = held[a], kinds[a]
        own = h["own"]
        if kind in ("xy", "yx"):
            name = "yy" if kind == "xy" else "xx"
            arrived(name, a, k)

            @pl.loop(0, DEPTH)
            def _(i):
                at = (k, x, i, y)
                own[at] = own[at] + h[name][k, i]

            for high in range(2):
                send(own.at[k, x, high * 2 + 1 - z_low, y], "za", k, a, to["low"], high)
        else:
            arrived("xx", a, k)

            @pl.loop(0, DEPTH)
            def _(i):
                for g in range(own.shape[1]):
                    for j in range(own.shape[3]):
                        at = (k, g, i, j)
                        own[at] = own[at] + h["xx"][at]

            for high in range(2):
                send(own.at[k, :, high * 2 + 1 - z_low], "za", k, a, to["low"], high)

    def fourth(a, k):
        h, kind = held[a], kinds[a]
        own = h["own"]
        arrived("za", a, k)
        if kind in ("xy", "yx"):
            for high in range(2):
                at = (k, x, high * 2 + z_low, y)
                own[at] = own[at] + h["za"][k, high]
            send(own.at[k, x, (1 - z_high) * 2 + z_low, y], "zb", k, a, to["high"])
        else:

            @pl.loop(0, own.shape[1])
            def _(g):
                for j in range(own.shape[3]):
                    for high in range(2):
                        at = (k, g, high * 2 + z_low, j)
                        own[at] = own[at] + h["za"][k, high, g, j]

            send(own.at[k, :, (1 - z_high) * 2 + z_low], "zb", k, a, to["high"])

    def fifth(a, k):
        h = held[a]
        kind, _, _, width, _, out, start = jobs[a]
        own = h["own"]
        arrived("zb", a, k)
        if kind in ("xy", "yx"):
            total = own[k, x, z, y].astype(f32) + h["zb"][k].astype(f32)
            outs[out][:, start + k * width : start + (k + 1) * width] = total
        elif kind == "down":
            h["sum"][k] = own[k, 0, z, 0] + h["zb"][k, 0, 0]

            @pl.when(moved)
            def _():
                send(h["sum"].at[k], "dd", k, a, owner)

            @pl.when(jnp.logical_not(moved))
            def _():
                h["dd"][k] = h["sum"][k]
        else:

            @pl.loop(0, CORES)
            def _(g):
                for j in range(n_y):
                    h["sum"][k, g * n_y + j] = own[k, g, z, j] + h["zb"][k, g, j]

            h["dd"][k, group] = h["sum"][k, group]
            for g, j in ((1 - c, y), (c, 1 - y), (1 - c, 1 - y)):
                send(h["sum"].at[k, g * n_y + j], "dd", k, a, device(c=g, y=j), group)

    def last(a, k):
        h = held[a]
        kind, _, _, width, chunks, out, start = jobs[a]
        if kind == "gates":
            part = h["dd"].at[k, pl.ds(0, 3)]
            copy(part, part, a, STAGES["dd"], k, to["core"]).wait_recv()
            for g in range(4):
                at = start + (g * chunks + k) * width
                outs[out][:, at : at + width] = h["dd"][k, g].astype(f32)
        elif kind == "down":

            @pl.when(moved)
            def _():
                arrived("dd", a, k)

            outs[out][:, start + k * width : start + (k + 1) * width] = h["dd"][k].astype(f32)

    lists = {"all": [], "rest": []}
    for a, job in enumerate(jobs):
        lists["all" if job[0] in ("xy", "yx") else "rest"].append([(a, k) for k in range(job[4])])
    stages = (begin, first, second, third, fourth, fifth, last)
    longest = max(len(interleave(parts)) for parts in lists.values())
    events = []
    for name, parts in lists.items():
        order = interleave(parts)
        for i, what in enumerate(order):
            for stage, lag in zip(stages, LAGS[name]):
                events.append((i * longest / len(order) + lag, len(events), stage, what))
    if light:
        own_ref, edge_ref, grad_ref, weights = given
        own_out, edge_out, edges_in = made
        ready, landed, edge_ssem, edge_rsem = refs
        pieces = own_ref.shape[0]
        reach = (seq > 0, seq < DEPTH * n_y - 1)
        inner = (own_ref, edge_ref, grad_ref, own_out, edge_out)

        def edge_copy(side, p):
            src = ready.at[p, pl.ds(side * RADIUS, RADIUS)]
            dst = landed.at[p, pl.ds((1 - side) * RADIUS, RADIUS)]
            return pltpu.make_async_remote_copy(
                src_ref=src,
                dst_ref=dst,
                send_sem=edge_ssem.at[side],
                recv_sem=edge_rsem.at[1 - side, p],
                device_id=(dp, seq - 1 + 2 * side),
                device_id_type=MESH,
            )

        def unit(p, g):
            light_back_unit(reach, (g,), *[ref.at[pl.ds(p, 1)] for ref in inner])
            if g == 1:
                rows = mm_nt(edge_out[p], weights[:, D:])
                ready[p] = rows.astype(bf16)
                for side in range(2):

                    @pl.when(reach[side])
                    def _():
                        edge_copy(side, p).start()

        for p in range(pieces):
            for g in range(2):
                events.append(((2 * p + g) * 1.2, len(events), unit, (p, g)))
    for _, _, stage, what in sorted(events, key=lambda e: e[:2]):
        stage(*what)

    if light:
        for side in range(2):
            rows = pl.ds(side * RADIUS, RADIUS)

            @pl.when(reach[side])
            def _():
                for p in range(pieces):
                    edge_copy(1 - side, p).wait_recv()
                    edges_in[p, rows] = landed[p, rows]
                whole = ready.at[:, rows]
                pltpu.make_async_remote_copy(
                    src_ref=whole,
                    dst_ref=whole,
                    send_sem=edge_ssem.at[side],
                    recv_sem=edge_rsem.at[side, 0],
                    device_id=(dp, seq - 1 + 2 * side),
                    device_id_type=MESH,
                ).wait_send()

            @pl.when(jnp.logical_not(reach[side]))
            def _():
                for p in range(pieces):
                    edges_in[p, rows] = jnp.zeros((RADIUS, D), bf16)

    for a, kind in enumerate(kinds):
        h = held[a]
        for name in ("core", "xx", "yy", "za", "zb"):
            if name in h:
                copy(h[name], h[name], a, STAGES[name], 0, to["core"]).wait_send()
        if kind == "gates":
            part = h["dd"].at[:, pl.ds(0, 3)]
            copy(part, part, a, STAGES["dd"], 0, to["core"]).wait_send()
        elif kind == "down":

            @pl.when(moved)
            def _():
                copy(h["dd"], h["dd"], a, STAGES["dd"], 0, to["core"]).wait_send()


def interleave(parts):
    keyed = [((i + 0.5) / len(p), n, v) for n, p in enumerate(parts) for i, v in enumerate(p)]
    return [v for _, _, v in sorted(keyed)]


LAGS = {"all": (-4, 0, 2, 4, 6, 8, 8), "rest": (-2, -1, -1, 1.5, 3.5, 5.5, 8)}
STAGES = {"core": 0, "xx": 1, "yy": 2, "za": 3, "zb": 4, "dd": 5}
SCRATCH = {
    "xy": ("own", "core", "xx", "yy", "za", "zb", "lsem", "rsem", "ssem"),
    "yx": ("own", "core", "xx", "yy", "za", "zb", "lsem", "rsem", "ssem"),
    "gates": ("own", "xx", "za", "zb", "sum", "dd", "lsem", "rsem", "ssem"),
    "down": ("own", "xx", "za", "zb", "sum", "dd", "lsem", "rsem", "ssem"),
}


def reduce_all(values, jobs, widths, n_y, collective_id, light=()):
    operands, scratch = [], []
    for value, inner in values:
        height, columns = value.shape
        lead = (2, CORES, DEPTH, n_y) if inner else (2, 1, DEPTH, 1)
        operands.append(value.reshape(lead + (height // math.prod(lead), columns)))
    heights = {job[5]: operands[job[1]].shape[4] for job in jobs}
    out_shape = [jax.ShapeDtypeStruct((heights[o], w), f32) for o, w in enumerate(widths)]
    for kind, source, _, width, k, _, _ in jobs:
        _, inner, _, outer, height, _ = operands[source].shape
        if kind == "xy":
            shapes = [(2, DEPTH, n_y)] * 2 + [(DEPTH, n_y), (DEPTH,), (2,), ()]
        elif kind == "yx":
            shapes = [(2, DEPTH, n_y)] * 2 + [(DEPTH,), (2, DEPTH), (2,), ()]
        else:
            both = (inner, outer)
            shapes = [(inner, DEPTH, outer)] * 2 + [(2,) + both, both]
            shapes += [(4,), (4,)] if kind == "gates" else [(), ()]
        scratch += [pltpu.VMEM((k,) + shape + (height, width), bf16) for shape in shapes]
        scratch += [
            pltpu.SemaphoreType.DMA((k,)),
            pltpu.SemaphoreType.DMA((6, k)),
            pltpu.SemaphoreType.DMA((6,)),
        ]
    if light:
        pieces, edge_rows = light[1].shape[:2]
        out_shape += [jax.ShapeDtypeStruct(v.shape, bf16) for v in light[:2]]
        out_shape.append(jax.ShapeDtypeStruct((pieces, edge_rows, D), bf16))
        scratch += [pltpu.VMEM((pieces, edge_rows, D), bf16)] * 2
        scratch += [pltpu.SemaphoreType.DMA((2,)), pltpu.SemaphoreType.DMA((2, pieces))]
    total = sum(v.size for v, _ in values)
    here = pl.BlockSpec(memory_space=pltpu.VMEM)
    return pl.pallas_call(
        functools.partial(
            reduce_kernel, tuple(jobs), (len(values), len(widths), bool(light)), n_y
        ),
        out_shape=out_shape,
        in_specs=[pl.BlockSpec(memory_space=pl.ANY)] * len(values) + [here] * len(light),
        out_specs=[here] * len(out_shape),
        scratch_shapes=scratch,
        compiler_params=pltpu.CompilerParams(
            collective_id=collective_id, has_side_effects=True, vmem_limit_bytes=60 << 20
        ),
        cost_estimate=pl.CostEstimate(
            flops=2 * total, bytes_accessed=32 * total, transcendentals=0
        ),
        name="reduce_gradients",
    )(*operands, *light)


def copy_kernel(*refs):
    count = len(refs) // 2
    for i in range(count):
        refs[count + i][...] = refs[i][...]


def copy_all(values):
    count = len(values)
    return pl.pallas_call(
        copy_kernel,
        out_shape=[jax.ShapeDtypeStruct(v.shape, v.dtype) for v in values],
        in_specs=[pl.BlockSpec(memory_space=pltpu.VMEM)] * count,
        out_specs=[pl.BlockSpec(memory_space=pltpu.VMEM)] * count,
        name="copy_outputs",
    )(*values)


def per_device(
    layer_input,
    cotangent,
    first_gain,
    light_inputs,
    light_output,
    heavy_queries,
    heavy_keyvalue,
    heavy_output,
    second_gain,
    router,
    light_gates,
    light_down,
    heavy_gates,
    heavy_down,
    query_index,
    query_count,
    key_index,
    key_count,
    feed_slot,
):
    pieces, tokens = layer_input.shape[:2]
    rows = pieces * tokens
    n_dp, n_seq = lax.axis_size("dp"), lax.axis_size("seq")
    n_x, n_y = n_dp // CORES, n_seq // DEPTH
    seq_rank = lax.axis_index("seq")
    core = Ring("dp", 1, CORES)
    ring_x = Ring("dp", CORES, n_x)
    ring_y = Ring("seq", 1, n_y)
    ring_z = Ring("seq", n_y, DEPTH)
    capacity = max(2, 3 * rows // (16 * n_seq))
    slots = n_seq * capacity
    each = D // (n_dp * n_seq)
    kernels = each % 8 == 0 and n_x == n_y == 2

    def reduce_grad(value, first, second):
        height, width = value.shape
        chunk = height // (n_dp * n_seq)
        parts = value.reshape(n_x, CORES, DEPTH, n_y, chunk, width)
        parts = core.scatter_sum(parts, 1).astype(bf16)
        dims = ["x", "z", "y"]
        rings = {"x": ring_x, "y": ring_y, "z": ring_z}
        order = [first, second, [d for d in dims if d not in (first, second)][0]]
        for i, d in enumerate(order):
            at = dims.index(d)
            parts = rings[d].scatter_sum(parts, at)
            if i < 2:
                parts = parts.astype(bf16)
            dims.remove(d)
        return parts

    def reduce_split(value):
        half = value.shape[1] // 2
        return jnp.concatenate(
            [
                reduce_grad(value[:, :half], "x", "y"),
                reduce_grad(value[:, half:], "y", "x"),
            ],
            axis=1,
        )

    def reduce_vectors(value):
        count, width = value.shape
        chunk = width // (n_dp * n_seq)
        parts = value.reshape(count, n_x, CORES, DEPTH, n_y, chunk)
        parts = core.scatter_sum(parts, 2)
        parts = ring_x.scatter_sum(parts, 1)
        parts = ring_z.scatter_sum(parts, 1)
        return ring_y.scatter_sum(parts, 1)

    ends = n_seq - 1
    left_rows = lax.ppermute(
        layer_input[:, tokens - RADIUS :], "seq", [(i, i + 1) for i in range(ends)]
    )
    right_rows = lax.ppermute(layer_input[:, :RADIUS], "seq", [(i + 1, i) for i in range(ends)])
    position = jnp.arange(tokens, dtype=jnp.int32)
    key_pick = (key_index[:, :, None] == position[None, None, :]).astype(bf16)
    query_live = jnp.arange(QCAP, dtype=jnp.int32)[None, :] < query_count
    query_pick = (query_index[:, :, None] == position[None, None, :]).astype(bf16)
    live_pick = query_pick * query_live[:, :, None].astype(bf16)
    key_raw = jnp.einsum("pkt,ptd->pkd", key_pick, layer_input, preferred_element_type=f32).astype(
        bf16
    )
    key_all = lax.all_gather(key_raw, "seq", axis=1, tiled=True)

    gain_first = first_gain.astype(f32)
    inputs = layer_input.astype(f32)
    unit_first, scale_first = norm_parts(inputs)
    normed_first = (unit_first * gain_first).astype(bf16)
    normed_flat = normed_first.reshape(rows, D)
    own_proj = mm(normed_flat, light_inputs).astype(bf16).reshape(pieces, tokens, 3 * D)
    edge_rows = jnp.concatenate([left_rows, right_rows], axis=1)
    normed_edge = (norm_parts(edge_rows.astype(f32))[0] * gain_first).astype(bf16)
    edge_flat = normed_edge.reshape(pieces * 2 * RADIUS, D)
    edge_proj = mm(edge_flat, light_inputs[:, D:]).astype(bf16)
    edge_proj = edge_proj.reshape(pieces, 2 * RADIUS, 2 * D)

    reach = jnp.stack([seq_rank > 0, seq_rank < n_seq - 1]).astype(jnp.int32)
    light_att = light_attention(reach, own_proj, edge_proj).reshape(rows, D)

    key_slots = n_seq * KCAP
    key_rows_all = key_all.reshape(pieces * key_slots, D)
    normed_keys = (norm_parts(key_rows_all.astype(f32))[0] * gain_first).astype(bf16)
    heavy_pairs = mm(normed_keys, heavy_keyvalue).astype(bf16).reshape(pieces, key_slots, 2 * D)
    key_live = jnp.arange(KCAP, dtype=jnp.int32)[None, None, :] < key_count[:, :, None]
    key_live = key_live.reshape(pieces, 1, key_slots).astype(f32)
    query_rows = (
        jnp.einsum("pqt,ptd->pqd", query_pick, normed_first, preferred_element_type=f32)
        .astype(bf16)
        .reshape(pieces * QCAP, D)
    )
    heavy_query = mm(query_rows, heavy_queries).astype(bf16).reshape(pieces, QCAP, D)
    heavy_att = heavy_attention(heavy_query, heavy_pairs, key_live)
    heavy_spread = (
        jnp.einsum("pqt,pqd->ptd", live_pick, heavy_att, preferred_element_type=f32)
        .astype(bf16)
        .reshape(rows, D)
    )

    middle = (
        inputs.reshape(rows, D) + mm(light_att, light_output) + mm(heavy_spread, heavy_output)
    )
    gain_second = second_gain.astype(f32)
    unit_second, scale_second = norm_parts(middle)
    normed_second = (unit_second * gain_second).astype(bf16)

    slot_of = feed_slot.reshape(1, rows)
    pick = (jnp.arange(slots, dtype=jnp.int32)[:, None] == slot_of).astype(bf16)
    routed = feed_slot.reshape(rows, 1) >= 0
    cot = cotangent.reshape(rows, D)
    gating = jax.nn.sigmoid(
        jnp.sum(normed_second.astype(f32) * router.astype(f32), axis=-1, keepdims=True)
    )
    grad_token = (gating * cot.astype(f32)).astype(bf16)
    feed_in = mm(pick, normed_second).astype(bf16)
    grad_in = mm(pick, grad_token).astype(bf16)

    wide = heavy_gates.shape[1] // 2
    share = wide // 4
    if kernels:
        light_act, grad_light_pre, light_feed, grad_light, back, feed_all, heavy_act, heavy_pre = (
            feed_forward(
                normed_second,
                cot,
                jnp.stack([feed_in, grad_in]),
                light_gates,
                light_down,
                heavy_gates,
                heavy_down,
                n_y,
            )
        )
        feed_rows = feed_all[:, 0].reshape(4 * slots, D)
        grad_rows = feed_all[:, 1].reshape(4 * slots, D)
        heavy_act = heavy_act.reshape(4 * slots, share)
        heavy_pre = heavy_pre.reshape(4 * slots, 2 * share)
        heavy_result, grad_feed_in = back[0], back[1]
    else:
        feed_rows, grad_rows = feed_in, grad_in
        hidden = light_down.shape[0]
        pre = mm(normed_second, light_gates)
        light_act, *grads = glu_and_pull(pre[:, :hidden], pre[:, hidden:], mm_nt(cot, light_down))
        light_act = light_act.astype(bf16)
        grad_light_pre = jnp.concatenate(grads, axis=1).astype(bf16)
        light_feed = mm(light_act, light_down)
        grad_light = mm_nt(grad_light_pre, light_gates)
        pre = mm(feed_in, heavy_gates)
        heavy_act, *grads = glu_and_pull(pre[:, :wide], pre[:, wide:], mm_nt(grad_in, heavy_down))
        heavy_act = heavy_act.astype(bf16)
        heavy_pre = jnp.concatenate(grads, axis=1).astype(bf16)
        heavy_result = mm(heavy_act, heavy_down).astype(bf16)
        grad_feed_in = mm_nt(heavy_pre, heavy_gates).astype(bf16)
    heavy_down_grad = mm_tn(heavy_act, grad_rows).astype(bf16)
    heavy_gates_grad = mm_tn(feed_rows, heavy_pre).astype(bf16)
    light_down_grad = mm_tn(light_act, cot).astype(bf16)
    light_gates_grad = mm_tn(normed_second, grad_light_pre).astype(bf16)

    token_result = mm_tn(pick, heavy_result)
    output = (middle + light_feed + gating * token_result).astype(bf16).reshape(layer_input.shape)
    grad_gating = jnp.sum(cot.astype(f32) * token_result, axis=-1, keepdims=True)
    grad_logit = grad_gating * gating * (1.0 - gating)
    grad_second = (
        grad_light
        + mm_tn(pick, grad_feed_in)
        + grad_logit * router.astype(f32)
    )
    router_grad = jnp.sum(grad_logit * normed_second.astype(f32), axis=0)
    second_gain_grad = jnp.sum(grad_second * unit_second, axis=0)
    grad_middle = cot.astype(f32) + norm_pull(grad_second, middle, scale_second, gain_second)
    grad_mid_low = grad_middle.astype(bf16)

    light_output_grad = mm_tn(light_att, grad_mid_low).astype(bf16)
    grad_light_att = mm_nt(grad_mid_low, light_output).astype(bf16)
    grad_query_rows = (
        jnp.einsum(
            "pqt,ptd->pqd",
            live_pick,
            grad_mid_low.reshape(pieces, tokens, D),
            preferred_element_type=f32,
        )
        .astype(bf16)
        .reshape(pieces * QCAP, D)
    )
    heavy_output_grad = mm_tn(heavy_att.reshape(pieces * QCAP, D), grad_query_rows).astype(bf16)
    grad_heavy_att = mm_nt(grad_query_rows, heavy_output).astype(bf16)

    grad_hq_low, grad_hkv_low = heavy_attention_back(
        heavy_query,
        heavy_pairs,
        key_live,
        grad_heavy_att.reshape(pieces, QCAP, D),
    )
    grad_hq_low = grad_hq_low.reshape(pieces * QCAP, D)
    grad_hkv_low = grad_hkv_low.reshape(pieces * key_slots, 2 * D)
    grad_key_rows = mm_nt(grad_hkv_low, heavy_keyvalue).astype(bf16)
    heavy_keyvalue_grad = mm_tn(normed_keys, grad_hkv_low).astype(bf16)
    heavy_queries_grad = mm_tn(query_rows, grad_hq_low).astype(bf16)

    grad_light_att, grad_key_rows = lax.optimization_barrier((grad_light_att, grad_key_rows))
    grad_key_own = lax.psum_scatter(
        grad_key_rows.reshape(pieces, key_slots, D), "seq", scatter_dimension=1, tiled=True
    )
    grad_light_att = grad_light_att.reshape(pieces, tokens, D)
    if kernels:
        early = [
            (light_gates_grad, True),
            (light_down_grad, True),
            (light_output_grad, True),
            (heavy_output_grad, True),
            (heavy_gates_grad, True),
            (heavy_down_grad, False),
        ]
        half = light_gates_grad.shape[1] // 2
        jobs = [
            ("xy", 0, 0, 512, half // 512, 0, 0),
            ("yx", 0, half, 512, half // 512, 0, half),
            ("yx", 1, 0, 384, D // 384, 1, 0),
            ("xy", 2, 0, 384, D // 384, 2, 0),
            ("yx", 3, 0, 384, D // 384, 3, 0),
            ("gates", 4, 0, 256, share // 256, 4, 0),
            ("gates", 4, share, 256, share // 256, 4, wide),
            ("down", 5, 0, 128, D // 128, 5, 0),
        ]
        widths = (2 * half, D, D, D, 2 * wide, D)
        *early, grad_own, grad_edge, grad_around = reduce_all(
            early, jobs, widths, n_y, 0, (own_proj, edge_proj, grad_light_att, light_inputs)
        )
    else:
        grad_own, grad_edge = light_attention_back(reach, own_proj, edge_proj, grad_light_att)
        early = [light_gates_grad, light_down_grad, light_output_grad, heavy_output_grad]
        early += [heavy_gates_grad, heavy_down_grad]
        early = [reduce_split(v) for v in early]
        grad_edge_rows = mm_nt(grad_edge.reshape(-1, 2 * D), light_inputs[:, D:]).astype(bf16)
        grad_edge_rows = grad_edge_rows.reshape(pieces, 2 * RADIUS, D)
        from_right = lax.ppermute(
            grad_edge_rows[:, :RADIUS], "seq", [(i + 1, i) for i in range(ends)]
        )
        from_left = lax.ppermute(
            grad_edge_rows[:, RADIUS:], "seq", [(i, i + 1) for i in range(ends)]
        )
        grad_around = jnp.concatenate([from_left, from_right], axis=1)
    grad_own = grad_own.reshape(rows, 3 * D)
    grad_edge = grad_edge.reshape(pieces * 2 * RADIUS, 2 * D)
    light_query_grad = mm_tn(normed_flat, grad_own[:, :D]).astype(bf16)
    light_pair_grad = mm_tn(normed_flat, grad_own[:, D:]) + mm_tn(edge_flat, grad_edge)
    light_pair_grad = light_pair_grad.astype(bf16)

    grad_hq_rows = mm_nt(grad_hq_low, heavy_queries).astype(bf16).reshape(pieces, QCAP, D)
    grad_first = mm_nt(grad_own, light_inputs).reshape(pieces, tokens, D)
    grad_slots = jnp.concatenate([grad_hq_rows, grad_key_own.astype(bf16)], axis=1)
    both_pick = jnp.concatenate([query_pick, key_pick], axis=1)
    grad_first = (
        grad_first
        + jnp.einsum("pkt,pkd->ptd", both_pick, grad_slots, preferred_element_type=f32)
        + grad_around.astype(f32)
    )
    first_gain_grad = jnp.sum(grad_first * unit_first, axis=(0, 1))
    input_grad = grad_middle.reshape(pieces, tokens, D) + norm_pull(
        grad_first, inputs, scale_first, gain_first
    )
    vectors = jnp.stack([first_gain_grad, second_gain_grad, router_grad])
    devices = n_dp * n_seq
    if kernels:
        lines = vectors.reshape(3, devices, each).transpose(1, 0, 2)
        lines = jnp.pad(lines, ((0, 0), (0, 5), (0, 256 - each))).reshape(devices * 8, 256)
        late = [light_query_grad, light_pair_grad, heavy_queries_grad, heavy_keyvalue_grad]
        late = [(v, True) for v in [*late, lines.astype(bf16)]]
        jobs = (
            ("xy", 0, 0, 384, 1, 0, 0),
            ("yx", 0, 384, 384, 1, 0, 384),
            ("xy", 1, 0, 384, 2, 0, D),
            ("yx", 1, D, 384, 2, 0, 2 * D),
            ("xy", 2, 0, 384, 1, 1, 0),
            ("yx", 2, 384, 384, 1, 1, 384),
            ("xy", 3, 0, 384, 2, 2, 0),
            ("yx", 3, D, 384, 2, 2, D),
            ("xy", 4, 0, 256, 1, 3, 0),
        )
        sums = reduce_all(late, jobs, (3 * D, D, 2 * D, 256), n_y, 1)
        *sums, lines = copy_all([*early, *sums])
        early, late = sums[: len(early)], sums[len(early) :]
        vectors = lines[:3, :each]
    else:
        late = [
            jnp.concatenate([light_query_grad, light_pair_grad], axis=1),
            heavy_queries_grad,
            heavy_keyvalue_grad,
        ]
        late = [reduce_split(v) for v in late]
        vectors = reduce_vectors(vectors)
    light_gates_grad, light_down_grad, light_output_grad, heavy_output_grad = early[:4]
    return (
        output,
        input_grad,
        vectors[0],
        late[0],
        light_output_grad,
        late[1],
        late[2],
        heavy_output_grad,
        vectors[1],
        vectors[2],
        light_gates_grad,
        light_down_grad,
        early[4],
        early[5],
    )


def solution(mesh):
    rows = P(("dp", "seq"), None)
    line = P(("dp", "seq"))
    tokens = P("dp", "seq", None)
    slots = P("dp", "seq")
    return jax.shard_map(
        per_device,
        mesh=mesh,
        in_specs=(tokens, tokens) + (P(),) * 12 + (slots, slots, slots, P("dp", None), slots),
        out_specs=(tokens, tokens, line) + (rows,) * 5 + (line, line) + (rows,) * 4,
        check_vma=False,
    )
```

```python
import functools
import math
import jax
import jax.numpy as jnp
from jax import lax
from jax.experimental import pallas as pl
from jax.experimental.pallas import tpu as pltpu
from jax.sharding import PartitionSpec as P
D = 768
HL = 8
LHD = 96
HH = 12
HHD = 64
RADIUS = 128
QCAP = 64
KCAP = 64
CORES = 2
DEPTH = 4
MESH = pl.DeviceIdType.MESH
epsilon = 1e-06
bf16 = jnp.bfloat16
f32 = jnp.float32


def dot(left, right, over):
    return lax.dot_general(left, right, (over, ((), ())), preferred_element_type=f32)


def mm(left, right):
    return dot(left, right, ((1,), (0,)))


def mm_nt(left, right):
    return dot(left, right, ((1,), (1,)))


def mm_tn(left, right):
    return dot(left, right, ((0,), (0,)))


class Ring:
    def __init__(self, axis, stride, count):
        self.axis, self.stride, self.count = axis, stride, count
        self.place = (lax.axis_index(axis) // stride) % count

    def shift(self, value, by):
        total = lax.axis_size(self.axis)
        pairs = []
        for i in range(total):
            c = (i // self.stride) % self.count
            pairs.append((i, i + ((c + by) % self.count - c) * self.stride))
        return lax.ppermute(value, self.axis, pairs)

    def scatter_sum(self, value, dim):
        own = lax.dynamic_index_in_dim(value, self.place, dim, keepdims=False)
        total = own.astype(f32)
        for by in range(1, self.count):
            send = lax.dynamic_index_in_dim(
                value, (self.place + by) % self.count, dim, keepdims=False
            )
            total = total + self.shift(send, by).astype(f32)
        return total

    def gather(self, value, dim):
        parts = [value] + [self.shift(value, by) for by in range(1, self.count)]
        return jnp.concatenate(parts, axis=dim)

    def return_sum(self, joined, dim):
        parts = jnp.split(joined, self.count, axis=dim)
        total = parts[0].astype(f32)
        for by in range(1, self.count):
            total = total + self.shift(parts[by], self.count - by).astype(f32)
        return total


def norm_parts(values):
    scale = lax.rsqrt(jnp.mean(values * values, axis=-1, keepdims=True) + epsilon)
    return values * scale, scale


def norm_pull(grad, values, scale, gain):
    weighted = grad * gain
    inner = jnp.mean(weighted * values, axis=-1, keepdims=True)
    return scale * weighted - values * (scale * scale * scale) * inner


def head_windows():
    windows = []
    for h in range(4):
        first, end = h * LHD, (h + 1) * LHD
        windows.append((first // 128 * 128, -(-end // 128) * 128, first, end))
    return windows


def lane_mask(shape, first, end):
    lane = lax.broadcasted_iota(jnp.int32, shape, 1)
    return (lane >= first) & (lane < end)


def join_heads(parts):
    lane = lax.broadcasted_iota(jnp.int32, (parts[0].shape[0], 128), 1)
    return jnp.concatenate(
        [
            jnp.where(lane < 96, parts[0], parts[1][:, :128]),
            jnp.where(lane < 64, parts[1][:, 128:], parts[2][:, :128]),
            jnp.where(lane < 32, parts[2][:, 128:], parts[3]),
        ],
        axis=1,
    )


def light_kernel(ends_ref, own_ref, edge_ref, out_ref):
    half = RADIUS
    factor = LHD ** (-0.5)
    for block in range(2):
        rows = slice(block * half, (block + 1) * half)
        row = lax.broadcasted_iota(jnp.int32, (half, 2 * half), 0)
        col = lax.broadcasted_iota(jnp.int32, (half, 2 * half), 1)
        keep_own = col <= row + half if block == 0 else col >= row
        row, col = row[:, :half], col[:, :half]
        keep_edge = (col >= row if block == 0 else col <= row) & (ends_ref[block] > 0)
        for group in range(2):
            mixed = []
            for a, b, first, end in head_windows():
                lanes = slice(group * 384 + a, group * 384 + b)
                keys = slice(D + lanes.start, D + lanes.stop)
                values = slice(2 * D + lanes.start, 2 * D + lanes.stop)
                query = own_ref[0, rows, lanes]
                query = jnp.where(
                    lane_mask(query.shape, first - a, end - a), query, jnp.zeros_like(query)
                )
                s_own = jnp.where(keep_own, mm_nt(query, own_ref[0, :, keys]), -1e30)
                s_edge = jnp.where(keep_edge, mm_nt(query, edge_ref[0, rows, lanes]), -1e30)
                top = jnp.maximum(
                    jnp.max(s_own, axis=1, keepdims=True), jnp.max(s_edge, axis=1, keepdims=True)
                )
                e_own = jnp.exp((s_own - top) * factor)
                e_edge = jnp.exp((s_edge - top) * factor)
                total = jnp.sum(e_own, axis=1, keepdims=True) + jnp.sum(
                    e_edge, axis=1, keepdims=True
                )
                mix = mm(e_own.astype(bf16), own_ref[0, :, values])
                mix += mm(
                    e_edge.astype(bf16), edge_ref[0, rows, slice(D + lanes.start, D + lanes.stop)]
                )
                mixed.append(mix * (1.0 / total))
            out_ref[0, rows, group * 384 : (group + 1) * 384] = join_heads(mixed).astype(bf16)


def light_attention(ends, own, edge):
    pieces, tokens = own.shape[:2]
    return pl.pallas_call(
        light_kernel,
        out_shape=jax.ShapeDtypeStruct((pieces, tokens, D), bf16),
        grid_spec=pltpu.PrefetchScalarGridSpec(
            num_scalar_prefetch=1,
            grid=(pieces,),
            in_specs=[
                pl.BlockSpec((1, tokens, 3 * D), lambda p, e: (p, 0, 0)),
                pl.BlockSpec((1, 2 * RADIUS, 2 * D), lambda p, e: (p, 0, 0)),
            ],
            out_specs=pl.BlockSpec((1, tokens, D), lambda p, e: (p, 0, 0)),
        ),
        compiler_params=pltpu.CompilerParams(vmem_limit_bytes=32 << 20),
        cost_estimate=pl.CostEstimate(
            flops=pieces * HL * tokens * 384 * 256 * 4,
            bytes_accessed=pieces * (tokens * 4 * D + 2 * RADIUS * 2 * D) * 2,
            transcendentals=pieces * HL * tokens * 384,
        ),
        name="light_attention",
    )(ends, own, edge)


def light_back_unit(reach, groups, own_ref, edge_ref, grad_ref, own_out, edge_out):
    half = RADIUS
    factor = LHD ** (-0.5)
    for group in groups:
        dk_own, dv_own = [None] * 4, [None] * 4
        for block in range(2):
            rows = slice(block * half, (block + 1) * half)
            key = lax.broadcasted_iota(jnp.int32, (2 * half, half), 0)
            que = lax.broadcasted_iota(jnp.int32, (2 * half, half), 1)
            keep_own = key <= que + half if block == 0 else key >= que
            key, que = key[:half], que[:half]
            keep_edge = (key >= que if block == 0 else key <= que) & reach[block]
            dq, dk_edge, dv_edge = [], [], []
            for h, (a, b, first, end) in enumerate(head_windows()):
                lanes = slice(group * 384 + a, group * 384 + b)
                after = slice(D + lanes.start, D + lanes.stop)
                last = slice(2 * D + lanes.start, 2 * D + lanes.stop)
                mask = lane_mask((half, b - a), first - a, end - a)
                query = own_ref[0, rows, lanes]
                query = jnp.where(mask, query, jnp.zeros_like(query))
                grad = grad_ref[0, rows, lanes]
                grad = jnp.where(mask, grad, jnp.zeros_like(grad))
                k_own, k_edge = own_ref[0, :, after], edge_ref[0, rows, lanes]
                v_own, v_edge = own_ref[0, :, last], edge_ref[0, rows, after]
                s_own = jnp.where(keep_own, mm_nt(k_own, query), -1e30)
                s_edge = jnp.where(keep_edge, mm_nt(k_edge, query), -1e30)
                top = jnp.maximum(
                    jnp.max(s_own, axis=0, keepdims=True), jnp.max(s_edge, axis=0, keepdims=True)
                )
                e_own = jnp.exp((s_own - top) * factor)
                e_edge = jnp.exp((s_edge - top) * factor)
                total = jnp.sum(e_own, axis=0, keepdims=True) + jnp.sum(
                    e_edge, axis=0, keepdims=True
                )
                scale = 1.0 / total
                p_own, p_edge = e_own * scale, e_edge * scale
                g_own, g_edge = mm_nt(v_own, grad), mm_nt(v_edge, grad)
                inner = jnp.sum(p_own * g_own, axis=0, keepdims=True) + jnp.sum(
                    p_edge * g_edge, axis=0, keepdims=True
                )
                d_own = (p_own * (g_own - inner)).astype(bf16)
                d_edge = (p_edge * (g_edge - inner)).astype(bf16)
                dv = mm(p_own.astype(bf16), grad)
                dk = mm(d_own, query)
                dv_own[h] = dv if block == 0 else dv_own[h] + dv
                dk_own[h] = dk if block == 0 else dk_own[h] + dk
                dv_edge.append(mm(p_edge.astype(bf16), grad))
                dk_edge.append(mm(d_edge, query) * factor)
                dq.append((mm_tn(d_own, k_own) + mm_tn(d_edge, k_edge)) * factor)
            at = slice(group * 384, (group + 1) * 384)
            at_v = slice(D + at.start, D + at.stop)
            own_out[0, rows, at] = join_heads(dq).astype(bf16)
            edge_out[0, rows, at] = join_heads(dk_edge).astype(bf16)
            edge_out[0, rows, at_v] = join_heads(dv_edge).astype(bf16)
        at_w = slice(2 * D + at.start, 2 * D + at.stop)
        own_out[0, :, at_v] = (join_heads(dk_own) * factor).astype(bf16)
        own_out[0, :, at_w] = join_heads(dv_own).astype(bf16)


def light_back_kernel(ends_ref, *refs):
    light_back_unit((ends_ref[0] > 0, ends_ref[1] > 0), range(2), *refs)


def light_attention_back(ends, own, edge, grad):
    pieces, tokens = own.shape[:2]
    return pl.pallas_call(
        light_back_kernel,
        out_shape=[
            jax.ShapeDtypeStruct((pieces, tokens, 3 * D), bf16),
            jax.ShapeDtypeStruct((pieces, 2 * RADIUS, 2 * D), bf16),
        ],
        grid_spec=pltpu.PrefetchScalarGridSpec(
            num_scalar_prefetch=1,
            grid=(pieces,),
            in_specs=[
                pl.BlockSpec((1, tokens, 3 * D), lambda p, e: (p, 0, 0)),
                pl.BlockSpec((1, 2 * RADIUS, 2 * D), lambda p, e: (p, 0, 0)),
                pl.BlockSpec((1, tokens, D), lambda p, e: (p, 0, 0)),
            ],
            out_specs=[
                pl.BlockSpec((1, tokens, 3 * D), lambda p, e: (p, 0, 0)),
                pl.BlockSpec((1, 2 * RADIUS, 2 * D), lambda p, e: (p, 0, 0)),
            ],
        ),
        compiler_params=pltpu.CompilerParams(vmem_limit_bytes=32 << 20),
        cost_estimate=pl.CostEstimate(
            flops=pieces * HL * tokens * 384 * 256 * 10,
            bytes_accessed=pieces * (tokens * 7 * D + 2 * RADIUS * 4 * D) * 2,
            transcendentals=pieces * HL * tokens * 384,
        ),
        name="light_attention_back",
    )(ends, own, edge, grad)


def spread_heads(value):
    tall = jnp.concatenate([value] * 4, axis=0)
    row = lax.broadcasted_iota(jnp.int32, tall.shape, 0) // QCAP
    lane = lax.broadcasted_iota(jnp.int32, tall.shape, 1) // HHD
    return jnp.where(row == lane, tall, jnp.zeros_like(tall))


def fold_heads(tall):
    lane = lax.broadcasted_iota(jnp.int32, (QCAP, 4 * HHD), 1) // HHD
    total = tall[:QCAP]
    for r in range(1, 4):
        total = jnp.where(lane == r, tall[r * QCAP : (r + 1) * QCAP], total)
    return total


def heavy_kernel(query_ref, pair_ref, live_ref, out_ref):
    factor = HHD ** (-0.5)
    keep = live_ref[0] > 0
    for group in range(HH // 4):
        lanes = slice(group * 256, (group + 1) * 256)
        query = spread_heads(query_ref[0, :, lanes])
        scores = jnp.where(keep, mm_nt(query, pair_ref[0, :, lanes]), -1e30)
        top = jnp.max(scores, axis=1, keepdims=True)
        raised = jnp.exp((scores - top) * factor)
        total = jnp.sum(raised, axis=1, keepdims=True)
        mix = mm(raised.astype(bf16), pair_ref[0, :, D + lanes.start : D + lanes.stop])
        out_ref[0, :, lanes] = fold_heads(mix * (1.0 / total)).astype(bf16)


def heavy_attention(query, pairs, live):
    pieces, slots = pairs.shape[:2]
    return pl.pallas_call(
        heavy_kernel,
        out_shape=jax.ShapeDtypeStruct((pieces, QCAP, D), bf16),
        grid=(pieces,),
        in_specs=[
            pl.BlockSpec((1, QCAP, D), lambda p: (p, 0, 0)),
            pl.BlockSpec((1, slots, 2 * D), lambda p: (p, 0, 0)),
            pl.BlockSpec((1, 1, slots), lambda p: (p, 0, 0)),
        ],
        out_specs=pl.BlockSpec((1, QCAP, D), lambda p: (p, 0, 0)),
        compiler_params=pltpu.CompilerParams(vmem_limit_bytes=32 << 20),
        cost_estimate=pl.CostEstimate(
            flops=pieces * 3 * 4 * 256 * 256 * slots,
            bytes_accessed=pieces * (slots + QCAP) * 2 * D * 2,
            transcendentals=pieces * HH * QCAP * slots,
        ),
        name="heavy_attention",
    )(query, pairs, live)


def heavy_back_kernel(query_ref, pair_ref, live_ref, grad_ref, query_out, pair_out):
    factor = HHD ** (-0.5)
    slots = pair_ref.shape[1]
    keep = jnp.broadcast_to(live_ref[0], (128, slots)).T[:, :1] > 0
    for group in range(HH // 4):
        lanes = slice(group * 256, (group + 1) * 256)
        after = slice(D + lanes.start, D + lanes.stop)
        query = spread_heads(query_ref[0, :, lanes])
        grad = spread_heads(grad_ref[0, :, lanes])
        keys = pair_ref[0, :, lanes]
        scores = jnp.where(keep, mm_nt(keys, query), -1e30)
        top = jnp.max(scores, axis=0, keepdims=True)
        raised = jnp.exp((scores - top) * factor)
        probs = raised * (1.0 / jnp.sum(raised, axis=0, keepdims=True))
        grad_probs = mm_nt(pair_ref[0, :, after], grad)
        inner = jnp.sum(probs * grad_probs, axis=0, keepdims=True)
        grad_scores = (probs * (grad_probs - inner)).astype(bf16)
        pair_out[0, :, after] = mm(probs.astype(bf16), grad).astype(bf16)
        pair_out[0, :, lanes] = (mm(grad_scores, query) * factor).astype(bf16)
        query_out[0, :, lanes] = (fold_heads(mm_tn(grad_scores, keys)) * factor).astype(bf16)


def heavy_attention_back(query, pairs, live, grad):
    pieces, slots = pairs.shape[:2]
    return pl.pallas_call(
        heavy_back_kernel,
        out_shape=[
            jax.ShapeDtypeStruct((pieces, QCAP, D), bf16),
            jax.ShapeDtypeStruct((pieces, slots, 2 * D), bf16),
        ],
        grid=(pieces,),
        in_specs=[
            pl.BlockSpec((1, QCAP, D), lambda p: (p, 0, 0)),
            pl.BlockSpec((1, slots, 2 * D), lambda p: (p, 0, 0)),
            pl.BlockSpec((1, 1, slots), lambda p: (p, 0, 0)),
            pl.BlockSpec((1, QCAP, D), lambda p: (p, 0, 0)),
        ],
        out_specs=[
            pl.BlockSpec((1, QCAP, D), lambda p: (p, 0, 0)),
            pl.BlockSpec((1, slots, 2 * D), lambda p: (p, 0, 0)),
        ],
        compiler_params=pltpu.CompilerParams(vmem_limit_bytes=32 << 20),
        cost_estimate=pl.CostEstimate(
            flops=pieces * 3 * 10 * 256 * 256 * slots,
            bytes_accessed=pieces * (2 * slots + 2 * QCAP) * 2 * D * 2,
            transcendentals=pieces * HH * QCAP * slots,
        ),
        name="heavy_attention_back",
    )(query, pairs, live, grad)


def glu_and_pull(gate, up, grad):
    slope = 0.7978845608028654
    square = gate * gate
    curve = jnp.tanh(gate * (slope + (slope * 0.044715) * square))
    half = 0.5 + 0.5 * curve
    gelu = gate * half
    bend = (0.5 * gate) * (1.0 - curve * curve) * (slope + (3 * slope * 0.044715) * square)
    return gelu * up, grad * up * (half + bend), grad * gelu


def feed_kernel(
    n_y,
    normed_in,
    cot_in,
    own_rows,
    gates_in,
    down_in,
    gates_heavy,
    down_heavy,
    act_to,
    pre_to,
    feed_to,
    grad_to,
    back_out,
    rows_to,
    heavy_act_to,
    heavy_pre_to,
    normed,
    cot,
    gates,
    down,
    act_out,
    pre_out,
    feed_out,
    grad_out,
    heavy_act_out,
    heavy_pre_out,
    wide,
    tall,
    rows,
    part,
    from_core,
    to_y,
    from_y,
    in_sem,
    out_sem,
    weight_sem,
    rows_rsem,
    rows_ssem,
    core_rsem,
    core_ssem,
    y_rsem,
    y_ssem,
):
    dp, seq = lax.axis_index("dp"), lax.axis_index("seq")
    c, y = dp % CORES, seq % n_y
    me = c * n_y + y
    to_core, to_beside = (dp + 1 - 2 * c, seq), (dp, seq + 1 - 2 * y)
    share = tall.shape[0]
    total = gates_heavy.shape[1] // 2
    inputs = [
        pltpu.make_async_copy(src, dst, in_sem.at[i])
        for i, (src, dst) in enumerate(
            (
                (own_rows, rows.at[me]),
                (gates_in, gates),
                (down_in, down),
                (normed_in, normed),
                (cot_in, cot),
            )
        )
    ]
    for load in inputs:
        load.start()
    loads = [
        pltpu.make_async_copy(
            gates_heavy.at[:, pl.ds(pl.multiple_of(i * total + me * share, share), share)],
            wide.at[i],
            weight_sem.at[i],
        )
        for i in range(2)
    ]
    loads.append(
        pltpu.make_async_copy(
            down_heavy.at[pl.ds(pl.multiple_of(me * share, share), share)], tall, weight_sem.at[2]
        )
    )
    for load in loads:
        load.start()
    barrier = pltpu.get_barrier_semaphore()
    for peer in (to_core, to_beside):
        pl.semaphore_signal(barrier, inc=1, device_id=peer, device_id_type=MESH)
    pl.semaphore_wait(barrier, 2)

    def copy(src, dst, ssem, rsem, peer):
        return pltpu.make_async_remote_copy(
            src_ref=src,
            dst_ref=dst,
            send_sem=ssem,
            recv_sem=rsem,
            device_id=peer,
            device_id_type=MESH,
        )

    def rows_copy(slot, i, peer):
        return copy(rows.at[slot], rows.at[slot], rows_ssem.at[i], rows_rsem.at[slot], peer)

    inputs[0].wait()
    rows_copy(me, 0, to_beside).start()
    rows_copy(me, 1, to_core).start()
    beside, diagonal, other = c * n_y + 1 - y, (1 - c) * n_y + 1 - y, (1 - c) * n_y + y
    hidden = down.shape[0]
    step = 256
    for load in inputs[1:]:
        load.wait()
    outputs = (
        (act_out, act_to),
        (pre_out, pre_to),
        (feed_out, feed_to),
        (grad_out, grad_to),
        (heavy_act_out, heavy_act_to),
        (heavy_pre_out, heavy_pre_to),
        (rows, rows_to),
    )

    @pl.loop(0, normed.shape[0] // step)
    def _(t):
        at = pl.ds(pl.multiple_of(t * step, step), step)
        gate = mm(normed[at], gates[:, :hidden])
        up = mm(normed[at], gates[:, hidden:])
        act, grad_gate, grad_up = glu_and_pull(gate, up, mm_nt(cot[at], down[...]))
        act = act.astype(bf16)
        grad_gate = grad_gate.astype(bf16)
        grad_up = grad_up.astype(bf16)
        act_out[at] = act
        pre_out[at, :hidden] = grad_gate
        pre_out[at, hidden:] = grad_up
        feed_out[at] = mm(act, down[...])
        grad_out[at] = mm_nt(grad_gate, gates[:, :hidden]) + mm_nt(grad_up, gates[:, hidden:])
        for i, (src, dst) in enumerate(outputs[:4]):
            pltpu.make_async_copy(src.at[at], dst.at[at], out_sem.at[i]).start()

    for load in loads:
        load.wait()
    rows_copy(beside, 2, to_core).wait_recv()
    rows_copy(beside, 2, to_core).start()

    @pl.loop(0, 4)
    def _(i):
        first, second, third = i == 0, i == 1, i == 2
        slot = jnp.where(
            first, me, jnp.where(second, diagonal, jnp.where(third, beside, other))
        )

        @pl.when(second)
        def _():
            rows_copy(diagonal, 0, to_core).wait_recv()

        @pl.when(i == 3)
        def _():
            rows_copy(other, 0, to_core).wait_recv()

        value, grad = rows[slot, 0], rows[slot, 1]
        gate, up = mm(value, wide[0]), mm(value, wide[1])
        act, grad_gate, grad_up = glu_and_pull(gate, up, mm_nt(grad, tall[...]))
        act = act.astype(bf16)
        grad_gate = grad_gate.astype(bf16)
        grad_up = grad_up.astype(bf16)
        heavy_act_out[slot] = act
        heavy_pre_out[slot, :, :share] = grad_gate
        heavy_pre_out[slot, :, share:] = grad_up
        for n, (src, dst) in enumerate(outputs[4:6]):
            pltpu.make_async_copy(src.at[slot], dst.at[slot], out_sem.at[4 + n]).start()
        part[i, 0] = mm(act, tall[...]).astype(bf16)
        part[i, 1] = (mm_nt(grad_gate, wide[0]) + mm_nt(grad_up, wide[1])).astype(bf16)

        @pl.when(second)
        def _():
            copy(part.at[1], from_core.at[0], core_ssem.at[0], core_rsem.at[0], to_core).start()

        @pl.when(third)
        def _():
            copy(part.at[1], from_core.at[0], core_ssem.at[0], core_rsem.at[0], to_core).wait_recv()
            to_y[...] = part[2] + from_core[0]
            copy(to_y, from_y, y_ssem, y_rsem, to_beside).start()

        @pl.when(i == 3)
        def _():
            copy(part.at[3], from_core.at[1], core_ssem.at[1], core_rsem.at[1], to_core).start()

    pltpu.make_async_copy(rows, rows_to, out_sem.at[6]).start()
    copy(part.at[3], from_core.at[1], core_ssem.at[1], core_rsem.at[1], to_core).wait()
    copy(to_y, from_y, y_ssem, y_rsem, to_beside).wait()
    sums = part[0].astype(f32) + from_core[1].astype(f32) + from_y[...].astype(f32)
    back_out[...] = sums.astype(bf16)
    copy(part.at[1], from_core.at[0], core_ssem.at[0], core_rsem.at[0], to_core).wait_send()
    for i, slot in enumerate((me, me, beside)):
        rows_copy(slot, i, to_core).wait_send()
    for i, (src, dst) in enumerate(outputs):
        pltpu.make_async_copy(src, dst, out_sem.at[i]).wait()


def feed_forward(normed, cot, own_rows, gates, down, gates_heavy, down_heavy, n_y):
    count, hidden = normed.shape[0], down.shape[0]
    slots = own_rows.shape[1]
    share = down_heavy.shape[0] // 4
    here, anywhere = pl.BlockSpec(memory_space=pltpu.VMEM), pl.BlockSpec(memory_space=pl.ANY)
    pair = (2, slots, D)
    return pl.pallas_call(
        functools.partial(feed_kernel, n_y),
        out_shape=[
            jax.ShapeDtypeStruct((count, hidden), bf16),
            jax.ShapeDtypeStruct((count, 2 * hidden), bf16),
            jax.ShapeDtypeStruct((count, D), f32),
            jax.ShapeDtypeStruct((count, D), f32),
            jax.ShapeDtypeStruct(pair, bf16),
            jax.ShapeDtypeStruct((4,) + pair, bf16),
            jax.ShapeDtypeStruct((4, slots, share), bf16),
            jax.ShapeDtypeStruct((4, slots, 2 * share), bf16),
        ],
        in_specs=[anywhere] * 7,
        out_specs=[anywhere] * 4 + [here] + [anywhere] * 3,
        scratch_shapes=[
            pltpu.VMEM((count, D), bf16),
            pltpu.VMEM((count, D), bf16),
            pltpu.VMEM((D, 2 * hidden), bf16),
            pltpu.VMEM((hidden, D), bf16),
            pltpu.VMEM((count, hidden), bf16),
            pltpu.VMEM((count, 2 * hidden), bf16),
            pltpu.VMEM((count, D), f32),
            pltpu.VMEM((count, D), f32),
            pltpu.VMEM((4, slots, share), bf16),
            pltpu.VMEM((4, slots, 2 * share), bf16),
            pltpu.VMEM((2, D, share), bf16),
            pltpu.VMEM((share, D), bf16),
            pltpu.VMEM((4,) + pair, bf16),
            pltpu.VMEM((4,) + pair, bf16),
            pltpu.VMEM((2,) + pair, bf16),
            pltpu.VMEM(pair, bf16),
            pltpu.VMEM(pair, bf16),
            pltpu.SemaphoreType.DMA((5,)),
            pltpu.SemaphoreType.DMA((7,)),
            pltpu.SemaphoreType.DMA((3,)),
            pltpu.SemaphoreType.DMA((4,)),
            pltpu.SemaphoreType.DMA((3,)),
            pltpu.SemaphoreType.DMA((2,)),
            pltpu.SemaphoreType.DMA((2,)),
            pltpu.SemaphoreType.DMA,
            pltpu.SemaphoreType.DMA,
        ],
        compiler_params=pltpu.CompilerParams(
            collective_id=2, has_side_effects=True, vmem_limit_bytes=60 << 20
        ),
        cost_estimate=pl.CostEstimate(
            flops=12 * count * D * hidden + 48 * slots * D * share,
            bytes_accessed=30 << 20,
            transcendentals=count * hidden + 4 * slots * share,
        ),
        name="feed_forward",
    )(normed, cot, own_rows, gates, down, gates_heavy, down_heavy)


def reduce_kernel(jobs, counts, n_y, *refs):
    n_sources, n_outs, light, factors = counts
    refs = list(refs)

    def take(count):
        taken = refs[:count]
        del refs[:count]
        return taken

    sources = take(n_sources)
    given = take(4 if light else factors)
    outs = take(n_outs)
    made = take(3 if light else 0)
    held = []
    for job in jobs:
        names = SCRATCH[job[0]] + (("full",) if len(job) > 7 else ())
        held.append(dict(zip(names, take(len(names)))))
    kinds = [job[0] for job in jobs]
    dp, seq = lax.axis_index("dp"), lax.axis_index("seq")
    x, c = dp // CORES, dp % CORES
    z, y = seq // n_y, seq % n_y
    z_high, z_low = z // 2, z % 2
    group = c * n_y + y

    def device(x=x, c=c, z=z, y=y):
        return (x * CORES + c, z * n_y + y)

    to = {
        "core": device(c=1 - c),
        "x": device(x=1 - x),
        "y": device(y=1 - y),
        "low": device(z=z_high * 2 + 1 - z_low),
        "high": device(z=(1 - z_high) * 2 + z_low),
    }
    owner = (group, x * DEPTH + z)
    origin = device(x=seq // DEPTH, c=dp // n_y, z=seq % DEPTH, y=dp % n_y)
    moved = jnp.logical_or(owner[0] != dp, owner[1] != seq)

    barrier = pltpu.get_barrier_semaphore()

    def greet(peer):
        pl.semaphore_signal(barrier, inc=1, device_id=peer, device_id_type=MESH)

    for peer in to.values():
        greet(peer)
    expected = len(to)
    if "gates" in kinds:
        greet(device(c=1 - c, y=1 - y))
        expected += 1
    pairs = []
    if "down" in kinds:
        pairs += [(moved, owner), (moved, origin)]
    if light:
        pairs += [(seq > 0, (dp, seq - 1)), (seq < DEPTH * n_y - 1, (dp, seq + 1))]
    for present, peer in pairs:

        @pl.when(present)
        def _():
            greet(peer)

    for present, _ in pairs:
        expected = expected + jnp.where(present, 1, 0)
    pl.semaphore_wait(barrier, expected)

    def copy(src, dst, a, stage, k, peer):
        return pltpu.make_async_remote_copy(
            src_ref=src,
            dst_ref=dst,
            send_sem=held[a]["ssem"].at[stage],
            recv_sem=held[a]["rsem"].at[stage, k],
            device_id=peer,
            device_id_type=MESH,
        )

    def send(src, name, k, a, place=None, slot=None):
        dst = held[a][name].at[k] if slot is None else held[a][name].at[k, slot]
        copy(src, dst, a, STAGES[name], k, place).start()

    def arrived(name, a, k):
        buffer = held[a][name].at[k]
        copy(buffer, buffer, a, STAGES[name], k, to["core"]).wait_recv()

    def columns(a, k):
        start, width = jobs[a][2:4]
        return pl.ds(start + k * width, width)

    if factors:
        *kept, factor_sem = refs
        wanted, fetched = [], set()
        for a, job in enumerate(jobs):
            for left, right, start in job[7:]:
                for k in range(job[4]):
                    wanted.append((k, a, left, right, pl.ds(start + k * job[3], job[3])))
        fetches = {}
        for k, a, left, right, cols in sorted(wanted, key=lambda w: w[:2]):
            for key, part in (((left,), slice(None)), ((right, cols.start), cols)):
                if key not in fetches:
                    src, dst = given[key[0]].at[:, part], kept[key[0]].at[:, part]
                    fetches[key] = pltpu.make_async_copy(src, dst, factor_sem.at[len(fetches)])
                    fetches[key].start()

    def produce(a, k):
        width, height = jobs[a][3], held[a]["full"].shape[-2]
        total = 0.0
        for left, right, start in jobs[a][7:]:
            for key in ((left,), (right, start + k * width)):
                if key not in fetched:
                    fetched.add(key)
                    fetches[key].wait()
            cols = slice(start + k * width, start + (k + 1) * width)
            total = total + mm_tn(kept[left][...], kept[right][:, cols])
        at = 0
        for i in range(2):
            for j in range(CORES):
                for m in range(DEPTH):
                    for n in range(n_y):
                        rows = total[at * height : (at + 1) * height]
                        held[a]["full"][k, i, j, m, n] = rows.astype(bf16)
                        at += 1

    def local(a, k):
        whole, cols = sources[jobs[a][1]], columns(a, k)
        if kinds[a] in ("xy", "yx"):
            part = whole.at[:, c, :, :, :, cols]
        else:
            part = whole.at[x, :, :, :, :, cols]
        return pltpu.make_async_copy(part, held[a]["own"].at[k], held[a]["lsem"].at[k])

    def begin(a, k):
        if len(jobs[a]) > 7:
            produce(a, k)
            send(held[a]["full"].at[k, :, 1 - c], "core", k, a, to["core"])
            return
        whole, cols = sources[jobs[a][1]], columns(a, k)
        local(a, k).start()
        if kinds[a] in ("xy", "yx"):
            send(whole.at[:, 1 - c, :, :, :, cols], "core", k, a, to["core"])
        else:
            send(whole.at[1 - x, :, :, :, :, cols], "xx", k, a, to["x"])

    def first(a, k):
        h, kind = held[a], kinds[a]
        own = h["own"]
        made_here = "full" in h
        if not made_here:
            local(a, k).wait()
        if kind not in ("xy", "yx"):
            return
        arrived("core", a, k)

        @pl.loop(0, 2 * DEPTH)
        def _(i):
            for j in range(n_y):
                at = (k, i // DEPTH, i % DEPTH, j)
                mine = h["full"][at[:2] + (c,) + at[2:]] if made_here else own[at]
                own[at] = mine + h["core"][at]

        if kind == "xy":
            send(own.at[k, 1 - x], "xx", k, a, to["x"])
        else:
            send(own.at[k, :, :, 1 - y], "yy", k, a, to["y"])

    def second(a, k):
        h, kind = held[a], kinds[a]
        own = h["own"]
        if kind == "xy":
            arrived("xx", a, k)

            @pl.loop(0, DEPTH)
            def _(i):
                for j in range(n_y):
                    at = (k, x, i, j)
                    own[at] = own[at] + h["xx"][k, i, j]

            send(own.at[k, x, :, 1 - y], "yy", k, a, to["y"])
        elif kind == "yx":
            arrived("yy", a, k)

            @pl.loop(0, DEPTH)
            def _(i):
                for j in range(2):
                    at = (k, j, i, y)
                    own[at] = own[at] + h["yy"][k, j, i]

            send(own.at[k, 1 - x, :, y], "xx", k, a, to["x"])

    def third(a, k):
        h, kind = held[a], kinds[a]
        own = h["own"]
        if kind in ("xy", "yx"):
            name = "yy" if kind == "xy" else "xx"
            arrived(name, a, k)

            @pl.loop(0, DEPTH)
            def _(i):
                at = (k, x, i, y)
                own[at] = own[at] + h[name][k, i]

            for high in range(2):
                send(own.at[k, x, high * 2 + 1 - z_low, y], "za", k, a, to["low"], high)
        else:
            arrived("xx", a, k)

            @pl.loop(0, DEPTH)
            def _(i):
                for g in range(own.shape[1]):
                    for j in range(own.shape[3]):
                        at = (k, g, i, j)
                        own[at] = own[at] + h["xx"][at]

            for high in range(2):
                send(own.at[k, :, high * 2 + 1 - z_low], "za", k, a, to["low"], high)

    def fourth(a, k):
        h, kind = held[a], kinds[a]
        own = h["own"]
        arrived("za", a, k)
        if kind in ("xy", "yx"):
            for high in range(2):
                at = (k, x, high * 2 + z_low, y)
                own[at] = own[at] + h["za"][k, high]
            send(own.at[k, x, (1 - z_high) * 2 + z_low, y], "zb", k, a, to["high"])
        else:

            @pl.loop(0, own.shape[1])
            def _(g):
                for j in range(own.shape[3]):
                    for high in range(2):
                        at = (k, g, high * 2 + z_low, j)
                        own[at] = own[at] + h["za"][k, high, g, j]

            send(own.at[k, :, (1 - z_high) * 2 + z_low], "zb", k, a, to["high"])

    def fifth(a, k):
        h = held[a]
        kind, _, _, width, _, out, start = jobs[a][:7]
        own = h["own"]
        arrived("zb", a, k)
        if kind in ("xy", "yx"):
            total = own[k, x, z, y].astype(f32) + h["zb"][k].astype(f32)
            outs[out][:, start + k * width : start + (k + 1) * width] = total
        elif kind == "down":
            h["sum"][k] = own[k, 0, z, 0] + h["zb"][k, 0, 0]

            @pl.when(moved)
            def _():
                send(h["sum"].at[k], "dd", k, a, owner)

            @pl.when(jnp.logical_not(moved))
            def _():
                h["dd"][k] = h["sum"][k]
        else:

            @pl.loop(0, CORES)
            def _(g):
                for j in range(n_y):
                    h["sum"][k, g * n_y + j] = own[k, g, z, j] + h["zb"][k, g, j]

            h["dd"][k, group] = h["sum"][k, group]
            for g, j in ((1 - c, y), (c, 1 - y), (1 - c, 1 - y)):
                send(h["sum"].at[k, g * n_y + j], "dd", k, a, device(c=g, y=j), group)

    def last(a, k):
        h = held[a]
        kind, _, _, width, chunks, out, start = jobs[a][:7]
        if kind == "gates":
            part = h["dd"].at[k, pl.ds(0, 3)]
            copy(part, part, a, STAGES["dd"], k, to["core"]).wait_recv()
            for g in range(4):
                at = start + (g * chunks + k) * width
                outs[out][:, at : at + width] = h["dd"][k, g].astype(f32)
        elif kind == "down":

            @pl.when(moved)
            def _():
                arrived("dd", a, k)

            outs[out][:, start + k * width : start + (k + 1) * width] = h["dd"][k].astype(f32)

    lists = {"all": [], "rest": []}
    for a, job in enumerate(jobs):
        lists["all" if job[0] in ("xy", "yx") else "rest"].append([(a, k) for k in range(job[4])])
    stages = (begin, first, second, third, fourth, fifth, last)
    longest = max(len(interleave(parts)) for parts in lists.values())
    events = []
    for name, parts in lists.items():
        order = interleave(parts)
        for i, what in enumerate(order):
            for stage, lag in zip(stages, LAGS[name]):
                events.append((i * longest / len(order) + lag, len(events), stage, what))
    if light:
        edges_in = made[2]
        *inner, weights, ready, landed, load_sem, weight_sem, out_sem, edge_ssem, edge_rsem = refs
        edge_out = inner[4]
        pieces = edge_out.shape[0]
        reach = (seq > 0, seq < DEPTH * n_y - 1)

        def load(i, p):
            return pltpu.make_async_copy(given[i].at[p], inner[i].at[p], load_sem.at[i, p])

        def store(i, p):
            src, dst = inner[3 + i], made[i]
            if p is not None:
                src, dst = src.at[p], dst.at[p]
            return pltpu.make_async_copy(src, dst, out_sem.at[i])

        for p in range(pieces):
            for i in range(3):
                load(i, p).start()
        load_weights = pltpu.make_async_copy(given[3], weights, weight_sem)
        load_weights.start()

        def edge_copy(side, p):
            src = ready.at[p, pl.ds(side * RADIUS, RADIUS)]
            dst = landed.at[p, pl.ds((1 - side) * RADIUS, RADIUS)]
            return pltpu.make_async_remote_copy(
                src_ref=src,
                dst_ref=dst,
                send_sem=edge_ssem.at[side],
                recv_sem=edge_rsem.at[1 - side, p],
                device_id=(dp, seq - 1 + 2 * side),
                device_id_type=MESH,
            )

        def unit(p, g):
            if g == 0:
                for i in range(3):
                    load(i, p).wait()
            light_back_unit(reach, (g,), *[ref.at[pl.ds(p, 1)] for ref in inner])
            if g == 1:
                for i in range(2):
                    store(i, p).start()
                if p == 0:
                    load_weights.wait()
                rows = mm_nt(edge_out[p], weights[:, D:])
                ready[p] = rows.astype(bf16)
                for side in range(2):

                    @pl.when(reach[side])
                    def _():
                        edge_copy(side, p).start()

        for p in range(pieces):
            for g in range(2):
                events.append(((2 * p + g) * 1.2, len(events), unit, (p, g)))
    for _, _, stage, what in sorted(events, key=lambda e: e[:2]):
        stage(*what)

    if light:
        for i in range(2):
            store(i, None).wait()
        for side in range(2):
            rows = pl.ds(side * RADIUS, RADIUS)

            @pl.when(reach[side])
            def _():
                for p in range(pieces):
                    edge_copy(1 - side, p).wait_recv()
                    edges_in[p, rows] = landed[p, rows]
                whole = ready.at[:, rows]
                pltpu.make_async_remote_copy(
                    src_ref=whole,
                    dst_ref=whole,
                    send_sem=edge_ssem.at[side],
                    recv_sem=edge_rsem.at[side, 0],
                    device_id=(dp, seq - 1 + 2 * side),
                    device_id_type=MESH,
                ).wait_send()

            @pl.when(jnp.logical_not(reach[side]))
            def _():
                for p in range(pieces):
                    edges_in[p, rows] = jnp.zeros((RADIUS, D), bf16)

    for a, kind in enumerate(kinds):
        h = held[a]
        for name in ("core", "xx", "yy", "za", "zb"):
            if name in h:
                copy(h[name], h[name], a, STAGES[name], 0, to["core"]).wait_send()
        if kind == "gates":
            part = h["dd"].at[:, pl.ds(0, 3)]
            copy(part, part, a, STAGES["dd"], 0, to["core"]).wait_send()
        elif kind == "down":

            @pl.when(moved)
            def _():
                copy(h["dd"], h["dd"], a, STAGES["dd"], 0, to["core"]).wait_send()


def interleave(parts):
    keyed = [((i + 0.5) / len(p), n, v) for n, p in enumerate(parts) for i, v in enumerate(p)]
    return [v for _, _, v in sorted(keyed)]


LAGS = {"all": (-4, 0, 2, 4, 6, 8, 8), "rest": (-2, -1, -1, 1.5, 3.5, 5.5, 8)}
STAGES = {"core": 0, "xx": 1, "yy": 2, "za": 3, "zb": 4, "dd": 5}
SCRATCH = {
    "xy": ("own", "core", "xx", "yy", "za", "zb", "lsem", "rsem", "ssem"),
    "yx": ("own", "core", "xx", "yy", "za", "zb", "lsem", "rsem", "ssem"),
    "gates": ("own", "xx", "za", "zb", "sum", "dd", "lsem", "rsem", "ssem"),
    "down": ("own", "xx", "za", "zb", "sum", "dd", "lsem", "rsem", "ssem"),
}


def reduce_all(values, jobs, widths, n_y, collective_id, light=(), factors=()):
    operands, scratch = [], []
    for value, inner in values:
        height, columns = value.shape
        lead = (2, CORES, DEPTH, n_y) if inner else (2, 1, DEPTH, 1)
        operands.append(value.reshape(lead + (height // math.prod(lead), columns)))
    heights = {job[5]: D // (8 * DEPTH) if len(job) > 7 else operands[job[1]].shape[4] for job in jobs}
    out_shape = [jax.ShapeDtypeStruct((heights[o], w), f32) for o, w in enumerate(widths)]
    for kind, source, _, width, k, out, *rest in jobs:
        _, inner, _, outer = operands[source].shape[:4]
        height = heights[out]
        if kind == "xy":
            shapes = [(2, DEPTH, n_y)] * 2 + [(DEPTH, n_y), (DEPTH,), (2,), ()]
        elif kind == "yx":
            shapes = [(2, DEPTH, n_y)] * 2 + [(DEPTH,), (2, DEPTH), (2,), ()]
        else:
            both = (inner, outer)
            shapes = [(inner, DEPTH, outer)] * 2 + [(2,) + both, both]
            shapes += [(4,), (4,)] if kind == "gates" else [(), ()]
        scratch += [pltpu.VMEM((k,) + shape + (height, width), bf16) for shape in shapes]
        scratch += [
            pltpu.SemaphoreType.DMA((k,)),
            pltpu.SemaphoreType.DMA((6, k)),
            pltpu.SemaphoreType.DMA((6,)),
        ]
        if len(rest) > 1:
            scratch.append(pltpu.VMEM((k, 2, CORES, DEPTH, n_y, height, width), bf16))
    if light:
        pieces, edge_rows = light[1].shape[:2]
        out_shape += [jax.ShapeDtypeStruct(v.shape, bf16) for v in light[:2]]
        out_shape.append(jax.ShapeDtypeStruct((pieces, edge_rows, D), bf16))
        own, edge, grad, weights = light
        scratch += [pltpu.VMEM(v.shape, bf16) for v in (own, edge, grad, own, edge, weights)]
        scratch += [pltpu.VMEM((pieces, edge_rows, D), bf16)] * 2
        scratch += [pltpu.SemaphoreType.DMA((3, pieces)), pltpu.SemaphoreType.DMA]
        scratch += [pltpu.SemaphoreType.DMA((2,))] * 2 + [pltpu.SemaphoreType.DMA((2, pieces))]
    if factors:
        scratch += [pltpu.VMEM(v.shape, bf16) for v in factors]
        scratch.append(pltpu.SemaphoreType.DMA((32,)))
    total = 16 * n_y * sum(math.prod(shape.shape) for shape in out_shape[: len(widths)])
    here, anywhere = pl.BlockSpec(memory_space=pltpu.VMEM), pl.BlockSpec(memory_space=pl.ANY)
    out_specs = [here] * len(widths) + ([anywhere] * 2 + [here] if light else [])
    return pl.pallas_call(
        functools.partial(
            reduce_kernel,
            tuple(jobs),
            (len(values), len(widths), bool(light), len(factors)),
            n_y,
        ),
        out_shape=out_shape,
        in_specs=[anywhere] * len([*values, *light, *factors]),
        out_specs=out_specs,
        scratch_shapes=scratch,
        compiler_params=pltpu.CompilerParams(
            collective_id=collective_id, has_side_effects=True, vmem_limit_bytes=60 << 20
        ),
        cost_estimate=pl.CostEstimate(
            flops=2 * total, bytes_accessed=32 * total, transcendentals=0
        ),
        name="reduce_gradients",
    )(*operands, *light, *factors)


def copy_kernel(*refs):
    count = len(refs) // 2
    for i in range(count):
        refs[count + i][...] = refs[i][...]


def copy_all(values):
    count = len(values)
    return pl.pallas_call(
        copy_kernel,
        out_shape=[jax.ShapeDtypeStruct(v.shape, v.dtype) for v in values],
        in_specs=[pl.BlockSpec(memory_space=pltpu.VMEM)] * count,
        out_specs=[pl.BlockSpec(memory_space=pltpu.VMEM)] * count,
        name="copy_outputs",
    )(*values)


def per_device(
    layer_input,
    cotangent,
    first_gain,
    light_inputs,
    light_output,
    heavy_queries,
    heavy_keyvalue,
    heavy_output,
    second_gain,
    router,
    light_gates,
    light_down,
    heavy_gates,
    heavy_down,
    query_index,
    query_count,
    key_index,
    key_count,
    feed_slot,
):
    pieces, tokens = layer_input.shape[:2]
    rows = pieces * tokens
    n_dp, n_seq = lax.axis_size("dp"), lax.axis_size("seq")
    n_x, n_y = n_dp // CORES, n_seq // DEPTH
    seq_rank = lax.axis_index("seq")
    core = Ring("dp", 1, CORES)
    ring_x = Ring("dp", CORES, n_x)
    ring_y = Ring("seq", 1, n_y)
    ring_z = Ring("seq", n_y, DEPTH)
    capacity = max(2, 3 * rows // (16 * n_seq))
    slots = n_seq * capacity
    each = D // (n_dp * n_seq)
    kernels = each % 8 == 0 and n_x == n_y == 2

    def reduce_grad(value, first, second):
        height, width = value.shape
        chunk = height // (n_dp * n_seq)
        parts = value.reshape(n_x, CORES, DEPTH, n_y, chunk, width)
        parts = core.scatter_sum(parts, 1).astype(bf16)
        dims = ["x", "z", "y"]
        rings = {"x": ring_x, "y": ring_y, "z": ring_z}
        order = [first, second, [d for d in dims if d not in (first, second)][0]]
        for i, d in enumerate(order):
            at = dims.index(d)
            parts = rings[d].scatter_sum(parts, at)
            if i < 2:
                parts = parts.astype(bf16)
            dims.remove(d)
        return parts

    def reduce_split(value):
        half = value.shape[1] // 2
        return jnp.concatenate(
            [
                reduce_grad(value[:, :half], "x", "y"),
                reduce_grad(value[:, half:], "y", "x"),
            ],
            axis=1,
        )

    def reduce_vectors(value):
        count, width = value.shape
        chunk = width // (n_dp * n_seq)
        parts = value.reshape(count, n_x, CORES, DEPTH, n_y, chunk)
        parts = core.scatter_sum(parts, 2)
        parts = ring_x.scatter_sum(parts, 1)
        parts = ring_z.scatter_sum(parts, 1)
        return ring_y.scatter_sum(parts, 1)

    ends = n_seq - 1
    left_rows = lax.ppermute(
        layer_input[:, tokens - RADIUS :], "seq", [(i, i + 1) for i in range(ends)]
    )
    right_rows = lax.ppermute(layer_input[:, :RADIUS], "seq", [(i + 1, i) for i in range(ends)])
    position = jnp.arange(tokens, dtype=jnp.int32)
    key_pick = (key_index[:, :, None] == position[None, None, :]).astype(bf16)
    query_live = jnp.arange(QCAP, dtype=jnp.int32)[None, :] < query_count
    query_pick = (query_index[:, :, None] == position[None, None, :]).astype(bf16)
    live_pick = query_pick * query_live[:, :, None].astype(bf16)
    key_raw = jnp.einsum("pkt,ptd->pkd", key_pick, layer_input, preferred_element_type=f32).astype(
        bf16
    )
    key_all = lax.all_gather(key_raw, "seq", axis=1, tiled=True)

    gain_first = first_gain.astype(f32)
    inputs = layer_input.astype(f32)
    unit_first, scale_first = norm_parts(inputs)
    normed_first = (unit_first * gain_first).astype(bf16)
    normed_flat = normed_first.reshape(rows, D)
    own_proj = mm(normed_flat, light_inputs).astype(bf16).reshape(pieces, tokens, 3 * D)
    edge_rows = jnp.concatenate([left_rows, right_rows], axis=1)
    normed_edge = (norm_parts(edge_rows.astype(f32))[0] * gain_first).astype(bf16)
    edge_flat = normed_edge.reshape(pieces * 2 * RADIUS, D)
    edge_proj = mm(edge_flat, light_inputs[:, D:]).astype(bf16)
    edge_proj = edge_proj.reshape(pieces, 2 * RADIUS, 2 * D)

    reach = jnp.stack([seq_rank > 0, seq_rank < n_seq - 1]).astype(jnp.int32)
    light_att = light_attention(reach, own_proj, edge_proj).reshape(rows, D)

    key_slots = n_seq * KCAP
    key_rows_all = key_all.reshape(pieces * key_slots, D)
    normed_keys = (norm_parts(key_rows_all.astype(f32))[0] * gain_first).astype(bf16)
    heavy_pairs = mm(normed_keys, heavy_keyvalue).astype(bf16).reshape(pieces, key_slots, 2 * D)
    key_live = jnp.arange(KCAP, dtype=jnp.int32)[None, None, :] < key_count[:, :, None]
    key_live = key_live.reshape(pieces, 1, key_slots).astype(f32)
    query_rows = (
        jnp.einsum("pqt,ptd->pqd", query_pick, normed_first, preferred_element_type=f32)
        .astype(bf16)
        .reshape(pieces * QCAP, D)
    )
    heavy_query = mm(query_rows, heavy_queries).astype(bf16).reshape(pieces, QCAP, D)
    heavy_att = heavy_attention(heavy_query, heavy_pairs, key_live)
    heavy_spread = (
        jnp.einsum("pqt,pqd->ptd", live_pick, heavy_att, preferred_element_type=f32)
        .astype(bf16)
        .reshape(rows, D)
    )

    middle = (
        inputs.reshape(rows, D) + mm(light_att, light_output) + mm(heavy_spread, heavy_output)
    )
    gain_second = second_gain.astype(f32)
    unit_second, scale_second = norm_parts(middle)
    normed_second = (unit_second * gain_second).astype(bf16)

    slot_of = feed_slot.reshape(1, rows)
    pick = (jnp.arange(slots, dtype=jnp.int32)[:, None] == slot_of).astype(bf16)
    routed = feed_slot.reshape(rows, 1) >= 0
    cot = cotangent.reshape(rows, D)
    gating = jax.nn.sigmoid(
        jnp.sum(normed_second.astype(f32) * router.astype(f32), axis=-1, keepdims=True)
    )
    grad_token = (gating * cot.astype(f32)).astype(bf16)
    feed_in = mm(pick, normed_second).astype(bf16)
    grad_in = mm(pick, grad_token).astype(bf16)

    wide = heavy_gates.shape[1] // 2
    share = wide // 4
    if kernels:
        light_act, grad_light_pre, light_feed, grad_light, back, feed_all, heavy_act, heavy_pre = (
            feed_forward(
                normed_second,
                cot,
                jnp.stack([feed_in, grad_in]),
                light_gates,
                light_down,
                heavy_gates,
                heavy_down,
                n_y,
            )
        )
        feed_rows = feed_all[:, 0].reshape(4 * slots, D)
        grad_rows = feed_all[:, 1].reshape(4 * slots, D)
        heavy_act = heavy_act.reshape(4 * slots, share)
        heavy_pre = heavy_pre.reshape(4 * slots, 2 * share)
        heavy_result, grad_feed_in = back[0], back[1]
    else:
        feed_rows, grad_rows = feed_in, grad_in
        hidden = light_down.shape[0]
        pre = mm(normed_second, light_gates)
        light_act, *grads = glu_and_pull(pre[:, :hidden], pre[:, hidden:], mm_nt(cot, light_down))
        light_act = light_act.astype(bf16)
        grad_light_pre = jnp.concatenate(grads, axis=1).astype(bf16)
        light_feed = mm(light_act, light_down)
        grad_light = mm_nt(grad_light_pre, light_gates)
        pre = mm(feed_in, heavy_gates)
        heavy_act, *grads = glu_and_pull(pre[:, :wide], pre[:, wide:], mm_nt(grad_in, heavy_down))
        heavy_act = heavy_act.astype(bf16)
        heavy_pre = jnp.concatenate(grads, axis=1).astype(bf16)
        heavy_result = mm(heavy_act, heavy_down).astype(bf16)
        grad_feed_in = mm_nt(heavy_pre, heavy_gates).astype(bf16)
    heavy_down_grad = mm_tn(heavy_act, grad_rows).astype(bf16)
    heavy_gates_grad = mm_tn(feed_rows, heavy_pre).astype(bf16)
    light_down_grad = mm_tn(light_act, cot).astype(bf16)
    light_gates_grad = mm_tn(normed_second, grad_light_pre).astype(bf16)

    token_result = mm_tn(pick, heavy_result)
    output = (middle + light_feed + gating * token_result).astype(bf16).reshape(layer_input.shape)
    grad_gating = jnp.sum(cot.astype(f32) * token_result, axis=-1, keepdims=True)
    grad_logit = grad_gating * gating * (1.0 - gating)
    grad_second = (
        grad_light
        + mm_tn(pick, grad_feed_in)
        + grad_logit * router.astype(f32)
    )
    router_grad = jnp.sum(grad_logit * normed_second.astype(f32), axis=0)
    second_gain_grad = jnp.sum(grad_second * unit_second, axis=0)
    grad_middle = cot.astype(f32) + norm_pull(grad_second, middle, scale_second, gain_second)
    grad_mid_low = grad_middle.astype(bf16)

    light_output_grad = mm_tn(light_att, grad_mid_low).astype(bf16)
    grad_light_att = mm_nt(grad_mid_low, light_output).astype(bf16)
    grad_query_rows = (
        jnp.einsum(
            "pqt,ptd->pqd",
            live_pick,
            grad_mid_low.reshape(pieces, tokens, D),
            preferred_element_type=f32,
        )
        .astype(bf16)
        .reshape(pieces * QCAP, D)
    )
    heavy_output_grad = mm_tn(heavy_att.reshape(pieces * QCAP, D), grad_query_rows).astype(bf16)
    grad_heavy_att = mm_nt(grad_query_rows, heavy_output).astype(bf16)

    grad_hq_low, grad_hkv_low = heavy_attention_back(
        heavy_query,
        heavy_pairs,
        key_live,
        grad_heavy_att.reshape(pieces, QCAP, D),
    )
    grad_hq_low = grad_hq_low.reshape(pieces * QCAP, D)
    grad_hkv_low = grad_hkv_low.reshape(pieces * key_slots, 2 * D)
    grad_key_rows = mm_nt(grad_hkv_low, heavy_keyvalue).astype(bf16)
    heavy_keyvalue_grad = mm_tn(normed_keys, grad_hkv_low).astype(bf16)
    heavy_queries_grad = mm_tn(query_rows, grad_hq_low).astype(bf16)

    grad_light_att, grad_key_rows = lax.optimization_barrier((grad_light_att, grad_key_rows))
    grad_key_own = lax.psum_scatter(
        grad_key_rows.reshape(pieces, key_slots, D), "seq", scatter_dimension=1, tiled=True
    )
    grad_light_att = grad_light_att.reshape(pieces, tokens, D)
    if kernels:
        early = [
            (light_gates_grad, True),
            (light_down_grad, True),
            (light_output_grad, True),
            (heavy_output_grad, True),
            (heavy_gates_grad, True),
            (heavy_down_grad, False),
            (heavy_queries_grad, True),
            (heavy_keyvalue_grad, True),
        ]
        half = light_gates_grad.shape[1] // 2
        jobs = [
            ("xy", 0, 0, 512, half // 512, 0, 0),
            ("yx", 0, half, 512, half // 512, 0, half),
            ("yx", 1, 0, 384, D // 384, 1, 0),
            ("xy", 2, 0, 384, D // 384, 2, 0),
            ("yx", 3, 0, 384, D // 384, 3, 0),
            ("gates", 4, 0, 256, share // 256, 4, 0),
            ("gates", 4, share, 256, share // 256, 4, wide),
            ("down", 5, 0, 128, D // 128, 5, 0),
            ("xy", 6, 0, 384, 2, 6, 0),
            ("xy", 7, 0, 512, 3, 7, 0),
        ]
        widths = (2 * half, D, D, D, 2 * wide, D, D, 2 * D)
        *early, grad_own, grad_edge, grad_around = reduce_all(
            early, jobs, widths, n_y, 0, (own_proj, edge_proj, grad_light_att, light_inputs)
        )
    else:
        grad_own, grad_edge = light_attention_back(reach, own_proj, edge_proj, grad_light_att)
        early = [light_gates_grad, light_down_grad, light_output_grad, heavy_output_grad]
        early += [heavy_gates_grad, heavy_down_grad]
        early = [reduce_split(v) for v in early]
        grad_edge_rows = mm_nt(grad_edge.reshape(-1, 2 * D), light_inputs[:, D:]).astype(bf16)
        grad_edge_rows = grad_edge_rows.reshape(pieces, 2 * RADIUS, D)
        from_right = lax.ppermute(
            grad_edge_rows[:, :RADIUS], "seq", [(i + 1, i) for i in range(ends)]
        )
        from_left = lax.ppermute(
            grad_edge_rows[:, RADIUS:], "seq", [(i, i + 1) for i in range(ends)]
        )
        grad_around = jnp.concatenate([from_left, from_right], axis=1)
    grad_own = grad_own.reshape(rows, 3 * D)
    grad_edge = grad_edge.reshape(pieces * 2 * RADIUS, 2 * D)
    grad_hq_rows = mm_nt(grad_hq_low, heavy_queries).astype(bf16).reshape(pieces, QCAP, D)
    grad_first = mm_nt(grad_own, light_inputs).reshape(pieces, tokens, D)
    grad_slots = jnp.concatenate([grad_hq_rows, grad_key_own.astype(bf16)], axis=1)
    both_pick = jnp.concatenate([query_pick, key_pick], axis=1)
    grad_first = (
        grad_first
        + jnp.einsum("pkt,pkd->ptd", both_pick, grad_slots, preferred_element_type=f32)
        + grad_around.astype(f32)
    )
    first_gain_grad = jnp.sum(grad_first * unit_first, axis=(0, 1))
    input_grad = grad_middle.reshape(pieces, tokens, D) + norm_pull(
        grad_first, inputs, scale_first, gain_first
    )
    vectors = jnp.stack([first_gain_grad, second_gain_grad, router_grad])
    devices = n_dp * n_seq
    if kernels:
        lines = vectors.reshape(3, devices, each).transpose(1, 0, 2)
        lines = jnp.pad(lines, ((0, 0), (0, 5), (0, 256 - each))).reshape(devices * 8, 256)
        jobs = (
            ("xy", 0, 0, 384, 1, 0, 0, (0, 2, 0)),
            ("yx", 0, 384, 384, 1, 0, 384, (0, 2, 384)),
            ("xy", 0, D, 384, 2, 0, D, (0, 2, D), (1, 3, 0)),
            ("yx", 0, 2 * D, 384, 2, 0, 2 * D, (0, 2, 2 * D), (1, 3, D)),
            ("xy", 0, 0, 256, 1, 1, 0),
        )
        factors = (normed_flat, edge_flat, grad_own, grad_edge)
        late = [(lines.astype(bf16), True)]
        light_inputs_grad, lines = reduce_all(
            late, jobs, (3 * D, 256), n_y, 1, (), factors
        )
        *early, light_inputs_grad, lines = copy_all([*early, light_inputs_grad, lines])
        late = [light_inputs_grad, *early[6:]]
        vectors = lines[:3, :each]
    else:
        light_pair_grad = mm_tn(normed_flat, grad_own[:, D:]) + mm_tn(edge_flat, grad_edge)
        late = [
            jnp.concatenate([mm_tn(normed_flat, grad_own[:, :D]), light_pair_grad], axis=1),
            heavy_queries_grad,
            heavy_keyvalue_grad,
        ]
        late = [reduce_split(v.astype(bf16)) for v in late]
        vectors = reduce_vectors(vectors)
    light_gates_grad, light_down_grad, light_output_grad, heavy_output_grad = early[:4]
    return (
        output,
        input_grad,
        vectors[0],
        late[0],
        light_output_grad,
        late[1],
        late[2],
        heavy_output_grad,
        vectors[1],
        vectors[2],
        light_gates_grad,
        light_down_grad,
        early[4],
        early[5],
    )


def solution(mesh):
    rows = P(("dp", "seq"), None)
    line = P(("dp", "seq"))
    tokens = P("dp", "seq", None)
    slots = P("dp", "seq")
    return jax.shard_map(
        per_device,
        mesh=mesh,
        in_specs=(tokens, tokens) + (P(),) * 12 + (slots, slots, slots, P("dp", None), slots),
        out_specs=(tokens, tokens, line) + (rows,) * 5 + (line, line) + (rows,) * 4,
        check_vma=False,
    )
```

```python
import functools
import math
import jax
import jax.numpy as jnp
from jax import lax
from jax.experimental import pallas as pl
from jax.experimental.pallas import tpu as pltpu
from jax.sharding import PartitionSpec as P
D = 768
HL = 8
LHD = 96
HH = 12
HHD = 64
RADIUS = 128
QCAP = 64
KCAP = 64
CORES = 2
DEPTH = 4
MESH = pl.DeviceIdType.MESH
epsilon = 1e-06
bf16 = jnp.bfloat16
f32 = jnp.float32


def dot(left, right, over):
    return lax.dot_general(left, right, (over, ((), ())), preferred_element_type=f32)


def mm(left, right):
    return dot(left, right, ((1,), (0,)))


def mm_nt(left, right):
    return dot(left, right, ((1,), (1,)))


def mm_tn(left, right):
    return dot(left, right, ((0,), (0,)))


class Ring:
    def __init__(self, axis, stride, count):
        self.axis, self.stride, self.count = axis, stride, count
        self.place = (lax.axis_index(axis) // stride) % count

    def shift(self, value, by):
        total = lax.axis_size(self.axis)
        pairs = []
        for i in range(total):
            c = (i // self.stride) % self.count
            pairs.append((i, i + ((c + by) % self.count - c) * self.stride))
        return lax.ppermute(value, self.axis, pairs)

    def scatter_sum(self, value, dim):
        own = lax.dynamic_index_in_dim(value, self.place, dim, keepdims=False)
        total = own.astype(f32)
        for by in range(1, self.count):
            send = lax.dynamic_index_in_dim(
                value, (self.place + by) % self.count, dim, keepdims=False
            )
            total = total + self.shift(send, by).astype(f32)
        return total

    def gather(self, value, dim):
        parts = [value] + [self.shift(value, by) for by in range(1, self.count)]
        return jnp.concatenate(parts, axis=dim)

    def return_sum(self, joined, dim):
        parts = jnp.split(joined, self.count, axis=dim)
        total = parts[0].astype(f32)
        for by in range(1, self.count):
            total = total + self.shift(parts[by], self.count - by).astype(f32)
        return total


def norm_parts(values):
    scale = lax.rsqrt(jnp.mean(values * values, axis=-1, keepdims=True) + epsilon)
    return values * scale, scale


def norm_pull(grad, values, scale, gain):
    weighted = grad * gain
    inner = jnp.mean(weighted * values, axis=-1, keepdims=True)
    return scale * weighted - values * (scale * scale * scale) * inner


def head_windows():
    windows = []
    for h in range(4):
        first, end = h * LHD, (h + 1) * LHD
        windows.append((first // 128 * 128, -(-end // 128) * 128, first, end))
    return windows


def lane_mask(shape, first, end):
    lane = lax.broadcasted_iota(jnp.int32, shape, 1)
    return (lane >= first) & (lane < end)


def join_heads(parts):
    lane = lax.broadcasted_iota(jnp.int32, (parts[0].shape[0], 128), 1)
    return jnp.concatenate(
        [
            jnp.where(lane < 96, parts[0], parts[1][:, :128]),
            jnp.where(lane < 64, parts[1][:, 128:], parts[2][:, :128]),
            jnp.where(lane < 32, parts[2][:, 128:], parts[3]),
        ],
        axis=1,
    )


def light_kernel(ends_ref, own_ref, edge_ref, out_ref):
    half = RADIUS
    factor = LHD ** (-0.5)
    for block in range(2):
        rows = slice(block * half, (block + 1) * half)
        row = lax.broadcasted_iota(jnp.int32, (half, 2 * half), 0)
        col = lax.broadcasted_iota(jnp.int32, (half, 2 * half), 1)
        keep_own = col <= row + half if block == 0 else col >= row
        row, col = row[:, :half], col[:, :half]
        keep_edge = (col >= row if block == 0 else col <= row) & (ends_ref[block] > 0)
        for group in range(2):
            mixed = []
            for a, b, first, end in head_windows():
                lanes = slice(group * 384 + a, group * 384 + b)
                keys = slice(D + lanes.start, D + lanes.stop)
                values = slice(2 * D + lanes.start, 2 * D + lanes.stop)
                query = own_ref[0, rows, lanes]
                query = jnp.where(
                    lane_mask(query.shape, first - a, end - a), query, jnp.zeros_like(query)
                )
                s_own = jnp.where(keep_own, mm_nt(query, own_ref[0, :, keys]), -1e30)
                s_edge = jnp.where(keep_edge, mm_nt(query, edge_ref[0, rows, lanes]), -1e30)
                top = jnp.maximum(
                    jnp.max(s_own, axis=1, keepdims=True), jnp.max(s_edge, axis=1, keepdims=True)
                )
                e_own = jnp.exp((s_own - top) * factor)
                e_edge = jnp.exp((s_edge - top) * factor)
                total = jnp.sum(e_own, axis=1, keepdims=True) + jnp.sum(
                    e_edge, axis=1, keepdims=True
                )
                mix = mm(e_own.astype(bf16), own_ref[0, :, values])
                mix += mm(
                    e_edge.astype(bf16), edge_ref[0, rows, slice(D + lanes.start, D + lanes.stop)]
                )
                mixed.append(mix * (1.0 / total))
            out_ref[0, rows, group * 384 : (group + 1) * 384] = join_heads(mixed).astype(bf16)


def light_attention(ends, own, edge):
    pieces, tokens = own.shape[:2]
    return pl.pallas_call(
        light_kernel,
        out_shape=jax.ShapeDtypeStruct((pieces, tokens, D), bf16),
        grid_spec=pltpu.PrefetchScalarGridSpec(
            num_scalar_prefetch=1,
            grid=(pieces,),
            in_specs=[
                pl.BlockSpec((1, tokens, 3 * D), lambda p, e: (p, 0, 0)),
                pl.BlockSpec((1, 2 * RADIUS, 2 * D), lambda p, e: (p, 0, 0)),
            ],
            out_specs=pl.BlockSpec((1, tokens, D), lambda p, e: (p, 0, 0)),
        ),
        compiler_params=pltpu.CompilerParams(vmem_limit_bytes=32 << 20),
        cost_estimate=pl.CostEstimate(
            flops=pieces * HL * tokens * 384 * 256 * 4,
            bytes_accessed=pieces * (tokens * 4 * D + 2 * RADIUS * 2 * D) * 2,
            transcendentals=pieces * HL * tokens * 384,
        ),
        name="light_attention",
    )(ends, own, edge)


def light_back_unit(reach, groups, own_ref, edge_ref, grad_ref, own_out, edge_out):
    half = RADIUS
    factor = LHD ** (-0.5)
    for group in groups:
        dk_own, dv_own = [None] * 4, [None] * 4
        for block in range(2):
            rows = slice(block * half, (block + 1) * half)
            key = lax.broadcasted_iota(jnp.int32, (2 * half, half), 0)
            que = lax.broadcasted_iota(jnp.int32, (2 * half, half), 1)
            keep_own = key <= que + half if block == 0 else key >= que
            key, que = key[:half], que[:half]
            keep_edge = (key >= que if block == 0 else key <= que) & reach[block]
            dq, dk_edge, dv_edge = [], [], []
            for h, (a, b, first, end) in enumerate(head_windows()):
                lanes = slice(group * 384 + a, group * 384 + b)
                after = slice(D + lanes.start, D + lanes.stop)
                last = slice(2 * D + lanes.start, 2 * D + lanes.stop)
                mask = lane_mask((half, b - a), first - a, end - a)
                query = own_ref[0, rows, lanes]
                query = jnp.where(mask, query, jnp.zeros_like(query))
                grad = grad_ref[0, rows, lanes]
                grad = jnp.where(mask, grad, jnp.zeros_like(grad))
                k_own, k_edge = own_ref[0, :, after], edge_ref[0, rows, lanes]
                v_own, v_edge = own_ref[0, :, last], edge_ref[0, rows, after]
                s_own = jnp.where(keep_own, mm_nt(k_own, query), -1e30)
                s_edge = jnp.where(keep_edge, mm_nt(k_edge, query), -1e30)
                top = jnp.maximum(
                    jnp.max(s_own, axis=0, keepdims=True), jnp.max(s_edge, axis=0, keepdims=True)
                )
                e_own = jnp.exp((s_own - top) * factor)
                e_edge = jnp.exp((s_edge - top) * factor)
                total = jnp.sum(e_own, axis=0, keepdims=True) + jnp.sum(
                    e_edge, axis=0, keepdims=True
                )
                scale = 1.0 / total
                p_own, p_edge = e_own * scale, e_edge * scale
                g_own, g_edge = mm_nt(v_own, grad), mm_nt(v_edge, grad)
                inner = jnp.sum(p_own * g_own, axis=0, keepdims=True) + jnp.sum(
                    p_edge * g_edge, axis=0, keepdims=True
                )
                d_own = (p_own * (g_own - inner)).astype(bf16)
                d_edge = (p_edge * (g_edge - inner)).astype(bf16)
                dv = mm(p_own.astype(bf16), grad)
                dk = mm(d_own, query)
                dv_own[h] = dv if block == 0 else dv_own[h] + dv
                dk_own[h] = dk if block == 0 else dk_own[h] + dk
                dv_edge.append(mm(p_edge.astype(bf16), grad))
                dk_edge.append(mm(d_edge, query) * factor)
                dq.append((mm_tn(d_own, k_own) + mm_tn(d_edge, k_edge)) * factor)
            at = slice(group * 384, (group + 1) * 384)
            at_v = slice(D + at.start, D + at.stop)
            own_out[0, rows, at] = join_heads(dq).astype(bf16)
            edge_out[0, rows, at] = join_heads(dk_edge).astype(bf16)
            edge_out[0, rows, at_v] = join_heads(dv_edge).astype(bf16)
        at_w = slice(2 * D + at.start, 2 * D + at.stop)
        own_out[0, :, at_v] = (join_heads(dk_own) * factor).astype(bf16)
        own_out[0, :, at_w] = join_heads(dv_own).astype(bf16)


def light_back_kernel(ends_ref, *refs):
    light_back_unit((ends_ref[0] > 0, ends_ref[1] > 0), range(2), *refs)


def light_attention_back(ends, own, edge, grad):
    pieces, tokens = own.shape[:2]
    return pl.pallas_call(
        light_back_kernel,
        out_shape=[
            jax.ShapeDtypeStruct((pieces, tokens, 3 * D), bf16),
            jax.ShapeDtypeStruct((pieces, 2 * RADIUS, 2 * D), bf16),
        ],
        grid_spec=pltpu.PrefetchScalarGridSpec(
            num_scalar_prefetch=1,
            grid=(pieces,),
            in_specs=[
                pl.BlockSpec((1, tokens, 3 * D), lambda p, e: (p, 0, 0)),
                pl.BlockSpec((1, 2 * RADIUS, 2 * D), lambda p, e: (p, 0, 0)),
                pl.BlockSpec((1, tokens, D), lambda p, e: (p, 0, 0)),
            ],
            out_specs=[
                pl.BlockSpec((1, tokens, 3 * D), lambda p, e: (p, 0, 0)),
                pl.BlockSpec((1, 2 * RADIUS, 2 * D), lambda p, e: (p, 0, 0)),
            ],
        ),
        compiler_params=pltpu.CompilerParams(vmem_limit_bytes=32 << 20),
        cost_estimate=pl.CostEstimate(
            flops=pieces * HL * tokens * 384 * 256 * 10,
            bytes_accessed=pieces * (tokens * 7 * D + 2 * RADIUS * 4 * D) * 2,
            transcendentals=pieces * HL * tokens * 384,
        ),
        name="light_attention_back",
    )(ends, own, edge, grad)


def spread_heads(value):
    tall = jnp.concatenate([value] * 4, axis=0)
    row = lax.broadcasted_iota(jnp.int32, tall.shape, 0) // QCAP
    lane = lax.broadcasted_iota(jnp.int32, tall.shape, 1) // HHD
    return jnp.where(row == lane, tall, jnp.zeros_like(tall))


def fold_heads(tall):
    lane = lax.broadcasted_iota(jnp.int32, (QCAP, 4 * HHD), 1) // HHD
    total = tall[:QCAP]
    for r in range(1, 4):
        total = jnp.where(lane == r, tall[r * QCAP : (r + 1) * QCAP], total)
    return total


def heavy_kernel(query_ref, pair_ref, live_ref, out_ref):
    factor = HHD ** (-0.5)
    keep = live_ref[0] > 0
    for group in range(HH // 4):
        lanes = slice(group * 256, (group + 1) * 256)
        query = spread_heads(query_ref[0, :, lanes])
        scores = jnp.where(keep, mm_nt(query, pair_ref[0, :, lanes]), -1e30)
        top = jnp.max(scores, axis=1, keepdims=True)
        raised = jnp.exp((scores - top) * factor)
        total = jnp.sum(raised, axis=1, keepdims=True)
        mix = mm(raised.astype(bf16), pair_ref[0, :, D + lanes.start : D + lanes.stop])
        out_ref[0, :, lanes] = fold_heads(mix * (1.0 / total)).astype(bf16)


def heavy_attention(query, pairs, live):
    pieces, slots = pairs.shape[:2]
    return pl.pallas_call(
        heavy_kernel,
        out_shape=jax.ShapeDtypeStruct((pieces, QCAP, D), bf16),
        grid=(pieces,),
        in_specs=[
            pl.BlockSpec((1, QCAP, D), lambda p: (p, 0, 0)),
            pl.BlockSpec((1, slots, 2 * D), lambda p: (p, 0, 0)),
            pl.BlockSpec((1, 1, slots), lambda p: (p, 0, 0)),
        ],
        out_specs=pl.BlockSpec((1, QCAP, D), lambda p: (p, 0, 0)),
        compiler_params=pltpu.CompilerParams(vmem_limit_bytes=32 << 20),
        cost_estimate=pl.CostEstimate(
            flops=pieces * 3 * 4 * 256 * 256 * slots,
            bytes_accessed=pieces * (slots + QCAP) * 2 * D * 2,
            transcendentals=pieces * HH * QCAP * slots,
        ),
        name="heavy_attention",
    )(query, pairs, live)


def heavy_back_kernel(query_ref, pair_ref, live_ref, grad_ref, query_out, pair_out):
    factor = HHD ** (-0.5)
    slots = pair_ref.shape[1]
    keep = jnp.broadcast_to(live_ref[0], (128, slots)).T[:, :1] > 0
    for group in range(HH // 4):
        lanes = slice(group * 256, (group + 1) * 256)
        after = slice(D + lanes.start, D + lanes.stop)
        query = spread_heads(query_ref[0, :, lanes])
        grad = spread_heads(grad_ref[0, :, lanes])
        keys = pair_ref[0, :, lanes]
        scores = jnp.where(keep, mm_nt(keys, query), -1e30)
        top = jnp.max(scores, axis=0, keepdims=True)
        raised = jnp.exp((scores - top) * factor)
        probs = raised * (1.0 / jnp.sum(raised, axis=0, keepdims=True))
        grad_probs = mm_nt(pair_ref[0, :, after], grad)
        inner = jnp.sum(probs * grad_probs, axis=0, keepdims=True)
        grad_scores = (probs * (grad_probs - inner)).astype(bf16)
        pair_out[0, :, after] = mm(probs.astype(bf16), grad).astype(bf16)
        pair_out[0, :, lanes] = (mm(grad_scores, query) * factor).astype(bf16)
        query_out[0, :, lanes] = (fold_heads(mm_tn(grad_scores, keys)) * factor).astype(bf16)


def heavy_attention_back(query, pairs, live, grad):
    pieces, slots = pairs.shape[:2]
    return pl.pallas_call(
        heavy_back_kernel,
        out_shape=[
            jax.ShapeDtypeStruct((pieces, QCAP, D), bf16),
            jax.ShapeDtypeStruct((pieces, slots, 2 * D), bf16),
        ],
        grid=(pieces,),
        in_specs=[
            pl.BlockSpec((1, QCAP, D), lambda p: (p, 0, 0)),
            pl.BlockSpec((1, slots, 2 * D), lambda p: (p, 0, 0)),
            pl.BlockSpec((1, 1, slots), lambda p: (p, 0, 0)),
            pl.BlockSpec((1, QCAP, D), lambda p: (p, 0, 0)),
        ],
        out_specs=[
            pl.BlockSpec((1, QCAP, D), lambda p: (p, 0, 0)),
            pl.BlockSpec((1, slots, 2 * D), lambda p: (p, 0, 0)),
        ],
        compiler_params=pltpu.CompilerParams(vmem_limit_bytes=32 << 20),
        cost_estimate=pl.CostEstimate(
            flops=pieces * 3 * 10 * 256 * 256 * slots,
            bytes_accessed=pieces * (2 * slots + 2 * QCAP) * 2 * D * 2,
            transcendentals=pieces * HH * QCAP * slots,
        ),
        name="heavy_attention_back",
    )(query, pairs, live, grad)


def glu_and_pull(gate, up, grad):
    slope = 0.7978845608028654
    square = gate * gate
    curve = jnp.tanh(gate * (slope + (slope * 0.044715) * square))
    half = 0.5 + 0.5 * curve
    gelu = gate * half
    bend = (0.5 * gate) * (1.0 - curve * curve) * (slope + (3 * slope * 0.044715) * square)
    return gelu * up, grad * up * (half + bend), grad * gelu


def feed_kernel(
    n_y,
    normed_in,
    cot_in,
    own_rows,
    gates_in,
    down_in,
    gates_heavy,
    down_heavy,
    act_to,
    pre_to,
    feed_to,
    grad_to,
    back_out,
    rows_to,
    heavy_act_to,
    heavy_pre_to,
    normed,
    cot,
    gates,
    down,
    act_out,
    pre_out,
    feed_out,
    grad_out,
    heavy_act_out,
    heavy_pre_out,
    wide,
    tall,
    rows,
    part,
    from_core,
    to_y,
    from_y,
    in_sem,
    out_sem,
    weight_sem,
    rows_rsem,
    rows_ssem,
    core_rsem,
    core_ssem,
    y_rsem,
    y_ssem,
):
    dp, seq = lax.axis_index("dp"), lax.axis_index("seq")
    c, y = dp % CORES, seq % n_y
    me = c * n_y + y
    to_core, to_beside = (dp + 1 - 2 * c, seq), (dp, seq + 1 - 2 * y)
    share = tall.shape[0]
    total = gates_heavy.shape[1] // 2
    inputs = [
        pltpu.make_async_copy(src, dst, in_sem.at[i])
        for i, (src, dst) in enumerate(
            (
                (own_rows, rows.at[me]),
                (gates_in, gates),
                (down_in, down),
                (normed_in, normed),
                (cot_in, cot),
            )
        )
    ]
    for load in inputs:
        load.start()
    loads = [
        pltpu.make_async_copy(
            gates_heavy.at[:, pl.ds(pl.multiple_of(i * total + me * share, share), share)],
            wide.at[i],
            weight_sem.at[i],
        )
        for i in range(2)
    ]
    loads.append(
        pltpu.make_async_copy(
            down_heavy.at[pl.ds(pl.multiple_of(me * share, share), share)], tall, weight_sem.at[2]
        )
    )
    for load in loads:
        load.start()
    barrier = pltpu.get_barrier_semaphore()
    for peer in (to_core, to_beside):
        pl.semaphore_signal(barrier, inc=1, device_id=peer, device_id_type=MESH)
    pl.semaphore_wait(barrier, 2)

    def copy(src, dst, ssem, rsem, peer):
        return pltpu.make_async_remote_copy(
            src_ref=src,
            dst_ref=dst,
            send_sem=ssem,
            recv_sem=rsem,
            device_id=peer,
            device_id_type=MESH,
        )

    def rows_copy(slot, i, peer):
        return copy(rows.at[slot], rows.at[slot], rows_ssem.at[i], rows_rsem.at[slot], peer)

    inputs[0].wait()
    rows_copy(me, 0, to_beside).start()
    rows_copy(me, 1, to_core).start()
    beside, diagonal, other = c * n_y + 1 - y, (1 - c) * n_y + 1 - y, (1 - c) * n_y + y
    hidden = down.shape[0]
    step = 256
    for load in inputs[1:]:
        load.wait()
    outputs = (
        (act_out, act_to),
        (pre_out, pre_to),
        (feed_out, feed_to),
        (grad_out, grad_to),
        (heavy_act_out, heavy_act_to),
        (heavy_pre_out, heavy_pre_to),
        (rows, rows_to),
    )

    @pl.loop(0, normed.shape[0] // step)
    def _(t):
        at = pl.ds(pl.multiple_of(t * step, step), step)
        gate = mm(normed[at], gates[:, :hidden])
        up = mm(normed[at], gates[:, hidden:])
        act, grad_gate, grad_up = glu_and_pull(gate, up, mm_nt(cot[at], down[...]))
        act = act.astype(bf16)
        grad_gate = grad_gate.astype(bf16)
        grad_up = grad_up.astype(bf16)
        act_out[at] = act
        pre_out[at, :hidden] = grad_gate
        pre_out[at, hidden:] = grad_up
        feed_out[at] = mm(act, down[...])
        grad_out[at] = mm_nt(grad_gate, gates[:, :hidden]) + mm_nt(grad_up, gates[:, hidden:])
        for i, (src, dst) in enumerate(outputs[:4]):
            pltpu.make_async_copy(src.at[at], dst.at[at], out_sem.at[i]).start()

    for load in loads:
        load.wait()
    rows_copy(beside, 2, to_core).wait_recv()
    rows_copy(beside, 2, to_core).start()

    @pl.loop(0, 4)
    def _(i):
        first, second, third = i == 0, i == 1, i == 2
        slot = jnp.where(
            first, me, jnp.where(second, diagonal, jnp.where(third, beside, other))
        )

        @pl.when(second)
        def _():
            rows_copy(diagonal, 0, to_core).wait_recv()

        @pl.when(i == 3)
        def _():
            rows_copy(other, 0, to_core).wait_recv()

        value, grad = rows[slot, 0], rows[slot, 1]
        gate, up = mm(value, wide[0]), mm(value, wide[1])
        act, grad_gate, grad_up = glu_and_pull(gate, up, mm_nt(grad, tall[...]))
        act = act.astype(bf16)
        grad_gate = grad_gate.astype(bf16)
        grad_up = grad_up.astype(bf16)
        heavy_act_out[slot] = act
        heavy_pre_out[slot, :, :share] = grad_gate
        heavy_pre_out[slot, :, share:] = grad_up
        for n, (src, dst) in enumerate(outputs[4:6]):
            pltpu.make_async_copy(src.at[slot], dst.at[slot], out_sem.at[4 + n]).start()
        part[i, 0] = mm(act, tall[...]).astype(bf16)
        part[i, 1] = (mm_nt(grad_gate, wide[0]) + mm_nt(grad_up, wide[1])).astype(bf16)

        @pl.when(second)
        def _():
            copy(part.at[1], from_core.at[0], core_ssem.at[0], core_rsem.at[0], to_core).start()

        @pl.when(third)
        def _():
            copy(part.at[1], from_core.at[0], core_ssem.at[0], core_rsem.at[0], to_core).wait_recv()
            to_y[...] = part[2] + from_core[0]
            copy(to_y, from_y, y_ssem, y_rsem, to_beside).start()

        @pl.when(i == 3)
        def _():
            copy(part.at[3], from_core.at[1], core_ssem.at[1], core_rsem.at[1], to_core).start()

    pltpu.make_async_copy(rows, rows_to, out_sem.at[6]).start()
    copy(part.at[3], from_core.at[1], core_ssem.at[1], core_rsem.at[1], to_core).wait()
    copy(to_y, from_y, y_ssem, y_rsem, to_beside).wait()
    sums = part[0].astype(f32) + from_core[1].astype(f32) + from_y[...].astype(f32)
    back_out[...] = sums.astype(bf16)
    copy(part.at[1], from_core.at[0], core_ssem.at[0], core_rsem.at[0], to_core).wait_send()
    for i, slot in enumerate((me, me, beside)):
        rows_copy(slot, i, to_core).wait_send()
    for i, (src, dst) in enumerate(outputs):
        pltpu.make_async_copy(src, dst, out_sem.at[i]).wait()


def feed_forward(normed, cot, own_rows, gates, down, gates_heavy, down_heavy, n_y):
    count, hidden = normed.shape[0], down.shape[0]
    slots = own_rows.shape[1]
    share = down_heavy.shape[0] // 4
    here, anywhere = pl.BlockSpec(memory_space=pltpu.VMEM), pl.BlockSpec(memory_space=pl.ANY)
    pair = (2, slots, D)
    return pl.pallas_call(
        functools.partial(feed_kernel, n_y),
        out_shape=[
            jax.ShapeDtypeStruct((count, hidden), bf16),
            jax.ShapeDtypeStruct((count, 2 * hidden), bf16),
            jax.ShapeDtypeStruct((count, D), f32),
            jax.ShapeDtypeStruct((count, D), f32),
            jax.ShapeDtypeStruct(pair, bf16),
            jax.ShapeDtypeStruct((4,) + pair, bf16),
            jax.ShapeDtypeStruct((4, slots, share), bf16),
            jax.ShapeDtypeStruct((4, slots, 2 * share), bf16),
        ],
        in_specs=[anywhere] * 7,
        out_specs=[anywhere] * 4 + [here] + [anywhere] * 3,
        scratch_shapes=[
            pltpu.VMEM((count, D), bf16),
            pltpu.VMEM((count, D), bf16),
            pltpu.VMEM((D, 2 * hidden), bf16),
            pltpu.VMEM((hidden, D), bf16),
            pltpu.VMEM((count, hidden), bf16),
            pltpu.VMEM((count, 2 * hidden), bf16),
            pltpu.VMEM((count, D), f32),
            pltpu.VMEM((count, D), f32),
            pltpu.VMEM((4, slots, share), bf16),
            pltpu.VMEM((4, slots, 2 * share), bf16),
            pltpu.VMEM((2, D, share), bf16),
            pltpu.VMEM((share, D), bf16),
            pltpu.VMEM((4,) + pair, bf16),
            pltpu.VMEM((4,) + pair, bf16),
            pltpu.VMEM((2,) + pair, bf16),
            pltpu.VMEM(pair, bf16),
            pltpu.VMEM(pair, bf16),
            pltpu.SemaphoreType.DMA((5,)),
            pltpu.SemaphoreType.DMA((7,)),
            pltpu.SemaphoreType.DMA((3,)),
            pltpu.SemaphoreType.DMA((4,)),
            pltpu.SemaphoreType.DMA((3,)),
            pltpu.SemaphoreType.DMA((2,)),
            pltpu.SemaphoreType.DMA((2,)),
            pltpu.SemaphoreType.DMA,
            pltpu.SemaphoreType.DMA,
        ],
        compiler_params=pltpu.CompilerParams(
            collective_id=2, has_side_effects=True, vmem_limit_bytes=60 << 20
        ),
        cost_estimate=pl.CostEstimate(
            flops=12 * count * D * hidden + 48 * slots * D * share,
            bytes_accessed=30 << 20,
            transcendentals=count * hidden + 4 * slots * share,
        ),
        name="feed_forward",
    )(normed, cot, own_rows, gates, down, gates_heavy, down_heavy)


def reduce_kernel(jobs, counts, n_y, *refs):
    n_sources, n_outs, light, factors = counts
    refs = list(refs)

    def take(count):
        taken = refs[:count]
        del refs[:count]
        return taken

    sources = take(n_sources)
    given = take(4 if light else factors)
    outs = take(n_outs)
    made = take(3 if light else 0)
    held = []
    for job in jobs:
        names = SCRATCH[job[0]] + (("full",) if len(job) > 7 else ())
        held.append(dict(zip(names, take(len(names)))))
    kinds = [job[0] for job in jobs]
    dp, seq = lax.axis_index("dp"), lax.axis_index("seq")
    x, c = dp // CORES, dp % CORES
    z, y = seq // n_y, seq % n_y
    z_high, z_low = z // 2, z % 2
    group = c * n_y + y

    def device(x=x, c=c, z=z, y=y):
        return (x * CORES + c, z * n_y + y)

    to = {
        "core": device(c=1 - c),
        "x": device(x=1 - x),
        "y": device(y=1 - y),
        "low": device(z=z_high * 2 + 1 - z_low),
        "high": device(z=(1 - z_high) * 2 + z_low),
    }
    owner = (group, x * DEPTH + z)
    origin = device(x=seq // DEPTH, c=dp // n_y, z=seq % DEPTH, y=dp % n_y)
    moved = jnp.logical_or(owner[0] != dp, owner[1] != seq)

    barrier = pltpu.get_barrier_semaphore()

    def greet(peer):
        pl.semaphore_signal(barrier, inc=1, device_id=peer, device_id_type=MESH)

    for peer in to.values():
        greet(peer)
    expected = len(to)
    if "gates" in kinds:
        greet(device(c=1 - c, y=1 - y))
        expected += 1
    pairs = []
    if "down" in kinds:
        pairs += [(moved, owner), (moved, origin)]
    if light:
        pairs += [(seq > 0, (dp, seq - 1)), (seq < DEPTH * n_y - 1, (dp, seq + 1))]
    for present, peer in pairs:

        @pl.when(present)
        def _():
            greet(peer)

    for present, _ in pairs:
        expected = expected + jnp.where(present, 1, 0)
    pl.semaphore_wait(barrier, expected)

    def copy(src, dst, a, stage, k, peer):
        return pltpu.make_async_remote_copy(
            src_ref=src,
            dst_ref=dst,
            send_sem=held[a]["ssem"].at[stage],
            recv_sem=held[a]["rsem"].at[stage, k],
            device_id=peer,
            device_id_type=MESH,
        )

    def send(src, name, k, a, place=None, slot=None):
        dst = held[a][name].at[k] if slot is None else held[a][name].at[k, slot]
        copy(src, dst, a, STAGES[name], k, place).start()

    def arrived(name, a, k):
        buffer = held[a][name].at[k]
        copy(buffer, buffer, a, STAGES[name], k, to["core"]).wait_recv()

    def columns(a, k):
        start, width = jobs[a][2:4]
        return pl.ds(start + k * width, width)

    if factors:
        *kept, factor_sem = refs
        wanted, fetched = [], set()
        for a, job in enumerate(jobs):
            for left, right, start in job[7:]:
                for k in range(job[4]):
                    wanted.append((k, a, left, right, pl.ds(start + k * job[3], job[3])))
        fetches = {}
        for k, a, left, right, cols in sorted(wanted, key=lambda w: w[:2]):
            for key, part in (((left,), slice(None)), ((right, cols.start), cols)):
                if key not in fetches:
                    src, dst = given[key[0]].at[:, part], kept[key[0]].at[:, part]
                    fetches[key] = pltpu.make_async_copy(src, dst, factor_sem.at[len(fetches)])
                    fetches[key].start()

    def produce(a, k):
        width, height = jobs[a][3], held[a]["full"].shape[-2]
        total = 0.0
        for left, right, start in jobs[a][7:]:
            for key in ((left,), (right, start + k * width)):
                if key not in fetched:
                    fetched.add(key)
                    fetches[key].wait()
            cols = slice(start + k * width, start + (k + 1) * width)
            total = total + mm_tn(kept[left][...], kept[right][:, cols])
        at = 0
        for i in range(2):
            for j in range(CORES):
                for m in range(DEPTH):
                    for n in range(n_y):
                        rows = total[at * height : (at + 1) * height]
                        held[a]["full"][k, i, j, m, n] = rows.astype(bf16)
                        at += 1

    def local(a, k):
        whole, cols = sources[jobs[a][1]], columns(a, k)
        if kinds[a] in ("xy", "yx"):
            part = whole.at[:, c, :, :, :, cols]
        else:
            part = whole.at[x, :, :, :, :, cols]
        return pltpu.make_async_copy(part, held[a]["own"].at[k], held[a]["lsem"].at[k])

    def begin(a, k):
        if len(jobs[a]) > 7:
            produce(a, k)
            send(held[a]["full"].at[k, :, 1 - c], "core", k, a, to["core"])
            return
        whole, cols = sources[jobs[a][1]], columns(a, k)
        local(a, k).start()
        if kinds[a] in ("xy", "yx"):
            send(whole.at[:, 1 - c, :, :, :, cols], "core", k, a, to["core"])
        else:
            send(whole.at[1 - x, :, :, :, :, cols], "xx", k, a, to["x"])

    def first(a, k):
        h, kind = held[a], kinds[a]
        own = h["own"]
        made_here = "full" in h
        if not made_here:
            local(a, k).wait()
        if kind not in ("xy", "yx"):
            return
        arrived("core", a, k)

        @pl.loop(0, 2 * DEPTH)
        def _(i):
            for j in range(n_y):
                at = (k, i // DEPTH, i % DEPTH, j)
                mine = h["full"][at[:2] + (c,) + at[2:]] if made_here else own[at]
                own[at] = mine + h["core"][at]

        if kind == "xy":
            send(own.at[k, 1 - x], "xx", k, a, to["x"])
        else:
            send(own.at[k, :, :, 1 - y], "yy", k, a, to["y"])

    def second(a, k):
        h, kind = held[a], kinds[a]
        own = h["own"]
        if kind == "xy":
            arrived("xx", a, k)

            @pl.loop(0, DEPTH)
            def _(i):
                for j in range(n_y):
                    at = (k, x, i, j)
                    own[at] = own[at] + h["xx"][k, i, j]

            send(own.at[k, x, :, 1 - y], "yy", k, a, to["y"])
        elif kind == "yx":
            arrived("yy", a, k)

            @pl.loop(0, DEPTH)
            def _(i):
                for j in range(2):
                    at = (k, j, i, y)
                    own[at] = own[at] + h["yy"][k, j, i]

            send(own.at[k, 1 - x, :, y], "xx", k, a, to["x"])

    def third(a, k):
        h, kind = held[a], kinds[a]
        own = h["own"]
        if kind in ("xy", "yx"):
            name = "yy" if kind == "xy" else "xx"
            arrived(name, a, k)

            @pl.loop(0, DEPTH)
            def _(i):
                at = (k, x, i, y)
                own[at] = own[at] + h[name][k, i]

            for high in range(2):
                send(own.at[k, x, high * 2 + 1 - z_low, y], "za", k, a, to["low"], high)
        else:
            arrived("xx", a, k)

            @pl.loop(0, DEPTH)
            def _(i):
                for g in range(own.shape[1]):
                    for j in range(own.shape[3]):
                        at = (k, g, i, j)
                        own[at] = own[at] + h["xx"][at]

            for high in range(2):
                send(own.at[k, :, high * 2 + 1 - z_low], "za", k, a, to["low"], high)

    def fourth(a, k):
        h, kind = held[a], kinds[a]
        own = h["own"]
        arrived("za", a, k)
        if kind in ("xy", "yx"):
            for high in range(2):
                at = (k, x, high * 2 + z_low, y)
                own[at] = own[at] + h["za"][k, high]
            send(own.at[k, x, (1 - z_high) * 2 + z_low, y], "zb", k, a, to["high"])
        else:

            @pl.loop(0, own.shape[1])
            def _(g):
                for j in range(own.shape[3]):
                    for high in range(2):
                        at = (k, g, high * 2 + z_low, j)
                        own[at] = own[at] + h["za"][k, high, g, j]

            send(own.at[k, :, (1 - z_high) * 2 + z_low], "zb", k, a, to["high"])

    def fifth(a, k):
        h = held[a]
        kind, _, _, width, _, out, start = jobs[a][:7]
        own = h["own"]
        arrived("zb", a, k)
        if kind in ("xy", "yx"):
            total = own[k, x, z, y].astype(f32) + h["zb"][k].astype(f32)
            outs[out][:, start + k * width : start + (k + 1) * width] = total
        elif kind == "down":
            h["sum"][k] = own[k, 0, z, 0] + h["zb"][k, 0, 0]

            @pl.when(moved)
            def _():
                send(h["sum"].at[k], "dd", k, a, owner)

            @pl.when(jnp.logical_not(moved))
            def _():
                h["dd"][k] = h["sum"][k]
        else:

            @pl.loop(0, CORES)
            def _(g):
                for j in range(n_y):
                    h["sum"][k, g * n_y + j] = own[k, g, z, j] + h["zb"][k, g, j]

            h["dd"][k, group] = h["sum"][k, group]
            for g, j in ((1 - c, y), (c, 1 - y), (1 - c, 1 - y)):
                send(h["sum"].at[k, g * n_y + j], "dd", k, a, device(c=g, y=j), group)

    def last(a, k):
        h = held[a]
        kind, _, _, width, chunks, out, start = jobs[a][:7]
        if kind == "gates":
            part = h["dd"].at[k, pl.ds(0, 3)]
            copy(part, part, a, STAGES["dd"], k, to["core"]).wait_recv()
            for g in range(4):
                at = start + (g * chunks + k) * width
                outs[out][:, at : at + width] = h["dd"][k, g].astype(f32)
        elif kind == "down":

            @pl.when(moved)
            def _():
                arrived("dd", a, k)

            outs[out][:, start + k * width : start + (k + 1) * width] = h["dd"][k].astype(f32)

    lists = {"all": [], "rest": []}
    for a, job in enumerate(jobs):
        lists["all" if job[0] in ("xy", "yx") else "rest"].append([(a, k) for k in range(job[4])])
    stages = (begin, first, second, third, fourth, fifth, last)
    longest = max(len(interleave(parts)) for parts in lists.values())
    events = []
    for name, parts in lists.items():
        order = interleave(parts)
        order.sort(key=lambda what: len(jobs[what[0]]) > 7)
        for i, what in enumerate(order):
            for stage, lag in zip(stages, LAGS[name]):
                if factors and stage is begin and len(jobs[what[0]]) == 7:
                    lag = -20
                events.append((i * longest / len(order) + lag, len(events), stage, what))
    if light:
        edges_in = made[2]
        *inner, weights, ready, landed, load_sem, weight_sem, out_sem, edge_ssem, edge_rsem = refs
        edge_out = inner[4]
        pieces = edge_out.shape[0]
        reach = (seq > 0, seq < DEPTH * n_y - 1)

        def load(i, p):
            return pltpu.make_async_copy(given[i].at[p], inner[i].at[p], load_sem.at[i, p])

        def store(i, p):
            src, dst = inner[3 + i], made[i]
            if p is not None:
                src, dst = src.at[p], dst.at[p]
            return pltpu.make_async_copy(src, dst, out_sem.at[i])

        for p in range(pieces):
            for i in range(3):
                load(i, p).start()
        load_weights = pltpu.make_async_copy(given[3], weights, weight_sem)
        load_weights.start()

        def edge_copy(side, p):
            src = ready.at[p, pl.ds(side * RADIUS, RADIUS)]
            dst = landed.at[p, pl.ds((1 - side) * RADIUS, RADIUS)]
            return pltpu.make_async_remote_copy(
                src_ref=src,
                dst_ref=dst,
                send_sem=edge_ssem.at[side],
                recv_sem=edge_rsem.at[1 - side, p],
                device_id=(dp, seq - 1 + 2 * side),
                device_id_type=MESH,
            )

        def unit(p, g):
            if g == 0:
                for i in range(3):
                    load(i, p).wait()
            light_back_unit(reach, (g,), *[ref.at[pl.ds(p, 1)] for ref in inner])
            if g == 1:
                for i in range(2):
                    store(i, p).start()
                if p == 0:
                    load_weights.wait()
                rows = mm_nt(edge_out[p], weights[:, D:])
                ready[p] = rows.astype(bf16)
                for side in range(2):

                    @pl.when(reach[side])
                    def _():
                        edge_copy(side, p).start()

        for p in range(pieces):
            for g in range(2):
                events.append(((2 * p + g) * 1.2, len(events), unit, (p, g)))
    for _, _, stage, what in sorted(events, key=lambda e: e[:2]):
        stage(*what)

    if light:
        for i in range(2):
            store(i, None).wait()
        for side in range(2):
            rows = pl.ds(side * RADIUS, RADIUS)

            @pl.when(reach[side])
            def _():
                for p in range(pieces):
                    edge_copy(1 - side, p).wait_recv()
                    edges_in[p, rows] = landed[p, rows]
                whole = ready.at[:, rows]
                pltpu.make_async_remote_copy(
                    src_ref=whole,
                    dst_ref=whole,
                    send_sem=edge_ssem.at[side],
                    recv_sem=edge_rsem.at[side, 0],
                    device_id=(dp, seq - 1 + 2 * side),
                    device_id_type=MESH,
                ).wait_send()

            @pl.when(jnp.logical_not(reach[side]))
            def _():
                for p in range(pieces):
                    edges_in[p, rows] = jnp.zeros((RADIUS, D), bf16)

    for a, kind in enumerate(kinds):
        h = held[a]
        for name in ("core", "xx", "yy", "za", "zb"):
            if name in h:
                copy(h[name], h[name], a, STAGES[name], 0, to["core"]).wait_send()
        if kind == "gates":
            part = h["dd"].at[:, pl.ds(0, 3)]
            copy(part, part, a, STAGES["dd"], 0, to["core"]).wait_send()
        elif kind == "down":

            @pl.when(moved)
            def _():
                copy(h["dd"], h["dd"], a, STAGES["dd"], 0, to["core"]).wait_send()


def interleave(parts):
    keyed = [((i + 0.5) / len(p), n, v) for n, p in enumerate(parts) for i, v in enumerate(p)]
    return [v for _, _, v in sorted(keyed)]


LAGS = {"all": (-4, 0, 2, 4, 6, 8, 8), "rest": (-2, -1, -1, 1.5, 3.5, 5.5, 8)}
STAGES = {"core": 0, "xx": 1, "yy": 2, "za": 3, "zb": 4, "dd": 5}
SCRATCH = {
    "xy": ("own", "core", "xx", "yy", "za", "zb", "lsem", "rsem", "ssem"),
    "yx": ("own", "core", "xx", "yy", "za", "zb", "lsem", "rsem", "ssem"),
    "gates": ("own", "xx", "za", "zb", "sum", "dd", "lsem", "rsem", "ssem"),
    "down": ("own", "xx", "za", "zb", "sum", "dd", "lsem", "rsem", "ssem"),
}


def reduce_all(values, jobs, widths, n_y, collective_id, light=(), factors=()):
    operands, scratch = [], []
    for value, inner in values:
        height, columns = value.shape
        lead = (2, CORES, DEPTH, n_y) if inner else (2, 1, DEPTH, 1)
        operands.append(value.reshape(lead + (height // math.prod(lead), columns)))
    heights = {job[5]: D // (8 * DEPTH) if len(job) > 7 else operands[job[1]].shape[4] for job in jobs}
    out_shape = [jax.ShapeDtypeStruct((heights[o], w), f32) for o, w in enumerate(widths)]
    for kind, source, _, width, k, out, *rest in jobs:
        _, inner, _, outer = operands[source].shape[:4]
        height = heights[out]
        if kind == "xy":
            shapes = [(2, DEPTH, n_y)] * 2 + [(DEPTH, n_y), (DEPTH,), (2,), ()]
        elif kind == "yx":
            shapes = [(2, DEPTH, n_y)] * 2 + [(DEPTH,), (2, DEPTH), (2,), ()]
        else:
            both = (inner, outer)
            shapes = [(inner, DEPTH, outer)] * 2 + [(2,) + both, both]
            shapes += [(4,), (4,)] if kind == "gates" else [(), ()]
        scratch += [pltpu.VMEM((k,) + shape + (height, width), bf16) for shape in shapes]
        scratch += [
            pltpu.SemaphoreType.DMA((k,)),
            pltpu.SemaphoreType.DMA((6, k)),
            pltpu.SemaphoreType.DMA((6,)),
        ]
        if len(rest) > 1:
            scratch.append(pltpu.VMEM((k, 2, CORES, DEPTH, n_y, height, width), bf16))
    if light:
        pieces, edge_rows = light[1].shape[:2]
        out_shape += [jax.ShapeDtypeStruct(v.shape, bf16) for v in light[:2]]
        out_shape.append(jax.ShapeDtypeStruct((pieces, edge_rows, D), bf16))
        own, edge, grad, weights = light
        scratch += [pltpu.VMEM(v.shape, bf16) for v in (own, edge, grad, own, edge, weights)]
        scratch += [pltpu.VMEM((pieces, edge_rows, D), bf16)] * 2
        scratch += [pltpu.SemaphoreType.DMA((3, pieces)), pltpu.SemaphoreType.DMA]
        scratch += [pltpu.SemaphoreType.DMA((2,))] * 2 + [pltpu.SemaphoreType.DMA((2, pieces))]
    if factors:
        scratch += [pltpu.VMEM(v.shape, bf16) for v in factors]
        scratch.append(pltpu.SemaphoreType.DMA((32,)))
    total = 16 * n_y * sum(math.prod(shape.shape) for shape in out_shape[: len(widths)])
    here, anywhere = pl.BlockSpec(memory_space=pltpu.VMEM), pl.BlockSpec(memory_space=pl.ANY)
    out_specs = [here] * len(widths) + ([anywhere] * 2 + [here] if light else [])
    return pl.pallas_call(
        functools.partial(
            reduce_kernel,
            tuple(jobs),
            (len(values), len(widths), bool(light), len(factors)),
            n_y,
        ),
        out_shape=out_shape,
        in_specs=[anywhere] * len([*values, *light, *factors]),
        out_specs=out_specs,
        scratch_shapes=scratch,
        compiler_params=pltpu.CompilerParams(
            collective_id=collective_id, has_side_effects=True, vmem_limit_bytes=60 << 20
        ),
        cost_estimate=pl.CostEstimate(
            flops=2 * total, bytes_accessed=32 * total, transcendentals=0
        ),
        name="reduce_gradients",
    )(*operands, *light, *factors)


def copy_kernel(*refs):
    count = len(refs) // 2
    for i in range(count):
        refs[count + i][...] = refs[i][...]


def copy_all(values):
    count = len(values)
    return pl.pallas_call(
        copy_kernel,
        out_shape=[jax.ShapeDtypeStruct(v.shape, v.dtype) for v in values],
        in_specs=[pl.BlockSpec(memory_space=pltpu.VMEM)] * count,
        out_specs=[pl.BlockSpec(memory_space=pltpu.VMEM)] * count,
        name="copy_outputs",
    )(*values)


def per_device(
    layer_input,
    cotangent,
    first_gain,
    light_inputs,
    light_output,
    heavy_queries,
    heavy_keyvalue,
    heavy_output,
    second_gain,
    router,
    light_gates,
    light_down,
    heavy_gates,
    heavy_down,
    query_index,
    query_count,
    key_index,
    key_count,
    feed_slot,
):
    pieces, tokens = layer_input.shape[:2]
    rows = pieces * tokens
    n_dp, n_seq = lax.axis_size("dp"), lax.axis_size("seq")
    n_x, n_y = n_dp // CORES, n_seq // DEPTH
    seq_rank = lax.axis_index("seq")
    core = Ring("dp", 1, CORES)
    ring_x = Ring("dp", CORES, n_x)
    ring_y = Ring("seq", 1, n_y)
    ring_z = Ring("seq", n_y, DEPTH)
    capacity = max(2, 3 * rows // (16 * n_seq))
    slots = n_seq * capacity
    each = D // (n_dp * n_seq)
    kernels = each % 8 == 0 and n_x == n_y == 2

    def reduce_grad(value, first, second):
        height, width = value.shape
        chunk = height // (n_dp * n_seq)
        parts = value.reshape(n_x, CORES, DEPTH, n_y, chunk, width)
        parts = core.scatter_sum(parts, 1).astype(bf16)
        dims = ["x", "z", "y"]
        rings = {"x": ring_x, "y": ring_y, "z": ring_z}
        order = [first, second, [d for d in dims if d not in (first, second)][0]]
        for i, d in enumerate(order):
            at = dims.index(d)
            parts = rings[d].scatter_sum(parts, at)
            if i < 2:
                parts = parts.astype(bf16)
            dims.remove(d)
        return parts

    def reduce_split(value):
        half = value.shape[1] // 2
        return jnp.concatenate(
            [
                reduce_grad(value[:, :half], "x", "y"),
                reduce_grad(value[:, half:], "y", "x"),
            ],
            axis=1,
        )

    def reduce_vectors(value):
        count, width = value.shape
        chunk = width // (n_dp * n_seq)
        parts = value.reshape(count, n_x, CORES, DEPTH, n_y, chunk)
        parts = core.scatter_sum(parts, 2)
        parts = ring_x.scatter_sum(parts, 1)
        parts = ring_z.scatter_sum(parts, 1)
        return ring_y.scatter_sum(parts, 1)

    ends = n_seq - 1
    left_rows = lax.ppermute(
        layer_input[:, tokens - RADIUS :], "seq", [(i, i + 1) for i in range(ends)]
    )
    right_rows = lax.ppermute(layer_input[:, :RADIUS], "seq", [(i + 1, i) for i in range(ends)])
    position = jnp.arange(tokens, dtype=jnp.int32)
    key_pick = (key_index[:, :, None] == position[None, None, :]).astype(bf16)
    query_live = jnp.arange(QCAP, dtype=jnp.int32)[None, :] < query_count
    query_pick = (query_index[:, :, None] == position[None, None, :]).astype(bf16)
    live_pick = query_pick * query_live[:, :, None].astype(bf16)
    key_raw = jnp.einsum("pkt,ptd->pkd", key_pick, layer_input, preferred_element_type=f32).astype(
        bf16
    )
    key_all = lax.all_gather(key_raw, "seq", axis=1, tiled=True)

    gain_first = first_gain.astype(f32)
    inputs = layer_input.astype(f32)
    unit_first, scale_first = norm_parts(inputs)
    normed_first = (unit_first * gain_first).astype(bf16)
    normed_flat = normed_first.reshape(rows, D)
    own_proj = mm(normed_flat, light_inputs).astype(bf16).reshape(pieces, tokens, 3 * D)
    edge_rows = jnp.concatenate([left_rows, right_rows], axis=1)
    normed_edge = (norm_parts(edge_rows.astype(f32))[0] * gain_first).astype(bf16)
    edge_flat = normed_edge.reshape(pieces * 2 * RADIUS, D)
    edge_proj = mm(edge_flat, light_inputs[:, D:]).astype(bf16)
    edge_proj = edge_proj.reshape(pieces, 2 * RADIUS, 2 * D)

    reach = jnp.stack([seq_rank > 0, seq_rank < n_seq - 1]).astype(jnp.int32)
    light_att = light_attention(reach, own_proj, edge_proj).reshape(rows, D)

    key_slots = n_seq * KCAP
    key_rows_all = key_all.reshape(pieces * key_slots, D)
    normed_keys = (norm_parts(key_rows_all.astype(f32))[0] * gain_first).astype(bf16)
    heavy_pairs = mm(normed_keys, heavy_keyvalue).astype(bf16).reshape(pieces, key_slots, 2 * D)
    key_live = jnp.arange(KCAP, dtype=jnp.int32)[None, None, :] < key_count[:, :, None]
    key_live = key_live.reshape(pieces, 1, key_slots).astype(f32)
    query_rows = (
        jnp.einsum("pqt,ptd->pqd", query_pick, normed_first, preferred_element_type=f32)
        .astype(bf16)
        .reshape(pieces * QCAP, D)
    )
    heavy_query = mm(query_rows, heavy_queries).astype(bf16).reshape(pieces, QCAP, D)
    heavy_att = heavy_attention(heavy_query, heavy_pairs, key_live)
    heavy_spread = (
        jnp.einsum("pqt,pqd->ptd", live_pick, heavy_att, preferred_element_type=f32)
        .astype(bf16)
        .reshape(rows, D)
    )

    middle = (
        inputs.reshape(rows, D) + mm(light_att, light_output) + mm(heavy_spread, heavy_output)
    )
    gain_second = second_gain.astype(f32)
    unit_second, scale_second = norm_parts(middle)
    normed_second = (unit_second * gain_second).astype(bf16)

    slot_of = feed_slot.reshape(1, rows)
    pick = (jnp.arange(slots, dtype=jnp.int32)[:, None] == slot_of).astype(bf16)
    routed = feed_slot.reshape(rows, 1) >= 0
    cot = cotangent.reshape(rows, D)
    gating = jax.nn.sigmoid(
        jnp.sum(normed_second.astype(f32) * router.astype(f32), axis=-1, keepdims=True)
    )
    grad_token = (gating * cot.astype(f32)).astype(bf16)
    feed_in = mm(pick, normed_second).astype(bf16)
    grad_in = mm(pick, grad_token).astype(bf16)

    wide = heavy_gates.shape[1] // 2
    share = wide // 4
    if kernels:
        light_act, grad_light_pre, light_feed, grad_light, back, feed_all, heavy_act, heavy_pre = (
            feed_forward(
                normed_second,
                cot,
                jnp.stack([feed_in, grad_in]),
                light_gates,
                light_down,
                heavy_gates,
                heavy_down,
                n_y,
            )
        )
        feed_rows = feed_all[:, 0].reshape(4 * slots, D)
        grad_rows = feed_all[:, 1].reshape(4 * slots, D)
        heavy_act = heavy_act.reshape(4 * slots, share)
        heavy_pre = heavy_pre.reshape(4 * slots, 2 * share)
        heavy_result, grad_feed_in = back[0], back[1]
    else:
        feed_rows, grad_rows = feed_in, grad_in
        hidden = light_down.shape[0]
        pre = mm(normed_second, light_gates)
        light_act, *grads = glu_and_pull(pre[:, :hidden], pre[:, hidden:], mm_nt(cot, light_down))
        light_act = light_act.astype(bf16)
        grad_light_pre = jnp.concatenate(grads, axis=1).astype(bf16)
        light_feed = mm(light_act, light_down)
        grad_light = mm_nt(grad_light_pre, light_gates)
        pre = mm(feed_in, heavy_gates)
        heavy_act, *grads = glu_and_pull(pre[:, :wide], pre[:, wide:], mm_nt(grad_in, heavy_down))
        heavy_act = heavy_act.astype(bf16)
        heavy_pre = jnp.concatenate(grads, axis=1).astype(bf16)
        heavy_result = mm(heavy_act, heavy_down).astype(bf16)
        grad_feed_in = mm_nt(heavy_pre, heavy_gates).astype(bf16)
    heavy_down_grad = mm_tn(heavy_act, grad_rows).astype(bf16)
    heavy_gates_grad = mm_tn(feed_rows, heavy_pre).astype(bf16)
    light_down_grad = mm_tn(light_act, cot).astype(bf16)
    light_gates_grad = mm_tn(normed_second, grad_light_pre).astype(bf16)

    token_result = mm_tn(pick, heavy_result)
    output = (middle + light_feed + gating * token_result).astype(bf16).reshape(layer_input.shape)
    grad_gating = jnp.sum(cot.astype(f32) * token_result, axis=-1, keepdims=True)
    grad_logit = grad_gating * gating * (1.0 - gating)
    grad_second = (
        grad_light
        + mm_tn(pick, grad_feed_in)
        + grad_logit * router.astype(f32)
    )
    router_grad = jnp.sum(grad_logit * normed_second.astype(f32), axis=0)
    second_gain_grad = jnp.sum(grad_second * unit_second, axis=0)
    grad_middle = cot.astype(f32) + norm_pull(grad_second, middle, scale_second, gain_second)
    grad_mid_low = grad_middle.astype(bf16)

    light_output_grad = mm_tn(light_att, grad_mid_low).astype(bf16)
    grad_light_att = mm_nt(grad_mid_low, light_output).astype(bf16)
    grad_query_rows = (
        jnp.einsum(
            "pqt,ptd->pqd",
            live_pick,
            grad_mid_low.reshape(pieces, tokens, D),
            preferred_element_type=f32,
        )
        .astype(bf16)
        .reshape(pieces * QCAP, D)
    )
    heavy_output_grad = mm_tn(heavy_att.reshape(pieces * QCAP, D), grad_query_rows).astype(bf16)
    grad_heavy_att = mm_nt(grad_query_rows, heavy_output).astype(bf16)

    grad_hq_low, grad_hkv_low = heavy_attention_back(
        heavy_query,
        heavy_pairs,
        key_live,
        grad_heavy_att.reshape(pieces, QCAP, D),
    )
    grad_hq_low = grad_hq_low.reshape(pieces * QCAP, D)
    grad_hkv_low = grad_hkv_low.reshape(pieces * key_slots, 2 * D)
    grad_key_rows = mm_nt(grad_hkv_low, heavy_keyvalue).astype(bf16)
    heavy_keyvalue_grad = mm_tn(normed_keys, grad_hkv_low).astype(bf16)
    heavy_queries_grad = mm_tn(query_rows, grad_hq_low).astype(bf16)

    grad_light_att, grad_key_rows = lax.optimization_barrier((grad_light_att, grad_key_rows))
    grad_key_own = lax.psum_scatter(
        grad_key_rows.reshape(pieces, key_slots, D), "seq", scatter_dimension=1, tiled=True
    )
    grad_light_att = grad_light_att.reshape(pieces, tokens, D)
    if kernels:
        early = [
            (light_gates_grad, True),
            (light_output_grad, True),
            (heavy_gates_grad, True),
            (heavy_queries_grad, True),
            (heavy_keyvalue_grad, True),
        ]
        half = light_gates_grad.shape[1] // 2
        jobs = [
            ("xy", 0, 0, 512, half // 512, 0, 0),
            ("yx", 0, half, 512, half // 512, 0, half),
            ("xy", 1, 0, 384, D // 384, 1, 0),
            ("gates", 2, 0, 256, share // 256, 2, 0),
            ("gates", 2, share, 256, share // 256, 2, wide),
            ("xy", 3, 0, 384, 2, 3, 0),
            ("xy", 4, 0, 512, 3, 4, 0),
        ]
        widths = (2 * half, D, 2 * wide, D, 2 * D)
        *early, grad_own, grad_edge, grad_around = reduce_all(
            early, jobs, widths, n_y, 0, (own_proj, edge_proj, grad_light_att, light_inputs)
        )
    else:
        grad_own, grad_edge = light_attention_back(reach, own_proj, edge_proj, grad_light_att)
        grad_edge_rows = mm_nt(grad_edge.reshape(-1, 2 * D), light_inputs[:, D:]).astype(bf16)
        grad_edge_rows = grad_edge_rows.reshape(pieces, 2 * RADIUS, D)
        from_right = lax.ppermute(
            grad_edge_rows[:, :RADIUS], "seq", [(i + 1, i) for i in range(ends)]
        )
        from_left = lax.ppermute(
            grad_edge_rows[:, RADIUS:], "seq", [(i, i + 1) for i in range(ends)]
        )
        grad_around = jnp.concatenate([from_left, from_right], axis=1)
    grad_own = grad_own.reshape(rows, 3 * D)
    grad_edge = grad_edge.reshape(pieces * 2 * RADIUS, 2 * D)
    grad_hq_rows = mm_nt(grad_hq_low, heavy_queries).astype(bf16).reshape(pieces, QCAP, D)
    grad_first = mm_nt(grad_own, light_inputs).reshape(pieces, tokens, D)
    grad_slots = jnp.concatenate([grad_hq_rows, grad_key_own.astype(bf16)], axis=1)
    both_pick = jnp.concatenate([query_pick, key_pick], axis=1)
    grad_first = (
        grad_first
        + jnp.einsum("pkt,pkd->ptd", both_pick, grad_slots, preferred_element_type=f32)
        + grad_around.astype(f32)
    )
    first_gain_grad = jnp.sum(grad_first * unit_first, axis=(0, 1))
    input_grad = grad_middle.reshape(pieces, tokens, D) + norm_pull(
        grad_first, inputs, scale_first, gain_first
    )
    vectors = jnp.stack([first_gain_grad, second_gain_grad, router_grad])
    devices = n_dp * n_seq
    if kernels:
        lines = vectors.reshape(3, devices, each).transpose(1, 0, 2)
        lines = jnp.pad(lines, ((0, 0), (0, 5), (0, 256 - each))).reshape(devices * 8, 256)
        jobs = (
            ("xy", 0, 0, 384, 1, 0, 0, (0, 2, 0)),
            ("yx", 0, 384, 384, 1, 0, 384, (0, 2, 384)),
            ("xy", 0, D, 384, 2, 0, D, (0, 2, D), (1, 3, 0)),
            ("yx", 0, 2 * D, 384, 2, 0, 2 * D, (0, 2, 2 * D), (1, 3, D)),
            ("xy", 0, 0, 256, 1, 1, 0),
            ("yx", 1, 0, 384, 2, 2, 0),
            ("yx", 2, 0, 384, 2, 3, 0),
            ("down", 3, 0, 128, D // 128, 4, 0),
        )
        factors = (normed_flat, edge_flat, grad_own, grad_edge)
        late = [
            (lines.astype(bf16), True),
            (light_down_grad, True),
            (heavy_output_grad, True),
            (heavy_down_grad, False),
        ]
        late = reduce_all(late, jobs, (3 * D, 256, D, D, D), n_y, 1, (), factors)
        sums = copy_all([*early, *late])
        light_gates_grad, light_output_grad, heavy_gates_grad, heavy_queries_grad = sums[:4]
        heavy_keyvalue_grad, light_inputs_grad, lines = sums[4:7]
        light_down_grad, heavy_output_grad, heavy_down_grad = sums[7:]
        vectors = lines[:3, :each]
    else:
        light_pair_grad = mm_tn(normed_flat, grad_own[:, D:]) + mm_tn(edge_flat, grad_edge)
        light_inputs_grad = jnp.concatenate(
            [mm_tn(normed_flat, grad_own[:, :D]), light_pair_grad], axis=1
        ).astype(bf16)
        light_inputs_grad = reduce_split(light_inputs_grad)
        light_output_grad = reduce_split(light_output_grad)
        heavy_queries_grad = reduce_split(heavy_queries_grad)
        heavy_keyvalue_grad = reduce_split(heavy_keyvalue_grad)
        heavy_output_grad = reduce_split(heavy_output_grad)
        light_gates_grad = reduce_split(light_gates_grad)
        light_down_grad = reduce_split(light_down_grad)
        heavy_gates_grad = reduce_split(heavy_gates_grad)
        heavy_down_grad = reduce_split(heavy_down_grad)
        vectors = reduce_vectors(vectors)
    return (
        output,
        input_grad,
        vectors[0],
        light_inputs_grad,
        light_output_grad,
        heavy_queries_grad,
        heavy_keyvalue_grad,
        heavy_output_grad,
        vectors[1],
        vectors[2],
        light_gates_grad,
        light_down_grad,
        heavy_gates_grad,
        heavy_down_grad,
    )


def solution(mesh):
    rows = P(("dp", "seq"), None)
    line = P(("dp", "seq"))
    tokens = P("dp", "seq", None)
    slots = P("dp", "seq")
    return jax.shard_map(
        per_device,
        mesh=mesh,
        in_specs=(tokens, tokens) + (P(),) * 12 + (slots, slots, slots, P("dp", None), slots),
        out_specs=(tokens, tokens, line) + (rows,) * 5 + (line, line) + (rows,) * 4,
        check_vma=False,
    )
```

```python
import functools
import math
import jax
import jax.numpy as jnp
from jax import lax
from jax.experimental import pallas as pl
from jax.experimental.pallas import tpu as pltpu
from jax.sharding import PartitionSpec as P
D = 768
HL = 8
LHD = 96
HH = 12
HHD = 64
RADIUS = 128
QCAP = 64
KCAP = 64
CORES = 2
DEPTH = 4
MESH = pl.DeviceIdType.MESH
epsilon = 1e-06
bf16 = jnp.bfloat16
f32 = jnp.float32


def dot(left, right, over):
    return lax.dot_general(left, right, (over, ((), ())), preferred_element_type=f32)


def mm(left, right):
    return dot(left, right, ((1,), (0,)))


def mm_nt(left, right):
    return dot(left, right, ((1,), (1,)))


def mm_tn(left, right):
    return dot(left, right, ((0,), (0,)))


class Ring:
    def __init__(self, axis, stride, count):
        self.axis, self.stride, self.count = axis, stride, count
        self.place = (lax.axis_index(axis) // stride) % count

    def shift(self, value, by):
        total = lax.axis_size(self.axis)
        pairs = []
        for i in range(total):
            c = (i // self.stride) % self.count
            pairs.append((i, i + ((c + by) % self.count - c) * self.stride))
        return lax.ppermute(value, self.axis, pairs)

    def scatter_sum(self, value, dim):
        own = lax.dynamic_index_in_dim(value, self.place, dim, keepdims=False)
        total = own.astype(f32)
        for by in range(1, self.count):
            send = lax.dynamic_index_in_dim(
                value, (self.place + by) % self.count, dim, keepdims=False
            )
            total = total + self.shift(send, by).astype(f32)
        return total

    def gather(self, value, dim):
        parts = [value] + [self.shift(value, by) for by in range(1, self.count)]
        return jnp.concatenate(parts, axis=dim)

    def return_sum(self, joined, dim):
        parts = jnp.split(joined, self.count, axis=dim)
        total = parts[0].astype(f32)
        for by in range(1, self.count):
            total = total + self.shift(parts[by], self.count - by).astype(f32)
        return total


def norm_parts(values):
    scale = lax.rsqrt(jnp.mean(values * values, axis=-1, keepdims=True) + epsilon)
    return values * scale, scale


def norm_pull(grad, values, scale, gain):
    weighted = grad * gain
    inner = jnp.mean(weighted * values, axis=-1, keepdims=True)
    return scale * weighted - values * (scale * scale * scale) * inner


def head_windows():
    windows = []
    for h in range(4):
        first, end = h * LHD, (h + 1) * LHD
        windows.append((first // 128 * 128, -(-end // 128) * 128, first, end))
    return windows


def lane_mask(shape, first, end):
    lane = lax.broadcasted_iota(jnp.int32, shape, 1)
    return (lane >= first) & (lane < end)


def join_heads(parts):
    lane = lax.broadcasted_iota(jnp.int32, (parts[0].shape[0], 128), 1)
    return jnp.concatenate(
        [
            jnp.where(lane < 96, parts[0], parts[1][:, :128]),
            jnp.where(lane < 64, parts[1][:, 128:], parts[2][:, :128]),
            jnp.where(lane < 32, parts[2][:, 128:], parts[3]),
        ],
        axis=1,
    )


def light_kernel(ends_ref, own_ref, edge_ref, out_ref):
    half = RADIUS
    factor = LHD ** (-0.5)
    for block in range(2):
        rows = slice(block * half, (block + 1) * half)
        row = lax.broadcasted_iota(jnp.int32, (half, 2 * half), 0)
        col = lax.broadcasted_iota(jnp.int32, (half, 2 * half), 1)
        keep_own = col <= row + half if block == 0 else col >= row
        row, col = row[:, :half], col[:, :half]
        keep_edge = (col >= row if block == 0 else col <= row) & (ends_ref[block] > 0)
        for group in range(2):
            mixed = []
            for a, b, first, end in head_windows():
                lanes = slice(group * 384 + a, group * 384 + b)
                keys = slice(D + lanes.start, D + lanes.stop)
                values = slice(2 * D + lanes.start, 2 * D + lanes.stop)
                query = own_ref[0, rows, lanes]
                query = jnp.where(
                    lane_mask(query.shape, first - a, end - a), query, jnp.zeros_like(query)
                )
                s_own = jnp.where(keep_own, mm_nt(query, own_ref[0, :, keys]), -1e30)
                s_edge = jnp.where(keep_edge, mm_nt(query, edge_ref[0, rows, lanes]), -1e30)
                top = jnp.maximum(
                    jnp.max(s_own, axis=1, keepdims=True), jnp.max(s_edge, axis=1, keepdims=True)
                )
                e_own = jnp.exp((s_own - top) * factor)
                e_edge = jnp.exp((s_edge - top) * factor)
                total = jnp.sum(e_own, axis=1, keepdims=True) + jnp.sum(
                    e_edge, axis=1, keepdims=True
                )
                mix = mm(e_own.astype(bf16), own_ref[0, :, values])
                mix += mm(
                    e_edge.astype(bf16), edge_ref[0, rows, slice(D + lanes.start, D + lanes.stop)]
                )
                mixed.append(mix * (1.0 / total))
            out_ref[0, rows, group * 384 : (group + 1) * 384] = join_heads(mixed).astype(bf16)


def light_attention(ends, own, edge):
    pieces, tokens = own.shape[:2]
    return pl.pallas_call(
        light_kernel,
        out_shape=jax.ShapeDtypeStruct((pieces, tokens, D), bf16),
        grid_spec=pltpu.PrefetchScalarGridSpec(
            num_scalar_prefetch=1,
            grid=(pieces,),
            in_specs=[
                pl.BlockSpec((1, tokens, 3 * D), lambda p, e: (p, 0, 0)),
                pl.BlockSpec((1, 2 * RADIUS, 2 * D), lambda p, e: (p, 0, 0)),
            ],
            out_specs=pl.BlockSpec((1, tokens, D), lambda p, e: (p, 0, 0)),
        ),
        compiler_params=pltpu.CompilerParams(vmem_limit_bytes=32 << 20),
        cost_estimate=pl.CostEstimate(
            flops=pieces * HL * tokens * 384 * 256 * 4,
            bytes_accessed=pieces * (tokens * 4 * D + 2 * RADIUS * 2 * D) * 2,
            transcendentals=pieces * HL * tokens * 384,
        ),
        name="light_attention",
    )(ends, own, edge)


def light_back_unit(reach, groups, own_ref, edge_ref, grad_ref, own_out, edge_out):
    half = RADIUS
    factor = LHD ** (-0.5)
    for group in groups:
        dk_own, dv_own = [None] * 4, [None] * 4
        for block in range(2):
            rows = slice(block * half, (block + 1) * half)
            key = lax.broadcasted_iota(jnp.int32, (2 * half, half), 0)
            que = lax.broadcasted_iota(jnp.int32, (2 * half, half), 1)
            keep_own = key <= que + half if block == 0 else key >= que
            key, que = key[:half], que[:half]
            keep_edge = (key >= que if block == 0 else key <= que) & reach[block]
            dq, dk_edge, dv_edge = [], [], []
            for h, (a, b, first, end) in enumerate(head_windows()):
                lanes = slice(group * 384 + a, group * 384 + b)
                after = slice(D + lanes.start, D + lanes.stop)
                last = slice(2 * D + lanes.start, 2 * D + lanes.stop)
                mask = lane_mask((half, b - a), first - a, end - a)
                query = own_ref[0, rows, lanes]
                query = jnp.where(mask, query, jnp.zeros_like(query))
                grad = grad_ref[0, rows, lanes]
                grad = jnp.where(mask, grad, jnp.zeros_like(grad))
                k_own, k_edge = own_ref[0, :, after], edge_ref[0, rows, lanes]
                v_own, v_edge = own_ref[0, :, last], edge_ref[0, rows, after]
                s_own = jnp.where(keep_own, mm_nt(k_own, query), -1e30)
                s_edge = jnp.where(keep_edge, mm_nt(k_edge, query), -1e30)
                top = jnp.maximum(
                    jnp.max(s_own, axis=0, keepdims=True), jnp.max(s_edge, axis=0, keepdims=True)
                )
                e_own = jnp.exp((s_own - top) * factor)
                e_edge = jnp.exp((s_edge - top) * factor)
                total = jnp.sum(e_own, axis=0, keepdims=True) + jnp.sum(
                    e_edge, axis=0, keepdims=True
                )
                scale = 1.0 / total
                p_own, p_edge = e_own * scale, e_edge * scale
                g_own, g_edge = mm_nt(v_own, grad), mm_nt(v_edge, grad)
                inner = jnp.sum(p_own * g_own, axis=0, keepdims=True) + jnp.sum(
                    p_edge * g_edge, axis=0, keepdims=True
                )
                d_own = (p_own * (g_own - inner)).astype(bf16)
                d_edge = (p_edge * (g_edge - inner)).astype(bf16)
                dv = mm(p_own.astype(bf16), grad)
                dk = mm(d_own, query)
                dv_own[h] = dv if block == 0 else dv_own[h] + dv
                dk_own[h] = dk if block == 0 else dk_own[h] + dk
                dv_edge.append(mm(p_edge.astype(bf16), grad))
                dk_edge.append(mm(d_edge, query) * factor)
                dq.append((mm_tn(d_own, k_own) + mm_tn(d_edge, k_edge)) * factor)
            at = slice(group * 384, (group + 1) * 384)
            at_v = slice(D + at.start, D + at.stop)
            own_out[0, rows, at] = join_heads(dq).astype(bf16)
            edge_out[0, rows, at] = join_heads(dk_edge).astype(bf16)
            edge_out[0, rows, at_v] = join_heads(dv_edge).astype(bf16)
        at_w = slice(2 * D + at.start, 2 * D + at.stop)
        own_out[0, :, at_v] = (join_heads(dk_own) * factor).astype(bf16)
        own_out[0, :, at_w] = join_heads(dv_own).astype(bf16)


def light_back_kernel(ends_ref, *refs):
    light_back_unit((ends_ref[0] > 0, ends_ref[1] > 0), range(2), *refs)


def light_attention_back(ends, own, edge, grad):
    pieces, tokens = own.shape[:2]
    return pl.pallas_call(
        light_back_kernel,
        out_shape=[
            jax.ShapeDtypeStruct((pieces, tokens, 3 * D), bf16),
            jax.ShapeDtypeStruct((pieces, 2 * RADIUS, 2 * D), bf16),
        ],
        grid_spec=pltpu.PrefetchScalarGridSpec(
            num_scalar_prefetch=1,
            grid=(pieces,),
            in_specs=[
                pl.BlockSpec((1, tokens, 3 * D), lambda p, e: (p, 0, 0)),
                pl.BlockSpec((1, 2 * RADIUS, 2 * D), lambda p, e: (p, 0, 0)),
                pl.BlockSpec((1, tokens, D), lambda p, e: (p, 0, 0)),
            ],
            out_specs=[
                pl.BlockSpec((1, tokens, 3 * D), lambda p, e: (p, 0, 0)),
                pl.BlockSpec((1, 2 * RADIUS, 2 * D), lambda p, e: (p, 0, 0)),
            ],
        ),
        compiler_params=pltpu.CompilerParams(vmem_limit_bytes=32 << 20),
        cost_estimate=pl.CostEstimate(
            flops=pieces * HL * tokens * 384 * 256 * 10,
            bytes_accessed=pieces * (tokens * 7 * D + 2 * RADIUS * 4 * D) * 2,
            transcendentals=pieces * HL * tokens * 384,
        ),
        name="light_attention_back",
    )(ends, own, edge, grad)


def spread_heads(value):
    tall = jnp.concatenate([value] * 4, axis=0)
    row = lax.broadcasted_iota(jnp.int32, tall.shape, 0) // QCAP
    lane = lax.broadcasted_iota(jnp.int32, tall.shape, 1) // HHD
    return jnp.where(row == lane, tall, jnp.zeros_like(tall))


def fold_heads(tall):
    lane = lax.broadcasted_iota(jnp.int32, (QCAP, 4 * HHD), 1) // HHD
    total = tall[:QCAP]
    for r in range(1, 4):
        total = jnp.where(lane == r, tall[r * QCAP : (r + 1) * QCAP], total)
    return total


def heavy_kernel(query_ref, pair_ref, live_ref, out_ref):
    factor = HHD ** (-0.5)
    keep = live_ref[0] > 0
    for group in range(HH // 4):
        lanes = slice(group * 256, (group + 1) * 256)
        query = spread_heads(query_ref[0, :, lanes])
        scores = jnp.where(keep, mm_nt(query, pair_ref[0, :, lanes]), -1e30)
        top = jnp.max(scores, axis=1, keepdims=True)
        raised = jnp.exp((scores - top) * factor)
        total = jnp.sum(raised, axis=1, keepdims=True)
        mix = mm(raised.astype(bf16), pair_ref[0, :, D + lanes.start : D + lanes.stop])
        out_ref[0, :, lanes] = fold_heads(mix * (1.0 / total)).astype(bf16)


def heavy_attention(query, pairs, live):
    pieces, slots = pairs.shape[:2]
    return pl.pallas_call(
        heavy_kernel,
        out_shape=jax.ShapeDtypeStruct((pieces, QCAP, D), bf16),
        grid=(pieces,),
        in_specs=[
            pl.BlockSpec((1, QCAP, D), lambda p: (p, 0, 0)),
            pl.BlockSpec((1, slots, 2 * D), lambda p: (p, 0, 0)),
            pl.BlockSpec((1, 1, slots), lambda p: (p, 0, 0)),
        ],
        out_specs=pl.BlockSpec((1, QCAP, D), lambda p: (p, 0, 0)),
        compiler_params=pltpu.CompilerParams(vmem_limit_bytes=32 << 20),
        cost_estimate=pl.CostEstimate(
            flops=pieces * 3 * 4 * 256 * 256 * slots,
            bytes_accessed=pieces * (slots + QCAP) * 2 * D * 2,
            transcendentals=pieces * HH * QCAP * slots,
        ),
        name="heavy_attention",
    )(query, pairs, live)


def heavy_back_kernel(query_ref, pair_ref, live_ref, grad_ref, query_out, pair_out):
    factor = HHD ** (-0.5)
    slots = pair_ref.shape[1]
    keep = jnp.broadcast_to(live_ref[0], (128, slots)).T[:, :1] > 0
    for group in range(HH // 4):
        lanes = slice(group * 256, (group + 1) * 256)
        after = slice(D + lanes.start, D + lanes.stop)
        query = spread_heads(query_ref[0, :, lanes])
        grad = spread_heads(grad_ref[0, :, lanes])
        keys = pair_ref[0, :, lanes]
        scores = jnp.where(keep, mm_nt(keys, query), -1e30)
        top = jnp.max(scores, axis=0, keepdims=True)
        raised = jnp.exp((scores - top) * factor)
        probs = raised * (1.0 / jnp.sum(raised, axis=0, keepdims=True))
        grad_probs = mm_nt(pair_ref[0, :, after], grad)
        inner = jnp.sum(probs * grad_probs, axis=0, keepdims=True)
        grad_scores = (probs * (grad_probs - inner)).astype(bf16)
        pair_out[0, :, after] = mm(probs.astype(bf16), grad).astype(bf16)
        pair_out[0, :, lanes] = (mm(grad_scores, query) * factor).astype(bf16)
        query_out[0, :, lanes] = (fold_heads(mm_tn(grad_scores, keys)) * factor).astype(bf16)


def heavy_attention_back(query, pairs, live, grad):
    pieces, slots = pairs.shape[:2]
    return pl.pallas_call(
        heavy_back_kernel,
        out_shape=[
            jax.ShapeDtypeStruct((pieces, QCAP, D), bf16),
            jax.ShapeDtypeStruct((pieces, slots, 2 * D), bf16),
        ],
        grid=(pieces,),
        in_specs=[
            pl.BlockSpec((1, QCAP, D), lambda p: (p, 0, 0)),
            pl.BlockSpec((1, slots, 2 * D), lambda p: (p, 0, 0)),
            pl.BlockSpec((1, 1, slots), lambda p: (p, 0, 0)),
            pl.BlockSpec((1, QCAP, D), lambda p: (p, 0, 0)),
        ],
        out_specs=[
            pl.BlockSpec((1, QCAP, D), lambda p: (p, 0, 0)),
            pl.BlockSpec((1, slots, 2 * D), lambda p: (p, 0, 0)),
        ],
        compiler_params=pltpu.CompilerParams(vmem_limit_bytes=32 << 20),
        cost_estimate=pl.CostEstimate(
            flops=pieces * 3 * 10 * 256 * 256 * slots,
            bytes_accessed=pieces * (2 * slots + 2 * QCAP) * 2 * D * 2,
            transcendentals=pieces * HH * QCAP * slots,
        ),
        name="heavy_attention_back",
    )(query, pairs, live, grad)


def glu_and_pull(gate, up, grad):
    slope = 0.7978845608028654
    square = gate * gate
    curve = jnp.tanh(gate * (slope + (slope * 0.044715) * square))
    half = 0.5 + 0.5 * curve
    gelu = gate * half
    bend = (0.5 * gate) * (1.0 - curve * curve) * (slope + (3 * slope * 0.044715) * square)
    return gelu * up, grad * up * (half + bend), grad * gelu


def feed_kernel(
    n_y,
    normed_in,
    cot_in,
    own_rows,
    gates_in,
    down_in,
    gates_heavy,
    down_heavy,
    act_to,
    pre_to,
    feed_to,
    grad_to,
    back_out,
    rows_to,
    heavy_act_to,
    heavy_pre_to,
    normed,
    cot,
    gates,
    down,
    act_out,
    pre_out,
    feed_out,
    grad_out,
    heavy_act_out,
    heavy_pre_out,
    wide,
    tall,
    rows,
    part,
    from_core,
    to_y,
    from_y,
    in_sem,
    out_sem,
    weight_sem,
    rows_rsem,
    rows_ssem,
    core_rsem,
    core_ssem,
    y_rsem,
    y_ssem,
):
    dp, seq = lax.axis_index("dp"), lax.axis_index("seq")
    c, y = dp % CORES, seq % n_y
    me = c * n_y + y
    to_core, to_beside = (dp + 1 - 2 * c, seq), (dp, seq + 1 - 2 * y)
    share = tall.shape[0]
    total = gates_heavy.shape[1] // 2
    inputs = [
        pltpu.make_async_copy(src, dst, in_sem.at[i])
        for i, (src, dst) in enumerate(
            (
                (own_rows, rows.at[me]),
                (gates_in, gates),
                (down_in, down),
                (normed_in, normed),
                (cot_in, cot),
            )
        )
    ]
    for load in inputs:
        load.start()
    loads = [
        pltpu.make_async_copy(
            gates_heavy.at[:, pl.ds(pl.multiple_of(i * total + me * share, share), share)],
            wide.at[i],
            weight_sem.at[i],
        )
        for i in range(2)
    ]
    loads.append(
        pltpu.make_async_copy(
            down_heavy.at[pl.ds(pl.multiple_of(me * share, share), share)], tall, weight_sem.at[2]
        )
    )
    for load in loads:
        load.start()
    barrier = pltpu.get_barrier_semaphore()
    for peer in (to_core, to_beside):
        pl.semaphore_signal(barrier, inc=1, device_id=peer, device_id_type=MESH)
    pl.semaphore_wait(barrier, 2)

    def copy(src, dst, ssem, rsem, peer):
        return pltpu.make_async_remote_copy(
            src_ref=src,
            dst_ref=dst,
            send_sem=ssem,
            recv_sem=rsem,
            device_id=peer,
            device_id_type=MESH,
        )

    def rows_copy(slot, i, peer):
        return copy(rows.at[slot], rows.at[slot], rows_ssem.at[i], rows_rsem.at[slot], peer)

    inputs[0].wait()
    rows_copy(me, 0, to_beside).start()
    rows_copy(me, 1, to_core).start()
    beside, diagonal, other = c * n_y + 1 - y, (1 - c) * n_y + 1 - y, (1 - c) * n_y + y
    hidden = down.shape[0]
    step = 256
    for load in inputs[1:]:
        load.wait()
    outputs = (
        (act_out, act_to),
        (pre_out, pre_to),
        (feed_out, feed_to),
        (grad_out, grad_to),
        (heavy_act_out, heavy_act_to),
        (heavy_pre_out, heavy_pre_to),
        (rows, rows_to),
    )

    @pl.loop(0, normed.shape[0] // step)
    def _(t):
        at = pl.ds(pl.multiple_of(t * step, step), step)
        gate = mm(normed[at], gates[:, :hidden])
        up = mm(normed[at], gates[:, hidden:])
        act, grad_gate, grad_up = glu_and_pull(gate, up, mm_nt(cot[at], down[...]))
        act = act.astype(bf16)
        grad_gate = grad_gate.astype(bf16)
        grad_up = grad_up.astype(bf16)
        act_out[at] = act
        pre_out[at, :hidden] = grad_gate
        pre_out[at, hidden:] = grad_up
        feed_out[at] = mm(act, down[...])
        grad_out[at] = mm_nt(grad_gate, gates[:, :hidden]) + mm_nt(grad_up, gates[:, hidden:])
        for i, (src, dst) in enumerate(outputs[:4]):
            pltpu.make_async_copy(src.at[at], dst.at[at], out_sem.at[i]).start()

    for load in loads:
        load.wait()
    rows_copy(beside, 2, to_core).wait_recv()
    rows_copy(beside, 2, to_core).start()

    @pl.loop(0, 4)
    def _(i):
        first, second, third = i == 0, i == 1, i == 2
        slot = jnp.where(
            first, me, jnp.where(second, diagonal, jnp.where(third, beside, other))
        )

        @pl.when(second)
        def _():
            rows_copy(diagonal, 0, to_core).wait_recv()

        @pl.when(i == 3)
        def _():
            rows_copy(other, 0, to_core).wait_recv()

        value, grad = rows[slot, 0], rows[slot, 1]
        gate, up = mm(value, wide[0]), mm(value, wide[1])
        act, grad_gate, grad_up = glu_and_pull(gate, up, mm_nt(grad, tall[...]))
        act = act.astype(bf16)
        grad_gate = grad_gate.astype(bf16)
        grad_up = grad_up.astype(bf16)
        heavy_act_out[slot] = act
        heavy_pre_out[slot, :, :share] = grad_gate
        heavy_pre_out[slot, :, share:] = grad_up
        for n, (src, dst) in enumerate(outputs[4:6]):
            pltpu.make_async_copy(src.at[slot], dst.at[slot], out_sem.at[4 + n]).start()
        part[i, 0] = mm(act, tall[...]).astype(bf16)
        part[i, 1] = (mm_nt(grad_gate, wide[0]) + mm_nt(grad_up, wide[1])).astype(bf16)

        @pl.when(second)
        def _():
            copy(part.at[1], from_core.at[0], core_ssem.at[0], core_rsem.at[0], to_core).start()

        @pl.when(third)
        def _():
            copy(part.at[1], from_core.at[0], core_ssem.at[0], core_rsem.at[0], to_core).wait_recv()
            to_y[...] = part[2] + from_core[0]
            copy(to_y, from_y, y_ssem, y_rsem, to_beside).start()

        @pl.when(i == 3)
        def _():
            copy(part.at[3], from_core.at[1], core_ssem.at[1], core_rsem.at[1], to_core).start()

    pltpu.make_async_copy(rows, rows_to, out_sem.at[6]).start()
    copy(part.at[3], from_core.at[1], core_ssem.at[1], core_rsem.at[1], to_core).wait()
    copy(to_y, from_y, y_ssem, y_rsem, to_beside).wait()
    sums = part[0].astype(f32) + from_core[1].astype(f32) + from_y[...].astype(f32)
    back_out[...] = sums.astype(bf16)
    copy(part.at[1], from_core.at[0], core_ssem.at[0], core_rsem.at[0], to_core).wait_send()
    for i, slot in enumerate((me, me, beside)):
        rows_copy(slot, i, to_core).wait_send()
    for i, (src, dst) in enumerate(outputs):
        pltpu.make_async_copy(src, dst, out_sem.at[i]).wait()


def feed_forward(normed, cot, own_rows, gates, down, gates_heavy, down_heavy, n_y):
    count, hidden = normed.shape[0], down.shape[0]
    slots = own_rows.shape[1]
    share = down_heavy.shape[0] // 4
    here, anywhere = pl.BlockSpec(memory_space=pltpu.VMEM), pl.BlockSpec(memory_space=pl.ANY)
    pair = (2, slots, D)
    return pl.pallas_call(
        functools.partial(feed_kernel, n_y),
        out_shape=[
            jax.ShapeDtypeStruct((count, hidden), bf16),
            jax.ShapeDtypeStruct((count, 2 * hidden), bf16),
            jax.ShapeDtypeStruct((count, D), f32),
            jax.ShapeDtypeStruct((count, D), f32),
            jax.ShapeDtypeStruct(pair, bf16),
            jax.ShapeDtypeStruct((4,) + pair, bf16),
            jax.ShapeDtypeStruct((4, slots, share), bf16),
            jax.ShapeDtypeStruct((4, slots, 2 * share), bf16),
        ],
        in_specs=[anywhere] * 7,
        out_specs=[anywhere] * 4 + [here] + [anywhere] * 3,
        scratch_shapes=[
            pltpu.VMEM((count, D), bf16),
            pltpu.VMEM((count, D), bf16),
            pltpu.VMEM((D, 2 * hidden), bf16),
            pltpu.VMEM((hidden, D), bf16),
            pltpu.VMEM((count, hidden), bf16),
            pltpu.VMEM((count, 2 * hidden), bf16),
            pltpu.VMEM((count, D), f32),
            pltpu.VMEM((count, D), f32),
            pltpu.VMEM((4, slots, share), bf16),
            pltpu.VMEM((4, slots, 2 * share), bf16),
            pltpu.VMEM((2, D, share), bf16),
            pltpu.VMEM((share, D), bf16),
            pltpu.VMEM((4,) + pair, bf16),
            pltpu.VMEM((4,) + pair, bf16),
            pltpu.VMEM((2,) + pair, bf16),
            pltpu.VMEM(pair, bf16),
            pltpu.VMEM(pair, bf16),
            pltpu.SemaphoreType.DMA((5,)),
            pltpu.SemaphoreType.DMA((7,)),
            pltpu.SemaphoreType.DMA((3,)),
            pltpu.SemaphoreType.DMA((4,)),
            pltpu.SemaphoreType.DMA((3,)),
            pltpu.SemaphoreType.DMA((2,)),
            pltpu.SemaphoreType.DMA((2,)),
            pltpu.SemaphoreType.DMA,
            pltpu.SemaphoreType.DMA,
        ],
        compiler_params=pltpu.CompilerParams(
            collective_id=2, has_side_effects=True, vmem_limit_bytes=60 << 20
        ),
        cost_estimate=pl.CostEstimate(
            flops=12 * count * D * hidden + 48 * slots * D * share,
            bytes_accessed=30 << 20,
            transcendentals=count * hidden + 4 * slots * share,
        ),
        name="feed_forward",
    )(normed, cot, own_rows, gates, down, gates_heavy, down_heavy)


def reduce_kernel(jobs, counts, n_y, *refs):
    n_sources, n_outs, light, factors = counts
    refs = list(refs)

    def take(count):
        taken = refs[:count]
        del refs[:count]
        return taken

    sources = take(n_sources)
    given = take(4 if light else factors)
    outs = take(n_outs)
    made = take(3 if light else 0)
    held = []
    for job in jobs:
        names = SCRATCH[job[0]] + (("full",) if len(job) > 7 else ())
        held.append(dict(zip(names, take(len(names)))))
    kinds = [job[0] for job in jobs]
    dp, seq = lax.axis_index("dp"), lax.axis_index("seq")
    x, c = dp // CORES, dp % CORES
    z, y = seq // n_y, seq % n_y
    z_high, z_low = z // 2, z % 2
    group = c * n_y + y

    def device(x=x, c=c, z=z, y=y):
        return (x * CORES + c, z * n_y + y)

    to = {
        "core": device(c=1 - c),
        "x": device(x=1 - x),
        "y": device(y=1 - y),
        "low": device(z=z_high * 2 + 1 - z_low),
        "high": device(z=(1 - z_high) * 2 + z_low),
    }
    owner = (group, x * DEPTH + z)
    origin = device(x=seq // DEPTH, c=dp // n_y, z=seq % DEPTH, y=dp % n_y)
    moved = jnp.logical_or(owner[0] != dp, owner[1] != seq)

    barrier = pltpu.get_barrier_semaphore()

    def greet(peer):
        pl.semaphore_signal(barrier, inc=1, device_id=peer, device_id_type=MESH)

    for peer in to.values():
        greet(peer)
    expected = len(to)
    if "gates" in kinds:
        greet(device(c=1 - c, y=1 - y))
        expected += 1
    pairs = []
    if "down" in kinds:
        pairs += [(moved, owner), (moved, origin)]
    if light:
        pairs += [(seq > 0, (dp, seq - 1)), (seq < DEPTH * n_y - 1, (dp, seq + 1))]
    for present, peer in pairs:

        @pl.when(present)
        def _():
            greet(peer)

    for present, _ in pairs:
        expected = expected + jnp.where(present, 1, 0)
    pl.semaphore_wait(barrier, expected)

    def copy(src, dst, a, stage, k, peer):
        return pltpu.make_async_remote_copy(
            src_ref=src,
            dst_ref=dst,
            send_sem=held[a]["ssem"].at[stage],
            recv_sem=held[a]["rsem"].at[stage, k],
            device_id=peer,
            device_id_type=MESH,
        )

    def send(src, name, k, a, place=None, slot=None):
        dst = held[a][name].at[k] if slot is None else held[a][name].at[k, slot]
        copy(src, dst, a, STAGES[name], k, place).start()

    def arrived(name, a, k):
        buffer = held[a][name].at[k]
        copy(buffer, buffer, a, STAGES[name], k, to["core"]).wait_recv()

    def columns(a, k):
        start, width = jobs[a][2:4]
        return pl.ds(start + k * width, width)

    if factors:
        *kept, factor_sem = refs
        wanted, fetched = [], set()
        for a, job in enumerate(jobs):
            for left, right, start in job[7:]:
                for k in range(job[4]):
                    wanted.append((k, a, left, right, pl.ds(start + k * job[3], job[3])))
        fetches = {}
        for k, a, left, right, cols in sorted(wanted, key=lambda w: w[:2]):
            for key, part in (((left,), slice(None)), ((right, cols.start), cols)):
                if key not in fetches:
                    src, dst = given[key[0]].at[:, part], kept[key[0]].at[:, part]
                    fetches[key] = pltpu.make_async_copy(src, dst, factor_sem.at[len(fetches)])
                    fetches[key].start()

    def produce(a, k):
        width, height = jobs[a][3], held[a]["full"].shape[-2]
        total = 0.0
        for left, right, start in jobs[a][7:]:
            for key in ((left,), (right, start + k * width)):
                if key not in fetched:
                    fetched.add(key)
                    fetches[key].wait()
            cols = slice(start + k * width, start + (k + 1) * width)
            total = total + mm_tn(kept[left][...], kept[right][:, cols])
        at = 0
        for i in range(2):
            for j in range(CORES):
                for m in range(DEPTH):
                    for n in range(n_y):
                        rows = total[at * height : (at + 1) * height]
                        held[a]["full"][k, i, j, m, n] = rows.astype(bf16)
                        at += 1

    def local(a, k):
        whole, cols = sources[jobs[a][1]], columns(a, k)
        if kinds[a] in ("xy", "yx"):
            part = whole.at[:, c, :, :, :, cols]
        else:
            part = whole.at[x, :, :, :, :, cols]
        return pltpu.make_async_copy(part, held[a]["own"].at[k], held[a]["lsem"].at[k])

    def begin(a, k):
        if len(jobs[a]) > 7:
            produce(a, k)
            send(held[a]["full"].at[k, :, 1 - c], "core", k, a, to["core"])
            return
        whole, cols = sources[jobs[a][1]], columns(a, k)
        local(a, k).start()
        if kinds[a] in ("xy", "yx"):
            send(whole.at[:, 1 - c, :, :, :, cols], "core", k, a, to["core"])
        else:
            send(whole.at[1 - x, :, :, :, :, cols], "xx", k, a, to["x"])

    def first(a, k):
        h, kind = held[a], kinds[a]
        own = h["own"]
        made_here = "full" in h
        if not made_here:
            local(a, k).wait()
        if kind not in ("xy", "yx"):
            return
        arrived("core", a, k)

        @pl.loop(0, 2 * DEPTH)
        def _(i):
            for j in range(n_y):
                at = (k, i // DEPTH, i % DEPTH, j)
                mine = h["full"][at[:2] + (c,) + at[2:]] if made_here else own[at]
                own[at] = mine + h["core"][at]

        if kind == "xy":
            send(own.at[k, 1 - x], "xx", k, a, to["x"])
        else:
            send(own.at[k, :, :, 1 - y], "yy", k, a, to["y"])

    def second(a, k):
        h, kind = held[a], kinds[a]
        own = h["own"]
        if kind == "xy":
            arrived("xx", a, k)

            @pl.loop(0, DEPTH)
            def _(i):
                for j in range(n_y):
                    at = (k, x, i, j)
                    own[at] = own[at] + h["xx"][k, i, j]

            send(own.at[k, x, :, 1 - y], "yy", k, a, to["y"])
        elif kind == "yx":
            arrived("yy", a, k)

            @pl.loop(0, DEPTH)
            def _(i):
                for j in range(2):
                    at = (k, j, i, y)
                    own[at] = own[at] + h["yy"][k, j, i]

            send(own.at[k, 1 - x, :, y], "xx", k, a, to["x"])

    def third(a, k):
        h, kind = held[a], kinds[a]
        own = h["own"]
        if kind in ("xy", "yx"):
            name = "yy" if kind == "xy" else "xx"
            arrived(name, a, k)

            @pl.loop(0, DEPTH)
            def _(i):
                at = (k, x, i, y)
                own[at] = own[at] + h[name][k, i]

            for high in range(2):
                send(own.at[k, x, high * 2 + 1 - z_low, y], "za", k, a, to["low"], high)
        else:
            arrived("xx", a, k)

            @pl.loop(0, DEPTH)
            def _(i):
                for g in range(own.shape[1]):
                    for j in range(own.shape[3]):
                        at = (k, g, i, j)
                        own[at] = own[at] + h["xx"][at]

            for high in range(2):
                send(own.at[k, :, high * 2 + 1 - z_low], "za", k, a, to["low"], high)

    def fourth(a, k):
        h, kind = held[a], kinds[a]
        own = h["own"]
        arrived("za", a, k)
        if kind in ("xy", "yx"):
            for high in range(2):
                at = (k, x, high * 2 + z_low, y)
                own[at] = own[at] + h["za"][k, high]
            send(own.at[k, x, (1 - z_high) * 2 + z_low, y], "zb", k, a, to["high"])
        else:

            @pl.loop(0, own.shape[1])
            def _(g):
                for j in range(own.shape[3]):
                    for high in range(2):
                        at = (k, g, high * 2 + z_low, j)
                        own[at] = own[at] + h["za"][k, high, g, j]

            send(own.at[k, :, (1 - z_high) * 2 + z_low], "zb", k, a, to["high"])

    def fifth(a, k):
        h = held[a]
        kind, _, _, width, _, out, start = jobs[a][:7]
        own = h["own"]
        arrived("zb", a, k)
        if kind in ("xy", "yx"):
            total = own[k, x, z, y].astype(f32) + h["zb"][k].astype(f32)
            outs[out][:, start + k * width : start + (k + 1) * width] = total
        elif kind == "down":
            h["sum"][k] = own[k, 0, z, 0] + h["zb"][k, 0, 0]

            @pl.when(moved)
            def _():
                send(h["sum"].at[k], "dd", k, a, owner)

            @pl.when(jnp.logical_not(moved))
            def _():
                h["dd"][k] = h["sum"][k]
        else:

            @pl.loop(0, CORES)
            def _(g):
                for j in range(n_y):
                    h["sum"][k, g * n_y + j] = own[k, g, z, j] + h["zb"][k, g, j]

            h["dd"][k, group] = h["sum"][k, group]
            for g, j in ((1 - c, y), (c, 1 - y), (1 - c, 1 - y)):
                send(h["sum"].at[k, g * n_y + j], "dd", k, a, device(c=g, y=j), group)

    def last(a, k):
        h = held[a]
        kind, _, _, width, chunks, out, start = jobs[a][:7]
        if kind == "gates":
            part = h["dd"].at[k, pl.ds(0, 3)]
            copy(part, part, a, STAGES["dd"], k, to["core"]).wait_recv()
            for g in range(4):
                at = start + (g * chunks + k) * width
                outs[out][:, at : at + width] = h["dd"][k, g].astype(f32)
        elif kind == "down":

            @pl.when(moved)
            def _():
                arrived("dd", a, k)

            outs[out][:, start + k * width : start + (k + 1) * width] = h["dd"][k].astype(f32)

    lists = {"all": [], "rest": []}
    for a, job in enumerate(jobs):
        lists["all" if job[0] in ("xy", "yx") else "rest"].append([(a, k) for k in range(job[4])])
    stages = (begin, first, second, third, fourth, fifth, last)
    longest = max(len(interleave(parts)) for parts in lists.values())
    events = []
    for name, parts in lists.items():
        order = interleave(parts)
        order.sort(key=lambda what: len(jobs[what[0]]) > 7)
        for i, what in enumerate(order):
            for stage, lag in zip(stages, LAGS[name]):
                if factors and stage is begin and len(jobs[what[0]]) == 7:
                    lag = -20
                events.append((i * longest / len(order) + lag, len(events), stage, what))
    if light:
        edges_in = made[2]
        *inner, weights, ready, landed, load_sem, weight_sem, out_sem, edge_ssem, edge_rsem = refs
        edge_out = inner[4]
        pieces = edge_out.shape[0]
        reach = (seq > 0, seq < DEPTH * n_y - 1)

        def load(i, p):
            return pltpu.make_async_copy(given[i].at[p], inner[i].at[p], load_sem.at[i, p])

        def store(i, p):
            src, dst = inner[3 + i], made[i]
            if p is not None:
                src, dst = src.at[p], dst.at[p]
            return pltpu.make_async_copy(src, dst, out_sem.at[i])

        for p in range(pieces):
            for i in range(3):
                load(i, p).start()
        load_weights = pltpu.make_async_copy(given[3], weights, weight_sem)
        load_weights.start()

        def edge_copy(side, p):
            src = ready.at[p, pl.ds(side * RADIUS, RADIUS)]
            dst = landed.at[p, pl.ds((1 - side) * RADIUS, RADIUS)]
            return pltpu.make_async_remote_copy(
                src_ref=src,
                dst_ref=dst,
                send_sem=edge_ssem.at[side],
                recv_sem=edge_rsem.at[1 - side, p],
                device_id=(dp, seq - 1 + 2 * side),
                device_id_type=MESH,
            )

        def unit(p, g):
            if g == 0:
                for i in range(3):
                    load(i, p).wait()
            light_back_unit(reach, (g,), *[ref.at[pl.ds(p, 1)] for ref in inner])
            if g == 1:
                for i in range(2):
                    store(i, p).start()
                if p == 0:
                    load_weights.wait()
                rows = mm_nt(edge_out[p], weights[:, D:])
                ready[p] = rows.astype(bf16)
                for side in range(2):

                    @pl.when(reach[side])
                    def _():
                        edge_copy(side, p).start()

        for p in range(pieces):
            for g in range(2):
                events.append(((2 * p + g) * 1.2, len(events), unit, (p, g)))
    for _, _, stage, what in sorted(events, key=lambda e: e[:2]):
        stage(*what)

    if light:
        for i in range(2):
            store(i, None).wait()
        for side in range(2):
            rows = pl.ds(side * RADIUS, RADIUS)

            @pl.when(reach[side])
            def _():
                for p in range(pieces):
                    edge_copy(1 - side, p).wait_recv()
                    edges_in[p, rows] = landed[p, rows]
                whole = ready.at[:, rows]
                pltpu.make_async_remote_copy(
                    src_ref=whole,
                    dst_ref=whole,
                    send_sem=edge_ssem.at[side],
                    recv_sem=edge_rsem.at[side, 0],
                    device_id=(dp, seq - 1 + 2 * side),
                    device_id_type=MESH,
                ).wait_send()

            @pl.when(jnp.logical_not(reach[side]))
            def _():
                for p in range(pieces):
                    edges_in[p, rows] = jnp.zeros((RADIUS, D), bf16)

    for a, kind in enumerate(kinds):
        h = held[a]
        for name in ("core", "xx", "yy", "za", "zb"):
            if name in h:
                copy(h[name], h[name], a, STAGES[name], 0, to["core"]).wait_send()
        if kind == "gates":
            part = h["dd"].at[:, pl.ds(0, 3)]
            copy(part, part, a, STAGES["dd"], 0, to["core"]).wait_send()
        elif kind == "down":

            @pl.when(moved)
            def _():
                copy(h["dd"], h["dd"], a, STAGES["dd"], 0, to["core"]).wait_send()


def interleave(parts):
    keyed = [((i + 0.5) / len(p), n, v) for n, p in enumerate(parts) for i, v in enumerate(p)]
    return [v for _, _, v in sorted(keyed)]


LAGS = {"all": (-4, 0, 2, 4, 6, 8, 8), "rest": (-2, -1, -1, 1.5, 3.5, 5.5, 8)}
STAGES = {"core": 0, "xx": 1, "yy": 2, "za": 3, "zb": 4, "dd": 5}
SCRATCH = {
    "xy": ("own", "core", "xx", "yy", "za", "zb", "lsem", "rsem", "ssem"),
    "yx": ("own", "core", "xx", "yy", "za", "zb", "lsem", "rsem", "ssem"),
    "gates": ("own", "xx", "za", "zb", "sum", "dd", "lsem", "rsem", "ssem"),
    "down": ("own", "xx", "za", "zb", "sum", "dd", "lsem", "rsem", "ssem"),
}


def reduce_all(values, jobs, widths, n_y, collective_id, light=(), factors=()):
    operands, scratch = [], []
    for value, inner in values:
        height, columns = value.shape
        lead = (2, CORES, DEPTH, n_y) if inner else (2, 1, DEPTH, 1)
        operands.append(value.reshape(lead + (height // math.prod(lead), columns)))
    heights = {job[5]: D // (8 * DEPTH) if len(job) > 7 else operands[job[1]].shape[4] for job in jobs}
    out_shape = [jax.ShapeDtypeStruct((heights[o], w), f32) for o, w in enumerate(widths)]
    for kind, source, _, width, k, out, *rest in jobs:
        _, inner, _, outer = operands[source].shape[:4]
        height = heights[out]
        if kind == "xy":
            shapes = [(2, DEPTH, n_y)] * 2 + [(DEPTH, n_y), (DEPTH,), (2,), ()]
        elif kind == "yx":
            shapes = [(2, DEPTH, n_y)] * 2 + [(DEPTH,), (2, DEPTH), (2,), ()]
        else:
            both = (inner, outer)
            shapes = [(inner, DEPTH, outer)] * 2 + [(2,) + both, both]
            shapes += [(4,), (4,)] if kind == "gates" else [(), ()]
        scratch += [pltpu.VMEM((k,) + shape + (height, width), bf16) for shape in shapes]
        scratch += [
            pltpu.SemaphoreType.DMA((k,)),
            pltpu.SemaphoreType.DMA((6, k)),
            pltpu.SemaphoreType.DMA((6,)),
        ]
        if len(rest) > 1:
            scratch.append(pltpu.VMEM((k, 2, CORES, DEPTH, n_y, height, width), bf16))
    if light:
        pieces, edge_rows = light[1].shape[:2]
        out_shape += [jax.ShapeDtypeStruct(v.shape, bf16) for v in light[:2]]
        out_shape.append(jax.ShapeDtypeStruct((pieces, edge_rows, D), bf16))
        own, edge, grad, weights = light
        scratch += [pltpu.VMEM(v.shape, bf16) for v in (own, edge, grad, own, edge, weights)]
        scratch += [pltpu.VMEM((pieces, edge_rows, D), bf16)] * 2
        scratch += [pltpu.SemaphoreType.DMA((3, pieces)), pltpu.SemaphoreType.DMA]
        scratch += [pltpu.SemaphoreType.DMA((2,))] * 2 + [pltpu.SemaphoreType.DMA((2, pieces))]
    if factors:
        scratch += [pltpu.VMEM(v.shape, bf16) for v in factors]
        scratch.append(pltpu.SemaphoreType.DMA((32,)))
    total = 16 * n_y * sum(math.prod(shape.shape) for shape in out_shape[: len(widths)])
    here, anywhere = pl.BlockSpec(memory_space=pltpu.VMEM), pl.BlockSpec(memory_space=pl.ANY)
    out_specs = [here] * len(widths) + ([anywhere] * 2 + [here] if light else [])
    return pl.pallas_call(
        functools.partial(
            reduce_kernel,
            tuple(jobs),
            (len(values), len(widths), bool(light), len(factors)),
            n_y,
        ),
        out_shape=out_shape,
        in_specs=[anywhere] * len([*values, *light, *factors]),
        out_specs=out_specs,
        scratch_shapes=scratch,
        compiler_params=pltpu.CompilerParams(
            collective_id=collective_id, has_side_effects=True, vmem_limit_bytes=60 << 20
        ),
        cost_estimate=pl.CostEstimate(
            flops=2 * total, bytes_accessed=32 * total, transcendentals=0
        ),
        name="reduce_gradients",
    )(*operands, *light, *factors)


def copy_kernel(*refs):
    count = len(refs) // 2
    for i in range(count):
        refs[count + i][...] = refs[i][...]


def copy_all(values):
    count = len(values)
    return pl.pallas_call(
        copy_kernel,
        out_shape=[jax.ShapeDtypeStruct(v.shape, v.dtype) for v in values],
        in_specs=[pl.BlockSpec(memory_space=pltpu.VMEM)] * count,
        out_specs=[pl.BlockSpec(memory_space=pltpu.VMEM)] * count,
        name="copy_outputs",
    )(*values)


def per_device(
    layer_input,
    cotangent,
    first_gain,
    light_inputs,
    light_output,
    heavy_queries,
    heavy_keyvalue,
    heavy_output,
    second_gain,
    router,
    light_gates,
    light_down,
    heavy_gates,
    heavy_down,
    query_index,
    query_count,
    key_index,
    key_count,
    feed_slot,
):
    pieces, tokens = layer_input.shape[:2]
    rows = pieces * tokens
    n_dp, n_seq = lax.axis_size("dp"), lax.axis_size("seq")
    n_x, n_y = n_dp // CORES, n_seq // DEPTH
    seq_rank = lax.axis_index("seq")
    core = Ring("dp", 1, CORES)
    ring_x = Ring("dp", CORES, n_x)
    ring_y = Ring("seq", 1, n_y)
    ring_z = Ring("seq", n_y, DEPTH)
    capacity = max(2, 3 * rows // (16 * n_seq))
    slots = n_seq * capacity
    each = D // (n_dp * n_seq)
    kernels = each % 8 == 0 and n_x == n_y == 2

    def reduce_grad(value, first, second):
        height, width = value.shape
        chunk = height // (n_dp * n_seq)
        parts = value.reshape(n_x, CORES, DEPTH, n_y, chunk, width)
        parts = core.scatter_sum(parts, 1).astype(bf16)
        dims = ["x", "z", "y"]
        rings = {"x": ring_x, "y": ring_y, "z": ring_z}
        order = [first, second, [d for d in dims if d not in (first, second)][0]]
        for i, d in enumerate(order):
            at = dims.index(d)
            parts = rings[d].scatter_sum(parts, at)
            if i < 2:
                parts = parts.astype(bf16)
            dims.remove(d)
        return parts

    def reduce_split(value):
        half = value.shape[1] // 2
        return jnp.concatenate(
            [
                reduce_grad(value[:, :half], "x", "y"),
                reduce_grad(value[:, half:], "y", "x"),
            ],
            axis=1,
        )

    def reduce_vectors(value):
        count, width = value.shape
        chunk = width // (n_dp * n_seq)
        parts = value.reshape(count, n_x, CORES, DEPTH, n_y, chunk)
        parts = core.scatter_sum(parts, 2)
        parts = ring_x.scatter_sum(parts, 1)
        parts = ring_z.scatter_sum(parts, 1)
        return ring_y.scatter_sum(parts, 1)

    ends = n_seq - 1
    left_rows = lax.ppermute(
        layer_input[:, tokens - RADIUS :], "seq", [(i, i + 1) for i in range(ends)]
    )
    right_rows = lax.ppermute(layer_input[:, :RADIUS], "seq", [(i + 1, i) for i in range(ends)])
    position = jnp.arange(tokens, dtype=jnp.int32)
    key_pick = (key_index[:, :, None] == position[None, None, :]).astype(bf16)
    query_live = jnp.arange(QCAP, dtype=jnp.int32)[None, :] < query_count
    query_pick = (query_index[:, :, None] == position[None, None, :]).astype(bf16)
    live_pick = query_pick * query_live[:, :, None].astype(bf16)
    key_raw = jnp.einsum("pkt,ptd->pkd", key_pick, layer_input, preferred_element_type=f32).astype(
        bf16
    )
    key_all = lax.all_gather(key_raw, "seq", axis=1, tiled=True)

    gain_first = first_gain.astype(f32)
    inputs = layer_input.astype(f32)
    unit_first, scale_first = norm_parts(inputs)
    normed_first = (unit_first * gain_first).astype(bf16)
    normed_flat = normed_first.reshape(rows, D)
    own_proj = mm(normed_flat, light_inputs).astype(bf16).reshape(pieces, tokens, 3 * D)
    edge_rows = jnp.concatenate([left_rows, right_rows], axis=1)
    normed_edge = (norm_parts(edge_rows.astype(f32))[0] * gain_first).astype(bf16)
    edge_flat = normed_edge.reshape(pieces * 2 * RADIUS, D)
    edge_proj = mm(edge_flat, light_inputs[:, D:]).astype(bf16)
    edge_proj = edge_proj.reshape(pieces, 2 * RADIUS, 2 * D)

    reach = jnp.stack([seq_rank > 0, seq_rank < n_seq - 1]).astype(jnp.int32)
    light_att = light_attention(reach, own_proj, edge_proj).reshape(rows, D)

    key_slots = n_seq * KCAP
    key_rows_all = key_all.reshape(pieces * key_slots, D)
    normed_keys = (norm_parts(key_rows_all.astype(f32))[0] * gain_first).astype(bf16)
    heavy_pairs = mm(normed_keys, heavy_keyvalue).astype(bf16).reshape(pieces, key_slots, 2 * D)
    key_live = jnp.arange(KCAP, dtype=jnp.int32)[None, None, :] < key_count[:, :, None]
    key_live = key_live.reshape(pieces, 1, key_slots).astype(f32)
    query_rows = (
        jnp.einsum("pqt,ptd->pqd", query_pick, normed_first, preferred_element_type=f32)
        .astype(bf16)
        .reshape(pieces * QCAP, D)
    )
    heavy_query = mm(query_rows, heavy_queries).astype(bf16).reshape(pieces, QCAP, D)
    heavy_att = heavy_attention(heavy_query, heavy_pairs, key_live)
    heavy_spread = (
        jnp.einsum("pqt,pqd->ptd", live_pick, heavy_att, preferred_element_type=f32)
        .astype(bf16)
        .reshape(rows, D)
    )

    middle = (
        inputs.reshape(rows, D) + mm(light_att, light_output) + mm(heavy_spread, heavy_output)
    )
    gain_second = second_gain.astype(f32)
    unit_second, scale_second = norm_parts(middle)
    normed_second = (unit_second * gain_second).astype(bf16)

    slot_of = feed_slot.reshape(1, rows)
    pick = (jnp.arange(slots, dtype=jnp.int32)[:, None] == slot_of).astype(bf16)
    routed = feed_slot.reshape(rows, 1) >= 0
    cot = cotangent.reshape(rows, D)
    gating = jax.nn.sigmoid(
        jnp.sum(normed_second.astype(f32) * router.astype(f32), axis=-1, keepdims=True)
    )
    grad_token = (gating * cot.astype(f32)).astype(bf16)
    feed_in = mm(pick, normed_second).astype(bf16)
    grad_in = mm(pick, grad_token).astype(bf16)

    wide = heavy_gates.shape[1] // 2
    share = wide // 4
    if kernels:
        light_act, grad_light_pre, light_feed, grad_light, back, feed_all, heavy_act, heavy_pre = (
            feed_forward(
                normed_second,
                cot,
                jnp.stack([feed_in, grad_in]),
                light_gates,
                light_down,
                heavy_gates,
                heavy_down,
                n_y,
            )
        )
        feed_rows = feed_all[:, 0].reshape(4 * slots, D)
        grad_rows = feed_all[:, 1].reshape(4 * slots, D)
        heavy_act = heavy_act.reshape(4 * slots, share)
        heavy_pre = heavy_pre.reshape(4 * slots, 2 * share)
        heavy_result, grad_feed_in = back[0], back[1]
    else:
        feed_rows, grad_rows = feed_in, grad_in
        hidden = light_down.shape[0]
        pre = mm(normed_second, light_gates)
        light_act, *grads = glu_and_pull(pre[:, :hidden], pre[:, hidden:], mm_nt(cot, light_down))
        light_act = light_act.astype(bf16)
        grad_light_pre = jnp.concatenate(grads, axis=1).astype(bf16)
        light_feed = mm(light_act, light_down)
        grad_light = mm_nt(grad_light_pre, light_gates)
        pre = mm(feed_in, heavy_gates)
        heavy_act, *grads = glu_and_pull(pre[:, :wide], pre[:, wide:], mm_nt(grad_in, heavy_down))
        heavy_act = heavy_act.astype(bf16)
        heavy_pre = jnp.concatenate(grads, axis=1).astype(bf16)
        heavy_result = mm(heavy_act, heavy_down).astype(bf16)
        grad_feed_in = mm_nt(heavy_pre, heavy_gates).astype(bf16)
    heavy_down_grad = mm_tn(heavy_act, grad_rows).astype(bf16)
    heavy_gates_grad = mm_tn(feed_rows, heavy_pre).astype(bf16)
    light_down_grad = mm_tn(light_act, cot).astype(bf16)
    light_gates_grad = mm_tn(normed_second, grad_light_pre).astype(bf16)

    token_result = mm_tn(pick, heavy_result)
    output = (middle + light_feed + gating * token_result).astype(bf16).reshape(layer_input.shape)
    grad_gating = jnp.sum(cot.astype(f32) * token_result, axis=-1, keepdims=True)
    grad_logit = grad_gating * gating * (1.0 - gating)
    grad_second = (
        grad_light
        + mm_tn(pick, grad_feed_in)
        + grad_logit * router.astype(f32)
    )
    router_grad = jnp.sum(grad_logit * normed_second.astype(f32), axis=0)
    second_gain_grad = jnp.sum(grad_second * unit_second, axis=0)
    grad_middle = cot.astype(f32) + norm_pull(grad_second, middle, scale_second, gain_second)
    grad_mid_low = grad_middle.astype(bf16)

    light_output_grad = mm_tn(light_att, grad_mid_low).astype(bf16)
    grad_light_att = mm_nt(grad_mid_low, light_output).astype(bf16)
    grad_query_rows = (
        jnp.einsum(
            "pqt,ptd->pqd",
            live_pick,
            grad_mid_low.reshape(pieces, tokens, D),
            preferred_element_type=f32,
        )
        .astype(bf16)
        .reshape(pieces * QCAP, D)
    )
    heavy_output_grad = mm_tn(heavy_att.reshape(pieces * QCAP, D), grad_query_rows).astype(bf16)
    grad_heavy_att = mm_nt(grad_query_rows, heavy_output).astype(bf16)

    grad_hq_low, grad_hkv_low = heavy_attention_back(
        heavy_query,
        heavy_pairs,
        key_live,
        grad_heavy_att.reshape(pieces, QCAP, D),
    )
    grad_hq_low = grad_hq_low.reshape(pieces * QCAP, D)
    grad_hkv_low = grad_hkv_low.reshape(pieces * key_slots, 2 * D)
    grad_key_rows = mm_nt(grad_hkv_low, heavy_keyvalue).astype(bf16)
    heavy_keyvalue_grad = mm_tn(normed_keys, grad_hkv_low).astype(bf16)
    heavy_queries_grad = mm_tn(query_rows, grad_hq_low).astype(bf16)

    grad_light_att, grad_key_rows = lax.optimization_barrier((grad_light_att, grad_key_rows))
    grad_key_own = lax.psum_scatter(
        grad_key_rows.reshape(pieces, key_slots, D), "seq", scatter_dimension=1, tiled=True
    )
    grad_light_att = grad_light_att.reshape(pieces, tokens, D)
    if kernels:
        early = [
            (light_gates_grad, True),
            (light_output_grad, True),
            (heavy_gates_grad, True),
            (heavy_queries_grad, True),
            (heavy_keyvalue_grad, True),
        ]
        half = light_gates_grad.shape[1] // 2
        jobs = [
            ("xy", 0, 0, 512, 2 * half // 512, 0, 0),
            ("xy", 1, 0, 384, D // 384, 1, 0),
            ("gates", 2, 0, 256, share // 256, 2, 0),
            ("gates", 2, share, 256, share // 256, 2, wide),
            ("xy", 3, 0, 384, 2, 3, 0),
            ("xy", 4, 0, 512, 3, 4, 0),
        ]
        widths = (2 * half, D, 2 * wide, D, 2 * D)
        *early, grad_own, grad_edge, grad_around = reduce_all(
            early, jobs, widths, n_y, 0, (own_proj, edge_proj, grad_light_att, light_inputs)
        )
    else:
        grad_own, grad_edge = light_attention_back(reach, own_proj, edge_proj, grad_light_att)
        grad_edge_rows = mm_nt(grad_edge.reshape(-1, 2 * D), light_inputs[:, D:]).astype(bf16)
        grad_edge_rows = grad_edge_rows.reshape(pieces, 2 * RADIUS, D)
        from_right = lax.ppermute(
            grad_edge_rows[:, :RADIUS], "seq", [(i + 1, i) for i in range(ends)]
        )
        from_left = lax.ppermute(
            grad_edge_rows[:, RADIUS:], "seq", [(i, i + 1) for i in range(ends)]
        )
        grad_around = jnp.concatenate([from_left, from_right], axis=1)
    grad_own = grad_own.reshape(rows, 3 * D)
    grad_edge = grad_edge.reshape(pieces * 2 * RADIUS, 2 * D)
    grad_hq_rows = mm_nt(grad_hq_low, heavy_queries).astype(bf16).reshape(pieces, QCAP, D)
    grad_first = mm_nt(grad_own, light_inputs).reshape(pieces, tokens, D)
    grad_slots = jnp.concatenate([grad_hq_rows, grad_key_own.astype(bf16)], axis=1)
    both_pick = jnp.concatenate([query_pick, key_pick], axis=1)
    grad_first = (
        grad_first
        + jnp.einsum("pkt,pkd->ptd", both_pick, grad_slots, preferred_element_type=f32)
        + grad_around.astype(f32)
    )
    first_gain_grad = jnp.sum(grad_first * unit_first, axis=(0, 1))
    input_grad = grad_middle.reshape(pieces, tokens, D) + norm_pull(
        grad_first, inputs, scale_first, gain_first
    )
    vectors = jnp.stack([first_gain_grad, second_gain_grad, router_grad])
    devices = n_dp * n_seq
    if kernels:
        lines = vectors.reshape(3, devices, each).transpose(1, 0, 2)
        lines = jnp.pad(lines, ((0, 0), (0, 5), (0, 256 - each))).reshape(devices * 8, 256)
        jobs = (
            ("xy", 0, 0, 384, 1, 0, 0, (0, 2, 0)),
            ("yx", 0, 384, 384, 1, 0, 384, (0, 2, 384)),
            ("xy", 0, D, 384, 2, 0, D, (0, 2, D), (1, 3, 0)),
            ("yx", 0, 2 * D, 384, 2, 0, 2 * D, (0, 2, 2 * D), (1, 3, D)),
            ("xy", 0, 0, 256, 1, 1, 0),
            ("yx", 1, 0, 384, 2, 2, 0),
            ("yx", 2, 0, 384, 2, 3, 0),
            ("down", 3, 0, 128, D // 128, 4, 0),
        )
        factors = (normed_flat, edge_flat, grad_own, grad_edge)
        late = [
            (lines.astype(bf16), True),
            (light_down_grad, True),
            (heavy_output_grad, True),
            (heavy_down_grad, False),
        ]
        late = reduce_all(late, jobs, (3 * D, 256, D, D, D), n_y, 1, (), factors)
        sums = copy_all([*early, *late])
        light_gates_grad, light_output_grad, heavy_gates_grad, heavy_queries_grad = sums[:4]
        heavy_keyvalue_grad, light_inputs_grad, lines = sums[4:7]
        light_down_grad, heavy_output_grad, heavy_down_grad = sums[7:]
        vectors = lines[:3, :each]
    else:
        light_pair_grad = mm_tn(normed_flat, grad_own[:, D:]) + mm_tn(edge_flat, grad_edge)
        light_inputs_grad = jnp.concatenate(
            [mm_tn(normed_flat, grad_own[:, :D]), light_pair_grad], axis=1
        ).astype(bf16)
        light_inputs_grad = reduce_split(light_inputs_grad)
        light_output_grad = reduce_split(light_output_grad)
        heavy_queries_grad = reduce_split(heavy_queries_grad)
        heavy_keyvalue_grad = reduce_split(heavy_keyvalue_grad)
        heavy_output_grad = reduce_split(heavy_output_grad)
        light_gates_grad = reduce_split(light_gates_grad)
        light_down_grad = reduce_split(light_down_grad)
        heavy_gates_grad = reduce_split(heavy_gates_grad)
        heavy_down_grad = reduce_split(heavy_down_grad)
        vectors = reduce_vectors(vectors)
    return (
        output,
        input_grad,
        vectors[0],
        light_inputs_grad,
        light_output_grad,
        heavy_queries_grad,
        heavy_keyvalue_grad,
        heavy_output_grad,
        vectors[1],
        vectors[2],
        light_gates_grad,
        light_down_grad,
        heavy_gates_grad,
        heavy_down_grad,
    )


def solution(mesh):
    rows = P(("dp", "seq"), None)
    line = P(("dp", "seq"))
    tokens = P("dp", "seq", None)
    slots = P("dp", "seq")
    return jax.shard_map(
        per_device,
        mesh=mesh,
        in_specs=(tokens, tokens) + (P(),) * 12 + (slots, slots, slots, P("dp", None), slots),
        out_specs=(tokens, tokens, line) + (rows,) * 5 + (line, line) + (rows,) * 4,
        check_vma=False,
    )
```
